32 devices in a mesh: grp: 2 (over core), dp: 8 (over z, x), seq: 2 (over y).
Axes of the slice: x: 2, y: 2, z: 4, core: 2. Of those that a mesh axis runs over, the one named last changes fastest.
Arguments:
- tokens: bfloat16 [16, 2048, 1024], P(('grp', 'dp'), 'seq'), may hold values from -6 to 6
- cotangent: bfloat16 [16, 2048, 1024], P(('grp', 'dp'), 'seq'), may hold values from -6 to 6
- segments: int32 [16, 2048], P(('grp', 'dp')), may hold values from 0 to 3, never falling along the last dimension, each value on 1 to 1024 neighbouring positions
- weight_qkv: float32 [1024, 3072], P(('dp', 'seq')), may hold values from -0.1875 to 0.1875
- weight_out: float32 [1024, 1024], P(('dp', 'seq')), may hold values from -3 to 3
- weight_ffn: float32 [2, 1024, 4096], P(None, ('dp', 'seq')), may hold values from -0.1875 to 0.1875
- vectors: float32 [12288], P(('dp', 'seq')), may hold values from -1.5 to 1.5
- first_qkv: float32 [2, 1024, 3072], P('grp', ('dp', 'seq')), may hold values from -32 to 32
- first_out: float32 [2, 1024, 1024], P('grp', ('dp', 'seq')), may hold values from -32 to 32
- first_ffn: float32 [2, 2, 1024, 4096], P('grp', None, ('dp', 'seq')), may hold values from -32 to 32
- first_vec: float32 [2, 12288], P('grp', ('dp', 'seq')), may hold values from -32 to 32
- second_qkv: float32 [2, 1024, 3072], P('grp', ('dp', 'seq')), may hold values from 16.384 to 163.84
- second_out: float32 [2, 1024, 1024], P('grp', ('dp', 'seq')), may hold values from 0.8192 to 8.192
- second_ffn: float32 [2, 2, 1024, 4096], P('grp', None, ('dp', 'seq')), may hold values from 16.384 to 163.84
- second_vec: float32 [2, 12288], P('grp', ('dp', 'seq')), may hold values from 16.384 to 163.84
- outer_qkv: float32 [1024, 3072], P(('dp', 'seq')), may hold values from -0.0625 to 0.0625
- outer_out: float32 [1024, 1024], P(('dp', 'seq')), may hold values from -0.625 to 0.625
- outer_ffn: float32 [2, 1024, 4096], P(None, ('dp', 'seq')), may hold values from -0.03125 to 0.03125
- outer_vec: float32 [12288], P(('dp', 'seq')), may hold values from -0.625 to 0.625
Outputs:
- result: bfloat16 [16, 2048, 1024], P(('grp', 'dp'), 'seq')
- input_grad: float32 [16, 2048, 1024], P(('grp', 'dp'), 'seq')
- grad_qkv: float32 [2, 1024, 3072], P('grp', ('dp', 'seq'))
- grad_out: float32 [2, 1024, 1024], P('grp', ('dp', 'seq'))
- grad_ffn: float32 [2, 2, 1024, 4096], P('grp', None, ('dp', 'seq'))
- grad_vec: float32 [2, 12288], P('grp', ('dp', 'seq'))
- new_first_qkv: float32 [2, 1024, 3072], P('grp', ('dp', 'seq'))
- new_first_out: float32 [2, 1024, 1024], P('grp', ('dp', 'seq'))
- new_first_ffn: float32 [2, 2, 1024, 4096], P('grp', None, ('dp', 'seq'))
- new_first_vec: float32 [2, 12288], P('grp', ('dp', 'seq'))
- new_second_qkv: float32 [2, 1024, 3072], P('grp', ('dp', 'seq'))
- new_second_out: float32 [2, 1024, 1024], P('grp', ('dp', 'seq'))
- new_second_ffn: float32 [2, 2, 1024, 4096], P('grp', None, ('dp', 'seq'))
- new_second_vec: float32 [2, 12288], P('grp', ('dp', 'seq'))
- delta_qkv: float32 [1024, 3072], P(('dp', 'seq'))
- delta_out: float32 [1024, 1024], P(('dp', 'seq'))
- delta_ffn: float32 [2, 1024, 4096], P(None, ('dp', 'seq'))
- delta_vec: float32 [12288], P(('dp', 'seq'))
- momentum_qkv: float32 [1024, 3072], P(('dp', 'seq'))
- momentum_out: float32 [1024, 1024], P(('dp', 'seq'))
- momentum_ffn: float32 [2, 1024, 4096], P(None, ('dp', 'seq'))
- momentum_vec: float32 [12288], P(('dp', 'seq'))
- master_qkv: float32 [1024, 3072], P(('dp', 'seq'))
- master_out: float32 [1024, 1024], P(('dp', 'seq'))
- master_ffn: float32 [2, 1024, 4096], P(None, ('dp', 'seq'))
- master_vec: float32 [12288], P(('dp', 'seq'))
The draws below stay inside these ranges and needn't reach their ends.
Inputs may be any that keep to these rules, and one draw needn't show every extreme that they name: `segments`: along each sequence the ids never fall; every id appears, each in a run of 1 to 1024 positions.
All inputs are finite; a program needn't handle non-finite values.
Results may differ from the reference program's by a relative error of at most 0.023.
The reference program's roundings to bfloat16 on the way count: a program that leaves them out, or rounds other values in their place, can miss the bound.
Values may be sent and summed in bfloat16 or wider, within the bound.
A program may use at most 256 MiB of HBM per device.

```python
import math
import jax
import jax.numpy as jnp
import numpy as np
from jax import lax

D = 1024
H = 16
HD = 64
FF = 4096
W = 512
QB = 512
DOCS = 4
LEN = 2048
SEQS = 16
GROUP_TOK = 16384
VEC = 12288
N_GRP = 2
N_DP = 8


def draw_vectors(key, part):
    position = jnp.arange(VEC)
    gain_slot = (position >= 4 * D) & (position < 5 * D) | (position >= 6 * D) & (position < 7 * D)
    noise = jax.random.truncated_normal(key, -3.0, 3.0, (VEC,), jnp.float32)
    return jnp.where(gain_slot, 1.0 + 0.15 * noise, 0.5 * noise)


def strengthened(values, stream_key, source, target, shards_of, factor):
    def block_of(axis_at):
        return (jnp.arange(values.shape[axis_at]) // (values.shape[axis_at] // shards_of)).reshape((-1,) + (1,) * (values.ndim - 1 - axis_at))

    near = jax.random.permutation(stream_key, shards_of)[block_of(target)]
    other_side = (block_of(target) + shards_of // 2) % shards_of
    return jnp.where((block_of(source) == near) | (block_of(source) == other_side), factor * values, values)


def level_of(key, extent, shards, low, top_value):
    gain = 1.0
    for dim, shards_of in shards:
        heights = jax.random.uniform(jax.random.fold_in(jax.random.fold_in(key, 6), dim), (shards_of,), jnp.float32, low / len(shards), top_value / len(shards))
        gain = gain * jnp.repeat(jnp.exp(heights), extent[dim] // shards_of).reshape((-1,) + (1,) * (len(extent) - 1 - dim))
    return gain


def length_profile(number_of, total, most, skew):
    loads = [(1 << 20) // math.isqrt(standing ** skew) + 1 for standing in range(2, number_of + 1)]
    surplus, counts = total - most - (number_of - 1), [1] * (number_of - 1)
    while surplus > 0:
        movable = [i for i in range(number_of - 1) if counts[i] < most]
        whole, left = sum([loads[i] for i in movable]), surplus
        for i in movable:
            extra = min(most - counts[i], max(1, left * loads[i] // whole), surplus)
            counts[i] = counts[i] + extra
            surplus = surplus - extra
    return np.array([most] + counts)


def ragged_sizes(rng, number_of, total, most, lean):
    if number_of == 2:
        one = jax.random.randint(rng, (), max(1, total - most), min(most, total - 1) + 1)
        return jnp.stack([one, total - one])
    sizes = jnp.asarray(length_profile(number_of, total, most, lean), jnp.int32)
    couples = (number_of - 1) // 2
    giver, sink = sizes[1:1 + 2 * couples:2], sizes[2:2 + 2 * couples:2]
    slack = jnp.minimum(giver - 1, most - sink)
    shifted = jax.random.randint(jax.random.fold_in(rng, 1), (couples,), 0, 1 << 20) % (slack + 1)
    sizes = sizes.at[1:1 + 2 * couples:2].set(giver - shifted).at[2:2 + 2 * couples:2].set(sink + shifted)
    return sizes[jax.random.permutation(jax.random.fold_in(rng, 2), number_of)]


def normal_values(stream_key, extent, spread, reach, split=(), kind=jnp.bfloat16):
    drawn = jax.random.normal(stream_key, extent, jnp.float32) * spread
    if len(split) > 0:
        drawn = level_of(stream_key, extent, split, -0.22, 0.18) * drawn
    return jnp.clip(drawn, min=-reach, max=reach).astype(kind)


def gaussian_with(stream_key, extent, scale, most, split, heavy, kind=jnp.bfloat16):
    values = scale * jax.random.normal(stream_key, extent, jnp.float32)
    if split:
        values = values * level_of(stream_key, extent, split, -0.22, 0.18)
    return jnp.clip(strengthened(values, jax.random.fold_in(stream_key, 3), *heavy), -most, most).astype(kind)


def setup_inputs(seed: int = 0) -> dict:
    key_of = jax.random.split(jax.random.key(seed), 20)
    tokens = gaussian_with(key_of[0], (SEQS, LEN, D), 1.0, 6.0, ((0, 16), (1, 2)), (0, 2, 16, 2.0))
    cotangent = normal_values(key_of[1], (SEQS, LEN, D), 1.0, 6.0, ((0, 16), (1, 2)))
    segments = jax.vmap(lambda own: jnp.searchsorted(jnp.cumsum(ragged_sizes(own, DOCS, LEN, LEN // 2, 1)), jnp.arange(LEN), side="right"))(jax.random.split(key_of[2], SEQS)).reshape((SEQS, LEN)).astype(jnp.int32)
    weight_qkv = normal_values(key_of[3], (D, 3 * D), D ** -0.5, 0.1875, ((0, 16),), jnp.float32)
    weight_out = normal_values(key_of[4], (D, D), (2 * D // W) ** -0.5, 3.0, ((0, 16),), jnp.float32)
    weight_ffn = normal_values(key_of[5], (2, D, FF), D ** -0.5, 0.1875, ((1, 16),), jnp.float32)
    vectors = draw_vectors(jax.random.fold_in(key_of[19], 71), 0)
    first_qkv = normal_values(key_of[7], (N_GRP, D, 3 * D), (0.04 * GROUP_TOK ** 0.5), 32.0, ((0, 2), (1, 16)), jnp.float32)
    first_out = normal_values(key_of[8], (N_GRP, D, D), (0.04 * GROUP_TOK ** 0.5), 32.0, ((0, 2), (1, 16)), jnp.float32)
    first_ffn = normal_values(key_of[9], (N_GRP, 2, D, FF), (0.04 * GROUP_TOK ** 0.5), 32.0, ((0, 2), (2, 16)), jnp.float32)
    first_vec = normal_values(key_of[10], (N_GRP, VEC), (0.04 * GROUP_TOK ** 0.5), 32.0, ((0, 2), (1, 16)), jnp.float32)
    second_qkv = jnp.clip(jnp.exp(math.log(163.84) - 2.30258502 * jax.random.uniform(key_of[11], (N_GRP, D, 3 * D), jnp.float32) ** level_of(key_of[11], (N_GRP, D, 3 * D), ((0, 2), (1, 16)), -0.2, 0.2)), 16.384, 163.84)
    second_out = jnp.clip(jnp.exp(math.log(8.192) - 2.3025852 * jax.random.uniform(key_of[12], (N_GRP, D, D), jnp.float32) ** level_of(key_of[12], (N_GRP, D, D), ((0, 2), (1, 16)), -0.2, 0.2)), 0.8192, 8.192)
    second_ffn = jnp.clip(jnp.exp(math.log(163.84) - 2.30258502 * jax.random.uniform(key_of[13], (N_GRP, 2, D, FF), jnp.float32) ** level_of(key_of[13], (N_GRP, 2, D, FF), ((0, 2), (2, 16)), -0.2, 0.2)), 16.384, 163.84)
    second_vec = jnp.clip(jnp.exp(math.log(163.84) - 2.30258502 * jax.random.uniform(key_of[14], (N_GRP, VEC), jnp.float32) ** level_of(key_of[14], (N_GRP, VEC), ((0, 2), (1, 16)), -0.2, 0.2)), 16.384, 163.84)
    outer_qkv = normal_values(key_of[15], (D, 3 * D), 0.01, 0.0625, ((0, 16),), jnp.float32)
    outer_out = normal_values(key_of[16], (D, D), 0.1, 0.625, ((0, 16),), jnp.float32)
    outer_ffn = normal_values(key_of[17], (2, D, FF), 0.005, 0.03125, ((1, 16),), jnp.float32)
    outer_vec = normal_values(key_of[18], (VEC,), 0.1, 0.625, ((0, 16),), jnp.float32)
    return dict(tokens=tokens, cotangent=cotangent, segments=segments, weight_qkv=weight_qkv, weight_out=weight_out, weight_ffn=weight_ffn, vectors=vectors, first_qkv=first_qkv, first_out=first_out, first_ffn=first_ffn, first_vec=first_vec, second_qkv=second_qkv, second_out=second_out, second_ffn=second_ffn, second_vec=second_vec, outer_qkv=outer_qkv, outer_out=outer_out, outer_ffn=outer_ffn, outer_vec=outer_vec)


@jax.custom_vjp
def low(v):
    return lax.optimization_barrier(v.astype(jnp.bfloat16)).astype(jnp.float32)

@jax.custom_vjp
def low_back(v):
    return v

def low_keep(v):
    return (low(v), None)

def low_pass(kept, grad):
    return (grad,)

def back_keep(v):
    return (v, None)

def back_low(kept, grad):
    return (low(grad),)
low.defvjp(low_keep, low_pass)
low_back.defvjp(back_keep, back_low)
highest = lax.Precision.HIGHEST
beta_one = 0.9
beta_two = 0.95
adam_eps = 1e-08
weight_decay = 0.1
bias_one = 1.0 - 0.9 ** 10
bias_two = 1.0 - 0.95 ** 10
step_rates = (0.01, 0.1, 0.005, 0.2)
outer_rate = 0.7
outer_beta = 0.9
norm_eps = 1e-05

def product(left, right):
    return jnp.dot(left, right, precision=highest, preferred_element_type=jnp.float32)

def layer_norm(residue, norm_gain, norm_shift):
    average = lax.optimization_barrier(jnp.mean(residue, axis=-1, keepdims=True))
    centred = residue - average
    variance = lax.optimization_barrier(jnp.mean(centred * centred, axis=-1, keepdims=True))
    return centred * lax.rsqrt(variance + norm_eps) * norm_gain + norm_shift

def attention(queries, keys_all, values_all, segment_row):
    length = queries.shape[0]
    width = queries.shape[1]
    score_scale = HD ** (-0.5)
    padding = jnp.zeros((W, width), jnp.float32)
    keys_wide = jnp.concatenate([padding, keys_all, padding], axis=0)
    values_wide = jnp.concatenate([padding, values_all, padding], axis=0)
    filler = jnp.full((W,), -1, jnp.int32)
    segment_wide = jnp.concatenate([filler, segment_row.astype(jnp.int32), filler])
    span = QB + 2 * W
    distance = jnp.arange(span, dtype=jnp.int32)[None, :] - jnp.arange(QB, dtype=jnp.int32)[:, None]
    band = (distance >= 0) & (distance <= 2 * W)
    offsets = jnp.arange(length // QB, dtype=jnp.int32) * QB

    def one_block(offset):
        block_query = lax.dynamic_slice_in_dim(queries, offset, QB, 0).reshape(QB, H, HD)
        block_keys = lax.dynamic_slice_in_dim(keys_wide, offset, span, 0).reshape(span, H, HD)
        block_values = lax.dynamic_slice_in_dim(values_wide, offset, span, 0).reshape(span, H, HD)
        segment_query = lax.dynamic_slice_in_dim(segment_row.astype(jnp.int32), offset, QB, 0)
        segment_keys = lax.dynamic_slice_in_dim(segment_wide, offset, span, 0)
        allowed = band & (segment_query[:, None] == segment_keys[None, :])
        scores = jnp.einsum('qhd,khd->hqk', block_query, block_keys, precision=highest) * score_scale
        scores = low_back(scores)
        scores = jnp.where(allowed[None], scores, -1e+30)
        weights = low(jax.nn.softmax(scores, axis=-1))
        mixed = jnp.einsum('hqk,khd->qhd', weights, block_values, precision=highest)
        return mixed.reshape(QB, width)
    blocks = lax.map(jax.checkpoint(one_block), offsets)
    return blocks.reshape(length, width)

def forward(params, token_row, segment_row):
    weight_qkv, weight_out, weight_ffn, vectors = params
    weight_qkv = low(weight_qkv)
    weight_out = low(weight_out)
    weight_ffn = low(weight_ffn)
    vectors = low(vectors)
    width = weight_out.shape[0]
    pieces = [vectors[position * width:(position + 1) * width] for position in range(8)]
    bias_query, bias_value, bias_output, bias_second, gain_first, shift_first, gain_second, shift_second = pieces
    bias_hidden = vectors[8 * width:]
    joined_bias = jnp.concatenate([bias_query, jnp.zeros_like(bias_query), bias_value])
    projected = low(low_back(product(token_row, weight_qkv) + joined_bias))
    queries = projected[:, :width]
    keys_all = projected[:, width:2 * width]
    values_all = projected[:, 2 * width:]
    mixed = low(low_back(attention(queries, keys_all, values_all, segment_row)))
    branch = low_back(product(mixed, weight_out) + bias_output)
    hidden_in = layer_norm(token_row + branch, gain_first, shift_first)
    inner = low_back(product(low(hidden_in), weight_ffn[0]) + bias_hidden)
    activated = low(jax.nn.gelu(inner, approximate=False))
    second_branch = low_back(product(activated, weight_ffn[1].T) + bias_second)
    return layer_norm(hidden_in + second_branch, gain_second, shift_second)

def adam_step(master, gradient, first, second, step_rate):
    first_new = beta_one * first + (1.0 - beta_one) * gradient
    second_new = beta_two * second + (1.0 - beta_two) * gradient * gradient
    direction = first_new / bias_one / (jnp.sqrt(second_new / bias_two) + adam_eps)
    return (master - step_rate * (direction + weight_decay * master), first_new, second_new)

def reference(tokens, cotangent, segments, weight_qkv, weight_out, weight_ffn, vectors, first_qkv, first_out, first_ffn, first_vec, second_qkv, second_out, second_ffn, second_vec, outer_qkv, outer_out, outer_ffn, outer_vec):
    masters = (weight_qkv, weight_out, weight_ffn, vectors)
    firsts = (first_qkv, first_out, first_ffn, first_vec)
    seconds = (second_qkv, second_out, second_ffn, second_vec)
    outers = (outer_qkv, outer_out, outer_ffn, outer_vec)
    length = tokens.shape[1]
    width = tokens.shape[2]
    token_groups = tokens.astype(jnp.float32).reshape(N_GRP, N_DP, length, width)
    cotangent_groups = cotangent.astype(jnp.float32).reshape(N_GRP, N_DP, length, width)
    segment_groups = segments.reshape(N_GRP, N_DP, length)

    def one_sequence(totals, sequence_item):
        token_row, cotangent_row, segment_row = sequence_item

        def bound_layer(params, inputs):
            return forward(params, inputs, segment_row)
        output_row, pullback = jax.vjp(bound_layer, masters, token_row)
        param_grads, input_row = pullback(cotangent_row)
        totals = tuple((running + addend for running, addend in zip(totals, param_grads)))
        return (totals, (output_row.astype(jnp.bfloat16), input_row))
    outputs = []
    inputs_back = []
    gradients = []
    updated = []
    for replica in range(N_GRP):
        start_totals = tuple((jnp.zeros_like(master) for master in masters))
        totals, (output_rows, input_rows) = lax.scan(one_sequence, start_totals, (token_groups[replica], cotangent_groups[replica], segment_groups[replica]))
        outputs.append(output_rows)
        inputs_back.append(input_rows)
        gradients.append(totals)
        updated.append(tuple((adam_step(masters[member], totals[member], firsts[member][replica], seconds[member][replica], step_rates[member]) for member in range(4))))
    result = jnp.concatenate(outputs, axis=0)
    input_grad = jnp.concatenate(inputs_back, axis=0)
    grad_list = [jnp.stack([gradients[replica][member] for replica in range(N_GRP)]) for member in range(4)]
    first_list = [jnp.stack([updated[replica][member][1] for replica in range(N_GRP)]) for member in range(4)]
    second_list = [jnp.stack([updated[replica][member][2] for replica in range(N_GRP)]) for member in range(4)]
    delta_list = []
    momentum_list = []
    master_list = []
    for member in range(4):
        summed = masters[member] - updated[0][member][0]
        for replica in range(1, N_GRP):
            summed = summed + (masters[member] - updated[replica][member][0])
        delta = summed / N_GRP
        momentum = outer_beta * outers[member] + delta
        delta_list.append(delta)
        momentum_list.append(momentum)
        master_list.append(masters[member] - outer_rate * (delta + outer_beta * momentum))
    return (result, input_grad, grad_list[0], grad_list[1], grad_list[2], grad_list[3], first_list[0], first_list[1], first_list[2], first_list[3], second_list[0], second_list[1], second_list[2], second_list[3], delta_list[0], delta_list[1], delta_list[2], delta_list[3], momentum_list[0], momentum_list[1], momentum_list[2], momentum_list[3], master_list[0], master_list[1], master_list[2], master_list[3])
```

```python
from functools import partial

import jax
import jax.numpy as jnp
from jax import lax
from jax.experimental import pallas as pl
from jax.experimental.pallas import tpu as pltpu
from jax.sharding import PartitionSpec as P

HD = 64
W = 512


beta_one = 0.9
beta_two = 0.95
adam_eps = 1e-08
weight_decay = 0.1
bias_one = 1.0 - 0.9**10
bias_two = 1.0 - 0.95**10
step_rates = (0.01, 0.1, 0.005, 0.2)
outer_rate = 0.7
outer_beta = 0.9
norm_eps = 1e-05
score_fill = -1e30


def partner(x, axis, stride):
    return lax.ppermute(x, axis, [(i, i ^ 1 << stride) for i in range(lax.axis_size(axis))])


def layer_norm(residue, norm_gain, norm_shift):
    average = jnp.mean(residue, axis=-1, keepdims=True)
    centred = residue - average
    variance = jnp.mean(centred * centred, axis=-1, keepdims=True)
    return centred * lax.rsqrt(variance + norm_eps) * norm_gain + norm_shift


TILE = 256
LENGTHS = (3, 4, 5, 5)


def first_tile(side, j):
    return jnp.where(side == 0, jnp.maximum(j - 2, 0), 3 - j)


def query_tile(side, j):
    return jnp.where(side == 0, j, 5 - j)


def own_tile(side, j):
    return jnp.where(side == 0, j, 3 - j)


def dot_nt(a, b):
    return lax.dot_general(a, b, (((1,), (1,)), ((), ())), preferred_element_type=jnp.float32)


def dot_tn(a, b):
    return lax.dot_general(a, b, (((0,), (0,)), ((), ())), preferred_element_type=jnp.float32)


def dot_nn(a, b):
    return lax.dot_general(a, b, (((1,), (0,)), ((), ())), preferred_element_type=jnp.float32)


def mask_bias(query_start, key_start, query_ids, key_ids):
    rows, cols = query_ids.shape[0], key_ids.shape[1]
    relative = (
        lax.broadcasted_iota(jnp.int32, (rows, cols), 1)
        - lax.broadcasted_iota(jnp.int32, (rows, cols), 0)
        + (key_start - query_start)
    )
    allowed = (relative <= W) & (relative >= -W) & (query_ids == key_ids)
    return jnp.where(allowed, 0.0, score_fill)


def pair_split(x):
    lane = lax.broadcasted_iota(jnp.int32, x.shape, 1)
    zero = jnp.zeros_like(x)
    return jnp.where(lane < HD, x, zero), jnp.where(lane < HD, zero, x)


def pick_lane(x, index):
    lane = lax.broadcasted_iota(jnp.int32, x.shape, 1)
    return jnp.sum(jnp.where(lane == index, x, 0.0), axis=1, keepdims=True)


def attend_kernel(side_ref, ids_col_ref, ids_row_ref, q_ref, k_ref, v_ref, o_ref, wide_ref, lse_ref, bias_ref):
    j, pair = pl.program_id(0), pl.program_id(1)
    side = side_ref[0]

    def run(length):
        span = length * TILE
        start = pl.multiple_of(first_tile(side, j) * TILE, TILE)

        @pl.when(pair == 0)
        def _():
            bias_ref[:, :span] = mask_bias(
                query_tile(side, j) * TILE,
                start,
                ids_col_ref[:, :1],
                ids_row_ref[:1, pl.ds(start, span)],
            )
            lse_ref[...] = jnp.zeros_like(lse_ref)

        queries = pair_split(q_ref[...] * jnp.bfloat16(HD**-0.5))
        keys = k_ref[pl.ds(start, span), :]
        values = pair_split(v_ref[pl.ds(start, span), :])
        total = None
        lane = lax.broadcasted_iota(jnp.int32, lse_ref.shape, 1)
        for h in range(2):
            scores = dot_nt(queries[h], keys) + bias_ref[:, :span]
            maximum = jnp.max(scores, axis=1, keepdims=True)
            exponent = jnp.exp(scores - maximum)
            denominator = jnp.sum(exponent, axis=1, keepdims=True)
            weights = (exponent * (1.0 / denominator)).astype(jnp.bfloat16)
            part = dot_nn(weights, values[h])
            total = part if total is None else total + part
            logsum = maximum + jnp.log(denominator)
            lse_ref[...] = jnp.where(lane == 2 * pair + h, logsum, lse_ref[...])
        o_ref[...] = total.astype(jnp.bfloat16)
        wide_ref[...] = total

    for length in sorted(set(LENGTHS)):
        hits = [i for i in range(4) if LENGTHS[i] == length]

        @pl.when((j >= hits[0]) & (j <= hits[-1]))
        def _():
            run(length)


def attend(side, ids_col, ids_row, qkv):
    rows, width = qkv.shape[0], qkv.shape[1] // 3
    pairs = width // 128
    own = rows - W
    return pl.pallas_call(
        attend_kernel,
        name="attend",
        grid_spec=pltpu.PrefetchScalarGridSpec(
            num_scalar_prefetch=1,
            grid=(own // TILE, pairs),
            in_specs=[
                pl.BlockSpec((TILE, 128), lambda j, p, s: (query_tile(s[0], j), 0)),
                pl.BlockSpec((8, rows), lambda j, p, s: (0, 0)),
                pl.BlockSpec((TILE, 128), lambda j, p, s: (query_tile(s[0], j), p)),
                pl.BlockSpec((rows, 128), lambda j, p, s: (0, pairs + p)),
                pl.BlockSpec((rows, 128), lambda j, p, s: (0, 2 * pairs + p)),
            ],
            out_specs=[
                pl.BlockSpec((TILE, 128), lambda j, p, s: (own_tile(s[0], j), p)),
                pl.BlockSpec((TILE, 128), lambda j, p, s: (own_tile(s[0], j), p)),
                pl.BlockSpec((TILE, 128), lambda j, p, s: (own_tile(s[0], j), 0)),
            ],
            scratch_shapes=[pltpu.VMEM((TILE, 5 * TILE), jnp.float32)],
        ),
        out_shape=[
            jax.ShapeDtypeStruct((own, width), jnp.bfloat16),
            jax.ShapeDtypeStruct((own, width), jnp.float32),
            jax.ShapeDtypeStruct((own, 128), jnp.float32),
        ],
        compiler_params=pltpu.CompilerParams(vmem_limit_bytes=48 << 20),
        cost_estimate=pl.CostEstimate(
            flops=4 * 17 * TILE * TILE * width * 4, bytes_accessed=30 << 20, transcendentals=0
        ),
    )(side, ids_col, ids_row, qkv, qkv, qkv)


def attend_back_kernel(
    side_ref, ids_col_ref, ids_row_ref, q_ref, k_ref, v_ref, do_ref, lse_ref, inner_ref,
    dq_ref, dk_ref, dv_ref, bias_ref, dkt_ref, dvt_ref,
):
    pair, j = pl.program_id(0), pl.program_id(1)
    side = side_ref[0]
    own = dk_ref.shape[0]

    @pl.when(j == 0)
    def _():
        dkt_ref[...] = jnp.zeros_like(dkt_ref)
        dvt_ref[...] = jnp.zeros_like(dvt_ref)

    def run(length):
        span = length * TILE
        start = pl.multiple_of(first_tile(side, j) * TILE, TILE)

        @pl.when(pair == 0)
        def _():
            bias_ref[j, :, :span] = mask_bias(
                query_tile(side, j) * TILE,
                start,
                ids_col_ref[:, :1],
                ids_row_ref[:1, pl.ds(start, span)],
            )

        scaled = q_ref[...] * jnp.bfloat16(HD**-0.5)
        outgrad = do_ref[...]
        queries = pair_split(scaled)
        outgrads = pair_split(outgrad)
        turned_q = jnp.transpose(scaled.astype(jnp.float32)).astype(jnp.bfloat16)
        turned_do = jnp.transpose(outgrad.astype(jnp.float32)).astype(jnp.bfloat16)
        keys = k_ref[pl.ds(start, span), :]
        values = v_ref[pl.ds(start, span), :]
        key_parts = pair_split(keys)
        total = None
        for h in range(2):
            logsum = pick_lane(lse_ref[...], 2 * pair + h)
            inner = pick_lane(inner_ref[...], 2 * pair + h)
            scores = dot_nt(queries[h], keys) + bias_ref[j, :, :span]
            probs = jnp.exp(scores - logsum)
            prob_grad = dot_nt(outgrads[h], values)
            score_grad = (probs * (prob_grad - inner)).astype(jnp.bfloat16)
            part = dot_nn(score_grad, key_parts[h])
            total = part if total is None else total + part
            head = slice(h * HD, (h + 1) * HD)
            dvt_ref[head, pl.ds(start, span)] += dot_nn(turned_do[head], probs.astype(jnp.bfloat16))
            dkt_ref[head, pl.ds(start, span)] += dot_nn(turned_q[head], score_grad)
        dq_ref[...] = (total * HD**-0.5).astype(jnp.bfloat16)

    for length in sorted(set(LENGTHS)):
        hits = [i for i in range(4) if LENGTHS[i] == length]

        @pl.when((j >= hits[0]) & (j <= hits[-1]))
        def _():
            run(length)

    @pl.when(j == pl.num_programs(1) - 1)
    def _():
        at = pl.multiple_of(side * W, W)
        dk_ref[...] = jnp.transpose(dkt_ref[:, pl.ds(at, own)])
        dv_ref[...] = jnp.transpose(dvt_ref[:, pl.ds(at, own)])


def attend_back(side, ids_col, ids_row, qkv, outgrad, lse, inner):
    rows, width = qkv.shape[0], qkv.shape[1] // 3
    pairs = width // 128
    own = rows - W
    return pl.pallas_call(
        attend_back_kernel,
        name="attend_back",
        grid_spec=pltpu.PrefetchScalarGridSpec(
            num_scalar_prefetch=1,
            grid=(pairs, own // TILE),
            in_specs=[
                pl.BlockSpec((TILE, 128), lambda p, j, s: (query_tile(s[0], j), 0)),
                pl.BlockSpec((8, rows), lambda p, j, s: (0, 0)),
                pl.BlockSpec((TILE, 128), lambda p, j, s: (query_tile(s[0], j), p)),
                pl.BlockSpec((rows, 128), lambda p, j, s: (0, pairs + p)),
                pl.BlockSpec((rows, 128), lambda p, j, s: (0, 2 * pairs + p)),
                pl.BlockSpec((TILE, 128), lambda p, j, s: (own_tile(s[0], j), p)),
                pl.BlockSpec((TILE, 128), lambda p, j, s: (own_tile(s[0], j), 0)),
                pl.BlockSpec((TILE, 128), lambda p, j, s: (own_tile(s[0], j), 0)),
            ],
            out_specs=[
                pl.BlockSpec((TILE, 128), lambda p, j, s: (own_tile(s[0], j), p)),
                pl.BlockSpec((own, 128), lambda p, j, s: (0, p)),
                pl.BlockSpec((own, 128), lambda p, j, s: (0, p)),
            ],
            scratch_shapes=[
                pltpu.VMEM((own // TILE, TILE, 5 * TILE), jnp.float32),
                pltpu.VMEM((128, rows), jnp.float32),
                pltpu.VMEM((128, rows), jnp.float32),
            ],
        ),
        out_shape=[
            jax.ShapeDtypeStruct((own, width), jnp.bfloat16),
            jax.ShapeDtypeStruct((own, width), jnp.float32),
            jax.ShapeDtypeStruct((own, width), jnp.float32),
        ],
        compiler_params=pltpu.CompilerParams(vmem_limit_bytes=48 << 20),
        cost_estimate=pl.CostEstimate(
            flops=10 * 17 * TILE * TILE * width * 4, bytes_accessed=40 << 20, transcendentals=0
        ),
    )(side, ids_col, ids_row, qkv, qkv, qkv, outgrad, lse, inner)


def attend_far_kernel(
    side_ref, ids_col_ref, ids_row_ref, q_ref, k_ref, v_ref, do_ref, lse_ref, inner_ref,
    dk_in_ref, dv_in_ref, dk_ref, dv_ref, bias_ref,
):
    pair = pl.program_id(0)
    side = side_ref[0]

    @pl.when(pair == 0)
    def _():
        bias_ref[...] = mask_bias(
            jnp.where(side == 0, 2 * W, 0), W, ids_col_ref[:, :1], ids_row_ref[:1, W : 2 * W]
        )

    scaled = q_ref[...] * jnp.bfloat16(HD**-0.5)
    outgrad = do_ref[...]
    queries = pair_split(scaled)
    outgrads = pair_split(outgrad)
    turned_q = jnp.transpose(scaled.astype(jnp.float32)).astype(jnp.bfloat16)
    turned_do = jnp.transpose(outgrad.astype(jnp.float32)).astype(jnp.bfloat16)
    keys, values = k_ref[...], v_ref[...]
    dk_parts, dv_parts = [], []
    for h in range(2):
        logsum = pick_lane(lse_ref[...], 2 * pair + h)
        inner = pick_lane(inner_ref[...], 2 * pair + h)
        scores = dot_nt(queries[h], keys) + bias_ref[...]
        probs = jnp.exp(scores - logsum)
        prob_grad = dot_nt(outgrads[h], values)
        score_grad = (probs * (prob_grad - inner)).astype(jnp.bfloat16)
        head = slice(h * HD, (h + 1) * HD)
        dv_parts.append(dot_nn(turned_do[head], probs.astype(jnp.bfloat16)))
        dk_parts.append(dot_nn(turned_q[head], score_grad))
    dk_far = jnp.transpose(jnp.concatenate(dk_parts, axis=0))
    dv_far = jnp.transpose(jnp.concatenate(dv_parts, axis=0))
    near = pl.multiple_of(jnp.where(side == 0, W, 0), W)
    rest = pl.multiple_of(jnp.where(side == 0, 0, W), W)
    dk_ref[pl.ds(near, W), :] = (dk_in_ref[pl.ds(near, W), :] + dk_far).astype(jnp.bfloat16)
    dv_ref[pl.ds(near, W), :] = (dv_in_ref[pl.ds(near, W), :] + dv_far).astype(jnp.bfloat16)
    dk_ref[pl.ds(rest, W), :] = dk_in_ref[pl.ds(rest, W), :].astype(jnp.bfloat16)
    dv_ref[pl.ds(rest, W), :] = dv_in_ref[pl.ds(rest, W), :].astype(jnp.bfloat16)


def attend_far(side, ids_col, ids_row, qkv, far_outgrad, far_lse, far_inner, dk, dv):
    rows, width = qkv.shape[0], qkv.shape[1] // 3
    pairs = width // 128
    own = rows - W
    far = lambda p, s: (jnp.where(s[0] == 0, 2, 0), p)
    return pl.pallas_call(
        attend_far_kernel,
        name="attend_far",
        grid_spec=pltpu.PrefetchScalarGridSpec(
            num_scalar_prefetch=1,
            grid=(pairs,),
            in_specs=[
                pl.BlockSpec((W, 128), lambda p, s: (jnp.where(s[0] == 0, 2, 0), 0)),
                pl.BlockSpec((8, rows), lambda p, s: (0, 0)),
                pl.BlockSpec((W, 128), far),
                pl.BlockSpec((W, 128), lambda p, s: (1, pairs + p)),
                pl.BlockSpec((W, 128), lambda p, s: (1, 2 * pairs + p)),
                pl.BlockSpec((W, 128), lambda p, s: (0, p)),
                pl.BlockSpec((W, 128), lambda p, s: (0, 0)),
                pl.BlockSpec((W, 128), lambda p, s: (0, 0)),
                pl.BlockSpec((own, 128), lambda p, s: (0, p)),
                pl.BlockSpec((own, 128), lambda p, s: (0, p)),
            ],
            out_specs=[
                pl.BlockSpec((own, 128), lambda p, s: (0, p)),
                pl.BlockSpec((own, 128), lambda p, s: (0, p)),
            ],
            scratch_shapes=[pltpu.VMEM((W, W), jnp.float32)],
        ),
        out_shape=[jax.ShapeDtypeStruct((own, width), jnp.bfloat16)] * 2,
        compiler_params=pltpu.CompilerParams(vmem_limit_bytes=48 << 20),
        cost_estimate=pl.CostEstimate(
            flops=8 * 4 * TILE * TILE * width * 4, bytes_accessed=20 << 20, transcendentals=0
        ),
    )(side, ids_col, ids_row, qkv, qkv, qkv, far_outgrad, far_lse, far_inner, dk, dv)


COLOURS = ((("y", "x", "z"), 3), (("x", "y", "z"), 3), (("z", "y", "x"), 2))


def axis_parts():
    total = lax.axis_size("dp")
    inner = 2 ** ((total.bit_length() - 1) // 2)
    return {"z": total // inner, "x": inner, "y": lax.axis_size("seq")}


def place(axis):
    inner = axis_parts()["x"]
    if axis == "y":
        return lax.axis_index("seq")
    return lax.axis_index("dp") // inner if axis == "z" else lax.axis_index("dp") % inner


def shift(x, axis):
    parts = axis_parts()
    size, inner = parts[axis], parts["x"]
    if axis == "y":
        return lax.ppermute(x, "seq", [(i, (i + 1) % size) for i in range(size)])
    total = parts["z"] * inner
    if axis == "z":
        return lax.ppermute(x, "dp", [(i, (i + inner) % total) for i in range(total)])
    return lax.ppermute(x, "dp", [(i, i - i % inner + (i + 1) % inner) for i in range(total)])


def add_up(terms):
    total = terms[0].astype(jnp.float32)
    for term in terms[1:]:
        total = total + term.astype(jnp.float32)
    return total


def scatter_colour(partial_rows, order):
    parts = axis_parts()
    columns = partial_rows.shape[1]
    left = ["z", "x", "y"]
    sources = [partial_rows.reshape(*[parts[a] for a in left], -1, columns)]
    for axis in order:
        size, spot = parts[axis], place(axis)
        at = left.index(axis)

        def piece(index):
            return [lax.dynamic_index_in_dim(s, index, at, keepdims=False) for s in sources]

        got = []
        for step in range(size - 1):
            chunk = (spot + 2 * size - 1 - step) % size
            got = [shift(add_up(piece(chunk) + got).astype(jnp.bfloat16), axis)]
        sources = piece(spot) + got
        left.remove(axis)
    return add_up(sources)


def scatter_rows(partial_rows):
    columns = partial_rows.shape[1] // 128
    shares = sum(share for _, share in COLOURS)
    cuts, begin, pieces = [], 0, []
    for order, share in COLOURS:
        cuts.append((begin, order))
        begin += share
    for start, share_order in enumerate(cuts):
        low = share_order[0] * columns // shares * 128
        high = cuts[start + 1][0] * columns // shares * 128 if start + 1 < len(cuts) else columns * 128
        pieces.append(scatter_colour(partial_rows[:, low:high], share_order[1]))
    return jnp.concatenate(pieces, axis=1)


def adam_step(master, gradient, first, second, step_rate):
    first_new = beta_one * first + (1.0 - beta_one) * gradient
    second_new = beta_two * second + (1.0 - beta_two) * gradient * gradient
    direction = first_new / bias_one / (jnp.sqrt(second_new / bias_two) + adam_eps)
    return (master - step_rate * (direction + weight_decay * master), first_new, second_new)


def on_device(
    tokens,
    cotangent,
    segments,
    weight_qkv,
    weight_out,
    weight_ffn,
    vectors,
    first_qkv,
    first_out,
    first_ffn,
    first_vec,
    second_qkv,
    second_out,
    second_ffn,
    second_vec,
    outer_qkv,
    outer_out,
    outer_ffn,
    outer_vec,
):
    masters = (weight_qkv, weight_out, weight_ffn, vectors)
    lowered = [master.astype(jnp.bfloat16) for master in masters]
    gathered = (
        lax.all_gather(lowered[0], ("dp", "seq"), axis=0, tiled=True),
        lax.all_gather(lowered[1], ("dp", "seq"), axis=0, tiled=True),
        lax.all_gather(lowered[2], ("dp", "seq"), axis=1, tiled=True),
        lax.all_gather(lowered[3], ("dp", "seq"), axis=0, tiled=True),
    )
    full_qkv, full_out, full_ffn, full_vec = gathered
    width = full_out.shape[0]
    vector_values = full_vec.astype(jnp.float32)
    pieces = [vector_values[position * width : (position + 1) * width] for position in range(8)]
    (
        bias_query,
        bias_value,
        bias_output,
        bias_second,
        gain_first,
        shift_first,
        gain_second,
        shift_second,
    ) = pieces
    bias_hidden = vector_values[8 * width :]
    token_rows = tokens[0]
    local_rows = token_rows.shape[0]
    side = lax.axis_index("seq")
    is_first = side == 0
    side_operand = jnp.reshape(side, (1,)).astype(jnp.int32)
    far_tokens = partner(jnp.where(is_first, token_rows[local_rows - W :], token_rows[:W]), "seq", 0)
    wide_tokens = jnp.where(
        is_first,
        jnp.concatenate([token_rows, far_tokens], axis=0),
        jnp.concatenate([far_tokens, token_rows], axis=0),
    )
    joined_bias = jnp.concatenate([bias_query, jnp.zeros_like(bias_query), bias_value])
    projected = (
        jnp.dot(wide_tokens, full_qkv, preferred_element_type=jnp.float32) + joined_bias
    ).astype(jnp.bfloat16)
    wide_ids = lax.dynamic_slice_in_dim(segments[0], side * (local_rows - W), local_rows + W, 0)
    ids_col = jnp.broadcast_to(wide_ids[:, None], (local_rows + W, 128))
    ids_row = jnp.broadcast_to(wide_ids[None, :], (8, local_rows + W))
    attended, attended_wide, logsum = attend(side_operand, ids_col, ids_row, projected)
    branch = jnp.dot(attended, full_out, preferred_element_type=jnp.float32) + bias_output
    residue_first = token_rows.astype(jnp.float32) + branch
    hidden_in, first_pullback = jax.vjp(layer_norm, residue_first, gain_first, shift_first)
    hidden_low = hidden_in.astype(jnp.bfloat16)
    inner = jnp.dot(hidden_low, full_ffn[0], preferred_element_type=jnp.float32) + bias_hidden
    activated, gelu_pullback = jax.vjp(partial(jax.nn.gelu, approximate=False), inner)
    activated_low = activated.astype(jnp.bfloat16)
    second_branch = (
        lax.dot_general(
            activated_low, full_ffn[1], (((1,), (1,)), ((), ())), preferred_element_type=jnp.float32
        )
        + bias_second
    )
    residue_second = hidden_in + second_branch
    result, second_pullback = jax.vjp(layer_norm, residue_second, gain_second, shift_second)
    upstream = cotangent[0].astype(jnp.float32)
    residue_second_grad, gain_second_grad, shift_second_grad = second_pullback(upstream)
    branch_two_low = residue_second_grad.astype(jnp.bfloat16)
    bias_second_grad = jnp.sum(branch_two_low.astype(jnp.float32), axis=0)
    down_grad = dot_tn(branch_two_low, activated_low).astype(jnp.bfloat16)
    activated_grad = jnp.dot(branch_two_low, full_ffn[1], preferred_element_type=jnp.float32)
    (inner_grad,) = gelu_pullback(activated_grad)
    inner_low = inner_grad.astype(jnp.bfloat16)
    bias_hidden_grad = jnp.sum(inner_low.astype(jnp.float32), axis=0)
    up_grad = dot_tn(hidden_low, inner_low).astype(jnp.bfloat16)
    hidden_grad = residue_second_grad + lax.dot_general(
        inner_low, full_ffn[0], (((1,), (1,)), ((), ())), preferred_element_type=jnp.float32
    )
    residue_first_grad, gain_first_grad, shift_first_grad = first_pullback(hidden_grad)
    branch_low = residue_first_grad.astype(jnp.bfloat16)
    bias_output_grad = jnp.sum(branch_low.astype(jnp.float32), axis=0)
    out_weight_grad = dot_tn(attended, branch_low).astype(jnp.bfloat16)
    mixed_grad = lax.dot_general(
        branch_low, full_out, (((1,), (1,)), ((), ())), preferred_element_type=jnp.float32
    ).astype(jnp.bfloat16)

    heads = width // HD
    head_of = jnp.arange(width, dtype=jnp.int32)[:, None] // HD
    collect = (head_of == jnp.arange(128, dtype=jnp.int32)[None, :]).astype(jnp.float32)
    inner_sums = jnp.dot(
        attended_wide * mixed_grad.astype(jnp.float32), collect, precision=lax.Precision.HIGHEST
    )

    def near_rows(x):
        return jnp.where(is_first, x[local_rows - W :], x[:W])

    far_stats = partner(
        jnp.concatenate([near_rows(logsum)[:, :heads], near_rows(inner_sums)[:, :heads]], axis=1),
        "seq",
        0,
    )
    far_outgrad = partner(near_rows(mixed_grad), "seq", 0)
    lane_pad = ((0, 0), (0, 128 - heads))
    far_logsum = jnp.pad(far_stats[:, :heads], lane_pad)
    far_inner = jnp.pad(far_stats[:, heads:], lane_pad)
    query_grad, key_near, value_near = attend_back(
        side_operand, ids_col, ids_row, projected, mixed_grad, logsum, inner_sums
    )
    key_grad, value_grad = attend_far(
        side_operand, ids_col, ids_row, projected, far_outgrad, far_logsum, far_inner, key_near, value_near
    )
    projected_grad = jnp.concatenate([query_grad, key_grad, value_grad], axis=1)
    qkv_weight_grad = dot_tn(token_rows, projected_grad).astype(jnp.bfloat16)
    projected_sums = jnp.sum(projected_grad.astype(jnp.float32), axis=0)
    input_grad = residue_first_grad + lax.dot_general(
        projected_grad, full_qkv, (((1,), (1,)), ((), ())), preferred_element_type=jnp.float32
    )
    vector_grad = jnp.concatenate(
        [
            projected_sums[:width],
            projected_sums[2 * width :],
            bias_output_grad,
            bias_second_grad,
            gain_first_grad,
            shift_first_grad,
            gain_second_grad,
            shift_second_grad,
            bias_hidden_grad,
        ]
    )
    vector_rows = vector_grad.reshape(width, -1)
    entries = vector_rows.shape[1]
    small = jnp.pad(vector_rows, ((0, 0), (0, 128 - entries))).astype(jnp.bfloat16)
    rest = scatter_rows(jnp.concatenate([qkv_weight_grad, out_weight_grad, small], axis=1))
    summed = (
        rest[:, : 3 * width],
        rest[:, 3 * width : 4 * width],
        jnp.stack([scatter_rows(up_grad), scatter_rows(down_grad)]),
        rest[:, 4 * width : 4 * width + entries].reshape(-1),
    )
    firsts = (first_qkv[0], first_out[0], first_ffn[0], first_vec[0])
    seconds = (second_qkv[0], second_out[0], second_ffn[0], second_vec[0])
    outers = (outer_qkv, outer_out, outer_ffn, outer_vec)
    stepped = [
        adam_step(
            masters[member], summed[member], firsts[member], seconds[member], step_rates[member]
        )
        for member in range(4)
    ]
    changes = [masters[member] - stepped[member][0] for member in range(4)]
    lowered_changes = [change.astype(jnp.bfloat16) for change in changes]
    other_changes = [partner(change, "grp", 0) for change in lowered_changes]
    deltas = [
        (lowered_changes[member].astype(jnp.float32) + other_changes[member].astype(jnp.float32)) / 2
        for member in range(4)
    ]
    momenta = [outer_beta * outers[member] + deltas[member] for member in range(4)]
    renewed = [
        masters[member] - outer_rate * (deltas[member] + outer_beta * momenta[member])
        for member in range(4)
    ]
    return (
        result.astype(jnp.bfloat16)[None],
        input_grad[None],
        summed[0][None],
        summed[1][None],
        summed[2][None],
        summed[3][None],
        stepped[0][1][None],
        stepped[1][1][None],
        stepped[2][1][None],
        stepped[3][1][None],
        stepped[0][2][None],
        stepped[1][2][None],
        stepped[2][2][None],
        stepped[3][2][None],
        deltas[0],
        deltas[1],
        deltas[2],
        deltas[3],
        momenta[0],
        momenta[1],
        momenta[2],
        momenta[3],
        renewed[0],
        renewed[1],
        renewed[2],
        renewed[3],
    )


def solution(mesh):
    return jax.shard_map(
        on_device,
        mesh=mesh,
        in_specs=(
            P(("grp", "dp"), "seq", None),
            P(("grp", "dp"), "seq", None),
            P(("grp", "dp"), None),
            P(("dp", "seq"), None),
            P(("dp", "seq"), None),
            P(None, ("dp", "seq"), None),
            P(("dp", "seq")),
            P("grp", ("dp", "seq"), None),
            P("grp", ("dp", "seq"), None),
            P("grp", None, ("dp", "seq"), None),
            P("grp", ("dp", "seq")),
            P("grp", ("dp", "seq"), None),
            P("grp", ("dp", "seq"), None),
            P("grp", None, ("dp", "seq"), None),
            P("grp", ("dp", "seq")),
            P(("dp", "seq"), None),
            P(("dp", "seq"), None),
            P(None, ("dp", "seq"), None),
            P(("dp", "seq")),
        ),
        out_specs=(
            P(("grp", "dp"), "seq", None),
            P(("grp", "dp"), "seq", None),
            P("grp", ("dp", "seq"), None),
            P("grp", ("dp", "seq"), None),
            P("grp", None, ("dp", "seq"), None),
            P("grp", ("dp", "seq")),
            P("grp", ("dp", "seq"), None),
            P("grp", ("dp", "seq"), None),
            P("grp", None, ("dp", "seq"), None),
            P("grp", ("dp", "seq")),
            P("grp", ("dp", "seq"), None),
            P("grp", ("dp", "seq"), None),
            P("grp", None, ("dp", "seq"), None),
            P("grp", ("dp", "seq")),
            P(("dp", "seq"), None),
            P(("dp", "seq"), None),
            P(None, ("dp", "seq"), None),
            P(("dp", "seq")),
            P(("dp", "seq"), None),
            P(("dp", "seq"), None),
            P(None, ("dp", "seq"), None),
            P(("dp", "seq")),
            P(("dp", "seq"), None),
            P(("dp", "seq"), None),
            P(None, ("dp", "seq"), None),
            P(("dp", "seq")),
        ),
        check_vma=False,
    )
```

```python
from functools import partial

import jax
import jax.numpy as jnp
from jax import lax
from jax.experimental import pallas as pl
from jax.experimental.pallas import tpu as pltpu
from jax.sharding import PartitionSpec as P

HD = 64
W = 512


beta_one = 0.9
beta_two = 0.95
adam_eps = 1e-08
weight_decay = 0.1
bias_one = 1.0 - 0.9**10
bias_two = 1.0 - 0.95**10
step_rates = (0.01, 0.1, 0.005, 0.2)
outer_rate = 0.7
outer_beta = 0.9
norm_eps = 1e-05
score_fill = -1e30


def partner(x, axis, stride):
    return lax.ppermute(x, axis, [(i, i ^ 1 << stride) for i in range(lax.axis_size(axis))])


def layer_norm(residue, norm_gain, norm_shift):
    average = jnp.mean(residue, axis=-1, keepdims=True)
    centred = residue - average
    variance = jnp.mean(centred * centred, axis=-1, keepdims=True)
    return centred * lax.rsqrt(variance + norm_eps) * norm_gain + norm_shift


TILE = 256
LENGTHS = (3, 4, 5, 5)


def first_tile(side, j):
    return jnp.where(side == 0, jnp.maximum(j - 2, 0), 3 - j)


def query_tile(side, j):
    return jnp.where(side == 0, j, 5 - j)


def own_tile(side, j):
    return jnp.where(side == 0, j, 3 - j)


def dot_nt(a, b):
    return lax.dot_general(a, b, (((1,), (1,)), ((), ())), preferred_element_type=jnp.float32)


def dot_tn(a, b):
    return lax.dot_general(a, b, (((0,), (0,)), ((), ())), preferred_element_type=jnp.float32)


def dot_nn(a, b):
    return lax.dot_general(a, b, (((1,), (0,)), ((), ())), preferred_element_type=jnp.float32)


def mask_bias(query_start, key_start, query_ids, key_ids):
    rows, cols = query_ids.shape[0], key_ids.shape[1]
    relative = (
        lax.broadcasted_iota(jnp.int32, (rows, cols), 1)
        - lax.broadcasted_iota(jnp.int32, (rows, cols), 0)
        + (key_start - query_start)
    )
    allowed = (relative <= W) & (relative >= -W) & (query_ids == key_ids)
    return jnp.where(allowed, 0.0, score_fill)


def pair_split(x):
    lane = lax.broadcasted_iota(jnp.int32, x.shape, 1)
    zero = jnp.zeros_like(x)
    return jnp.where(lane < HD, x, zero), jnp.where(lane < HD, zero, x)


def pick_lane(x, index):
    lane = lax.broadcasted_iota(jnp.int32, x.shape, 1)
    return jnp.sum(jnp.where(lane == index, x, 0.0), axis=1, keepdims=True)


def attend_kernel(side_ref, ids_col_ref, ids_row_ref, q_ref, k_ref, v_ref, o_ref, wide_ref, lse_ref, bias_ref):
    j, pair = pl.program_id(0), pl.program_id(1)
    side = side_ref[0]

    def run(length):
        span = length * TILE
        start = pl.multiple_of(first_tile(side, j) * TILE, TILE)

        @pl.when(pair == 0)
        def _():
            bias_ref[:, :span] = mask_bias(
                query_tile(side, j) * TILE,
                start,
                ids_col_ref[:, :1],
                ids_row_ref[:1, pl.ds(start, span)],
            )
            lse_ref[...] = jnp.zeros_like(lse_ref)

        queries = pair_split(q_ref[...] * jnp.bfloat16(HD**-0.5))
        keys = k_ref[pl.ds(start, span), :]
        values = pair_split(v_ref[pl.ds(start, span), :])
        total = None
        lane = lax.broadcasted_iota(jnp.int32, lse_ref.shape, 1)
        for h in range(2):
            scores = dot_nt(queries[h], keys) + bias_ref[:, :span]
            maximum = jnp.max(scores, axis=1, keepdims=True)
            exponent = jnp.exp(scores - maximum)
            denominator = jnp.sum(exponent, axis=1, keepdims=True)
            weights = (exponent * (1.0 / denominator)).astype(jnp.bfloat16)
            part = dot_nn(weights, values[h])
            total = part if total is None else total + part
            logsum = maximum + jnp.log(denominator)
            lse_ref[...] = jnp.where(lane == 2 * pair + h, logsum, lse_ref[...])
        o_ref[...] = total.astype(jnp.bfloat16)
        wide_ref[...] = total

    for length in sorted(set(LENGTHS)):
        hits = [i for i in range(4) if LENGTHS[i] == length]

        @pl.when((j >= hits[0]) & (j <= hits[-1]))
        def _():
            run(length)


def attend(side, ids_col, ids_row, qkv):
    rows, width = qkv.shape[0], qkv.shape[1] // 3
    pairs = width // 128
    own = rows - W
    return pl.pallas_call(
        attend_kernel,
        name="attend",
        grid_spec=pltpu.PrefetchScalarGridSpec(
            num_scalar_prefetch=1,
            grid=(own // TILE, pairs),
            in_specs=[
                pl.BlockSpec((TILE, 128), lambda j, p, s: (query_tile(s[0], j), 0)),
                pl.BlockSpec((8, rows), lambda j, p, s: (0, 0)),
                pl.BlockSpec((TILE, 128), lambda j, p, s: (query_tile(s[0], j), p)),
                pl.BlockSpec((rows, 128), lambda j, p, s: (0, pairs + p)),
                pl.BlockSpec((rows, 128), lambda j, p, s: (0, 2 * pairs + p)),
            ],
            out_specs=[
                pl.BlockSpec((TILE, 128), lambda j, p, s: (own_tile(s[0], j), p)),
                pl.BlockSpec((TILE, 128), lambda j, p, s: (own_tile(s[0], j), p)),
                pl.BlockSpec((TILE, 128), lambda j, p, s: (own_tile(s[0], j), 0)),
            ],
            scratch_shapes=[pltpu.VMEM((TILE, 5 * TILE), jnp.float32)],
        ),
        out_shape=[
            jax.ShapeDtypeStruct((own, width), jnp.bfloat16),
            jax.ShapeDtypeStruct((own, width), jnp.float32),
            jax.ShapeDtypeStruct((own, 128), jnp.float32),
        ],
        compiler_params=pltpu.CompilerParams(vmem_limit_bytes=48 << 20),
        cost_estimate=pl.CostEstimate(
            flops=4 * 17 * TILE * TILE * width * 4, bytes_accessed=30 << 20, transcendentals=0
        ),
    )(side, ids_col, ids_row, qkv, qkv, qkv)


def attend_back_kernel(
    side_ref, ids_col_ref, ids_row_ref, q_ref, k_ref, v_ref, do_ref, lse_ref, inner_ref,
    dq_ref, dk_ref, dv_ref, bias_ref, dkt_ref, dvt_ref,
):
    pair, j = pl.program_id(0), pl.program_id(1)
    side = side_ref[0]
    own = dk_ref.shape[0]

    @pl.when(j == 0)
    def _():
        dkt_ref[...] = jnp.zeros_like(dkt_ref)
        dvt_ref[...] = jnp.zeros_like(dvt_ref)

    def run(length):
        span = length * TILE
        start = pl.multiple_of(first_tile(side, j) * TILE, TILE)

        @pl.when(pair == 0)
        def _():
            bias_ref[j, :, :span] = mask_bias(
                query_tile(side, j) * TILE,
                start,
                ids_col_ref[:, :1],
                ids_row_ref[:1, pl.ds(start, span)],
            )

        scaled = q_ref[...] * jnp.bfloat16(HD**-0.5)
        outgrad = do_ref[...]
        queries = pair_split(scaled)
        outgrads = pair_split(outgrad)
        turned_q = jnp.transpose(scaled.astype(jnp.float32)).astype(jnp.bfloat16)
        turned_do = jnp.transpose(outgrad.astype(jnp.float32)).astype(jnp.bfloat16)
        keys = k_ref[pl.ds(start, span), :]
        values = v_ref[pl.ds(start, span), :]
        key_parts = pair_split(keys)
        total = None
        for h in range(2):
            logsum = pick_lane(lse_ref[...], 2 * pair + h)
            inner = pick_lane(inner_ref[...], 2 * pair + h)
            scores = dot_nt(queries[h], keys) + bias_ref[j, :, :span]
            probs = jnp.exp(scores - logsum)
            prob_grad = dot_nt(outgrads[h], values)
            score_grad = (probs * (prob_grad - inner)).astype(jnp.bfloat16)
            part = dot_nn(score_grad, key_parts[h])
            total = part if total is None else total + part
            head = slice(h * HD, (h + 1) * HD)
            dvt_ref[head, pl.ds(start, span)] += dot_nn(turned_do[head], probs.astype(jnp.bfloat16))
            dkt_ref[head, pl.ds(start, span)] += dot_nn(turned_q[head], score_grad)
        dq_ref[...] = (total * HD**-0.5).astype(jnp.bfloat16)

    for length in sorted(set(LENGTHS)):
        hits = [i for i in range(4) if LENGTHS[i] == length]

        @pl.when((j >= hits[0]) & (j <= hits[-1]))
        def _():
            run(length)

    @pl.when(j == pl.num_programs(1) - 1)
    def _():
        at = pl.multiple_of(side * W, W)
        dk_ref[...] = jnp.transpose(dkt_ref[:, pl.ds(at, own)])
        dv_ref[...] = jnp.transpose(dvt_ref[:, pl.ds(at, own)])


def attend_back(side, ids_col, ids_row, qkv, outgrad, lse, inner):
    rows, width = qkv.shape[0], qkv.shape[1] // 3
    pairs = width // 128
    own = rows - W
    return pl.pallas_call(
        attend_back_kernel,
        name="attend_back",
        grid_spec=pltpu.PrefetchScalarGridSpec(
            num_scalar_prefetch=1,
            grid=(pairs, own // TILE),
            in_specs=[
                pl.BlockSpec((TILE, 128), lambda p, j, s: (query_tile(s[0], j), 0)),
                pl.BlockSpec((8, rows), lambda p, j, s: (0, 0)),
                pl.BlockSpec((TILE, 128), lambda p, j, s: (query_tile(s[0], j), p)),
                pl.BlockSpec((rows, 128), lambda p, j, s: (0, pairs + p)),
                pl.BlockSpec((rows, 128), lambda p, j, s: (0, 2 * pairs + p)),
                pl.BlockSpec((TILE, 128), lambda p, j, s: (own_tile(s[0], j), p)),
                pl.BlockSpec((TILE, 128), lambda p, j, s: (own_tile(s[0], j), 0)),
                pl.BlockSpec((TILE, 128), lambda p, j, s: (own_tile(s[0], j), 0)),
            ],
            out_specs=[
                pl.BlockSpec((TILE, 128), lambda p, j, s: (own_tile(s[0], j), p)),
                pl.BlockSpec((own, 128), lambda p, j, s: (0, p)),
                pl.BlockSpec((own, 128), lambda p, j, s: (0, p)),
            ],
            scratch_shapes=[
                pltpu.VMEM((own // TILE, TILE, 5 * TILE), jnp.float32),
                pltpu.VMEM((128, rows), jnp.float32),
                pltpu.VMEM((128, rows), jnp.float32),
            ],
        ),
        out_shape=[
            jax.ShapeDtypeStruct((own, width), jnp.bfloat16),
            jax.ShapeDtypeStruct((own, width), jnp.float32),
            jax.ShapeDtypeStruct((own, width), jnp.float32),
        ],
        compiler_params=pltpu.CompilerParams(vmem_limit_bytes=48 << 20),
        cost_estimate=pl.CostEstimate(
            flops=10 * 17 * TILE * TILE * width * 4, bytes_accessed=40 << 20, transcendentals=0
        ),
    )(side, ids_col, ids_row, qkv, qkv, qkv, outgrad, lse, inner)


def attend_far_kernel(
    side_ref, ids_col_ref, ids_row_ref, q_ref, k_ref, v_ref, do_ref, lse_ref, inner_ref,
    dk_in_ref, dv_in_ref, dk_ref, dv_ref, bias_ref,
):
    pair = pl.program_id(0)
    side = side_ref[0]

    @pl.when(pair == 0)
    def _():
        bias_ref[...] = mask_bias(
            jnp.where(side == 0, 2 * W, 0), W, ids_col_ref[:, :1], ids_row_ref[:1, W : 2 * W]
        )

    scaled = q_ref[...] * jnp.bfloat16(HD**-0.5)
    outgrad = do_ref[...]
    queries = pair_split(scaled)
    outgrads = pair_split(outgrad)
    turned_q = jnp.transpose(scaled.astype(jnp.float32)).astype(jnp.bfloat16)
    turned_do = jnp.transpose(outgrad.astype(jnp.float32)).astype(jnp.bfloat16)
    keys, values = k_ref[...], v_ref[...]
    dk_parts, dv_parts = [], []
    for h in range(2):
        logsum = pick_lane(lse_ref[...], 2 * pair + h)
        inner = pick_lane(inner_ref[...], 2 * pair + h)
        scores = dot_nt(queries[h], keys) + bias_ref[...]
        probs = jnp.exp(scores - logsum)
        prob_grad = dot_nt(outgrads[h], values)
        score_grad = (probs * (prob_grad - inner)).astype(jnp.bfloat16)
        head = slice(h * HD, (h + 1) * HD)
        dv_parts.append(dot_nn(turned_do[head], probs.astype(jnp.bfloat16)))
        dk_parts.append(dot_nn(turned_q[head], score_grad))
    dk_far = jnp.transpose(jnp.concatenate(dk_parts, axis=0))
    dv_far = jnp.transpose(jnp.concatenate(dv_parts, axis=0))
    near = pl.multiple_of(jnp.where(side == 0, W, 0), W)
    rest = pl.multiple_of(jnp.where(side == 0, 0, W), W)
    dk_ref[pl.ds(near, W), :] = (dk_in_ref[pl.ds(near, W), :] + dk_far).astype(jnp.bfloat16)
    dv_ref[pl.ds(near, W), :] = (dv_in_ref[pl.ds(near, W), :] + dv_far).astype(jnp.bfloat16)
    dk_ref[pl.ds(rest, W), :] = dk_in_ref[pl.ds(rest, W), :].astype(jnp.bfloat16)
    dv_ref[pl.ds(rest, W), :] = dv_in_ref[pl.ds(rest, W), :].astype(jnp.bfloat16)


def attend_far(side, ids_col, ids_row, qkv, far_outgrad, far_lse, far_inner, dk, dv):
    rows, width = qkv.shape[0], qkv.shape[1] // 3
    pairs = width // 128
    own = rows - W
    far = lambda p, s: (jnp.where(s[0] == 0, 2, 0), p)
    return pl.pallas_call(
        attend_far_kernel,
        name="attend_far",
        grid_spec=pltpu.PrefetchScalarGridSpec(
            num_scalar_prefetch=1,
            grid=(pairs,),
            in_specs=[
                pl.BlockSpec((W, 128), lambda p, s: (jnp.where(s[0] == 0, 2, 0), 0)),
                pl.BlockSpec((8, rows), lambda p, s: (0, 0)),
                pl.BlockSpec((W, 128), far),
                pl.BlockSpec((W, 128), lambda p, s: (1, pairs + p)),
                pl.BlockSpec((W, 128), lambda p, s: (1, 2 * pairs + p)),
                pl.BlockSpec((W, 128), lambda p, s: (0, p)),
                pl.BlockSpec((W, 128), lambda p, s: (0, 0)),
                pl.BlockSpec((W, 128), lambda p, s: (0, 0)),
                pl.BlockSpec((own, 128), lambda p, s: (0, p)),
                pl.BlockSpec((own, 128), lambda p, s: (0, p)),
            ],
            out_specs=[
                pl.BlockSpec((own, 128), lambda p, s: (0, p)),
                pl.BlockSpec((own, 128), lambda p, s: (0, p)),
            ],
            scratch_shapes=[pltpu.VMEM((W, W), jnp.float32)],
        ),
        out_shape=[jax.ShapeDtypeStruct((own, width), jnp.bfloat16)] * 2,
        compiler_params=pltpu.CompilerParams(vmem_limit_bytes=48 << 20),
        cost_estimate=pl.CostEstimate(
            flops=8 * 4 * TILE * TILE * width * 4, bytes_accessed=20 << 20, transcendentals=0
        ),
    )(side, ids_col, ids_row, qkv, qkv, qkv, far_outgrad, far_lse, far_inner, dk, dv)


AXES = ("z", "x", "y")
GATHER_ORDERS = ((("z", "x", "y"), 3), (("z", "y", "x"), 3), (("x", "y", "z"), 2))
SCATTER_ORDERS = ((("y", "x", "z"), 3), (("x", "y", "z"), 3), (("z", "y", "x"), 2))
PIECE = 2048


def axis_parts():
    total = lax.axis_size("dp")
    inner = 2 ** ((total.bit_length() - 1) // 2)
    return {"z": total // inner, "x": inner, "y": lax.axis_size("seq")}


def places():
    inner = axis_parts()["x"]
    row = lax.axis_index("dp")
    return {"z": lax.div(row, inner), "x": lax.rem(row, inner), "y": lax.axis_index("seq")}


def neighbour(axis, step):
    parts, spots = axis_parts(), places()
    size = parts[axis]
    spots[axis] = lax.rem(spots[axis] + step + size, size)
    return (lax.axis_index("grp"), spots["z"] * parts["x"] + spots["x"], spots["y"])


def twin():
    return (1 - lax.axis_index("grp"), lax.axis_index("dp"), lax.axis_index("seq"))


def greet(peers):
    barrier = pltpu.get_barrier_semaphore()
    for peer in peers:
        pl.semaphore_signal(barrier, inc=1, device_id=peer, device_id_type=pl.DeviceIdType.MESH)
    pl.semaphore_wait(barrier, len(peers))


def ring_peers():
    return [neighbour(axis, step) for axis in AXES for step in (1, -1)]


def flows_of(widths, orders):
    flows = []
    for member, width in enumerate(widths):
        pieces = max(1, width // PIECE)
        for piece in range(pieces):
            tiles, begin = width // pieces // 128, piece * (width // pieces)
            if tiles < len(orders):
                flows.append((member, orders[0][0], begin, tiles * 128, piece))
                continue
            total = sum(share for _, share in orders)
            low, used = 0, 0
            for order, share in orders:
                used += share
                high = -(-used * tiles // total)
                flows.append((member, order, begin + low * 128, (high - low) * 128, piece))
                low = high
    return flows


def delays(flows, gap):
    seen, found = [], []
    for member, _, _, _, piece in flows:
        if (member, piece) not in seen:
            seen.append((member, piece))
        found.append((len(seen) - 1) * gap)
    return found


def gather_kernel(shared, *refs):
    count = len(shared)
    shards, wholes = refs[:count], refs[count : 2 * count]
    send_sems, recv_sems, own_sems = refs[2 * count :]
    parts, spots = axis_parts(), places()
    core = lax.axis_index("grp")
    greet(ring_peers() + [twin()])
    spans = [s.shape[1] if shared[m] else s.shape[1] // 2 for m, s in enumerate(shards)]

    def columns(member, begin, width):
        if shared[member]:
            return pl.ds(begin, width)
        return pl.ds(pl.multiple_of(core * spans[member] + begin, 128), width)

    own = []
    for member in range(count):
        cut = columns(member, 0, spans[member])
        own.append(
            pltpu.make_async_copy(
                shards[member].at[:, cut],
                wholes[member].at[spots["z"], spots["x"], spots["y"], :, cut],
                own_sems.at[member],
            )
        )
        own[-1].start()

    flows = flows_of(spans, GATHER_ORDERS)
    chains = []
    for member, order, begin, width, _ in flows:
        cut = columns(member, begin, width)
        steps, done = [], []
        for axis in order:
            for turn in range(parts[axis] - 1):
                select = []
                for a in AXES:
                    if a == axis:
                        select.append(pl.ds(lax.rem(spots[a] + parts[a] - turn, parts[a]), 1))
                    elif a in done:
                        select.append(pl.ds(0, parts[a]))
                    else:
                        select.append(pl.ds(spots[a], 1))
                steps.append((wholes[member].at[(*select, slice(None), cut)], neighbour(axis, 1)))
            done.append(axis)
        if not shared[member]:
            steps.append((wholes[member].at[:, :, :, :, cut], twin()))
        chains.append(steps)
    number, started = 0, []
    late = delays(flows, 2)
    length = max(late[i] + len(chains[i]) for i in range(len(flows)))
    last = [None] * len(flows)
    for copy in own:
        copy.wait()
    for tick in range(length + 1):
        for i, steps in enumerate(chains):
            at = tick - late[i]
            if at < 0 or at > len(steps):
                continue
            if last[i] is not None:
                last[i].wait_recv()
            if at < len(steps):
                block, peer = steps[at]
                last[i] = pltpu.make_async_remote_copy(
                    src_ref=block,
                    dst_ref=block,
                    send_sem=send_sems.at[number],
                    recv_sem=recv_sems.at[number],
                    device_id=peer,
                    device_id_type=pl.DeviceIdType.MESH,
                )
                last[i].start()
                started.append(last[i])
                number += 1
    for copy in started:
        copy.wait_send()


def gather_all(shards, shared):
    parts = axis_parts()
    hops = sum(size - 1 for size in parts.values()) + 1
    spans = [s.shape[1] if shared[m] else s.shape[1] // 2 for m, s in enumerate(shards)]
    copies = hops * len(flows_of(spans, GATHER_ORDERS))
    wholes = pl.pallas_call(
        partial(gather_kernel, shared),
        name="gather_all",
        in_specs=[pl.BlockSpec(memory_space=pltpu.VMEM)] * len(shards),
        out_specs=[pl.BlockSpec(memory_space=pl.ANY)] * len(shards),
        out_shape=[
            jax.ShapeDtypeStruct((parts["z"], parts["x"], parts["y"], *s.shape), s.dtype) for s in shards
        ],
        scratch_shapes=[
            pltpu.SemaphoreType.DMA((copies,)),
            pltpu.SemaphoreType.DMA((copies,)),
            pltpu.SemaphoreType.DMA((len(shards),)),
        ],
        compiler_params=pltpu.CompilerParams(collective_id=0, has_side_effects=True),
    )(*shards)
    return [w.reshape(-1, w.shape[-1]) for w in wholes]


def scatter_plan(widths):
    parts = axis_parts()
    plan = []
    for member, order, begin, width, piece in flows_of(widths, SCATTER_ORDERS):
        left, levels = list(AXES), []
        for axis in order:
            left.remove(axis)
            levels.append((axis, tuple(parts[a] for a in left), [a for a in left]))
        plan.append((member, order, begin, width, piece, levels))
    return plan


def scatter_kernel(widths, *refs):
    count = len(widths)
    partials, sums = refs[:count], refs[count : 2 * count]
    plan = scatter_plan(widths)
    rest = refs[2 * count :]
    send_sems, recv_sems, load_sems = rest[:3]
    buffers = list(rest[3:])
    parts, spots = axis_parts(), places()
    rows = sums[0].shape[0]
    greet(ring_peers())
    chains, loads = [], 0
    for member, order, begin, width, _, levels in plan:
        cut = pl.ds(begin, width)
        chain = []
        source, before = partials[member], list(AXES)
        for depth, (axis, extent, left) in enumerate(levels):
            size = parts[axis]
            inbox = [buffers.pop(0) for _ in range(size - 1)]
            terms = []
            for turn in range(size):
                index = lax.rem(spots[axis] + 2 * size - 1 - turn, size)
                select = tuple(index if a == axis else slice(None) for a in before)
                if depth:
                    terms.append(source.at[select])
                else:
                    terms.append(source.at[(*select, slice(None), cut)])
            ready = []
            if depth == 0:
                for turn in range(1, size):
                    local = buffers.pop(0)
                    copy = pltpu.make_async_copy(terms[turn], local, load_sems.at[loads])
                    copy.start()
                    loads += 1
                    ready.append(copy)
                    terms[turn] = local
            chain.append((axis, extent, inbox, terms, ready))
            source, before = inbox[-1], left
        chains.append(chain)

    def accumulate(target, term, extent):
        total = 1
        for size in extent:
            total *= size

        def body(index, carry):
            where, left = [], index
            for size in reversed(extent):
                where.insert(0, lax.rem(left, size))
                left = lax.div(left, size)
            where = tuple(where)
            target[where] = (
                target[where].astype(jnp.float32) + term[where].astype(jnp.float32)
            ).astype(jnp.bfloat16)
            return carry

        lax.fori_loop(0, total, body, 0)

    flat = []
    for chain in chains:
        steps = []
        for depth, (axis, extent, inbox, terms, ready) in enumerate(chain):
            size = parts[axis]
            for turn in range(size - 1):
                steps.append((depth, axis, turn))
        flat.append(steps)
    late = delays([p[:5] for p in plan], 2)
    length = max(late[i] + len(flat[i]) for i in range(len(plan)))
    last, started, number = [None] * len(plan), [], 0
    for tick in range(length + 1):
        for i, steps in enumerate(flat):
            at = tick - late[i]
            if at < 0 or at > len(steps):
                continue
            if last[i] is not None:
                last[i].wait_recv()
                depth, axis, turn = steps[at - 1]
                _, extent, inbox, terms, ready = chains[i][depth]
                if ready:
                    ready[turn].wait()
                if at < len(steps):
                    accumulate(inbox[turn], terms[turn + 1], extent)
                else:
                    member, _, begin, width = plan[i][:4]
                    sums[member][:, begin : begin + width] = inbox[turn][...].astype(
                        jnp.float32
                    ) + terms[turn + 1][...].astype(jnp.float32)
            if at < len(steps):
                depth, axis, turn = steps[at]
                _, extent, inbox, terms, ready = chains[i][depth]
                last[i] = pltpu.make_async_remote_copy(
                    src_ref=inbox[turn - 1] if turn else terms[0],
                    dst_ref=inbox[turn],
                    send_sem=send_sems.at[number],
                    recv_sem=recv_sems.at[number],
                    device_id=neighbour(axis, 1),
                    device_id_type=pl.DeviceIdType.MESH,
                )
                last[i].start()
                started.append(last[i])
                number += 1
    for copy in started:
        copy.wait_send()


def scatter_all(partials):
    parts = axis_parts()
    widths = [p.shape[1] for p in partials]
    rows = partials[0].shape[0] // (parts["z"] * parts["x"] * parts["y"])
    buffers, copies, loads = [], 0, 0
    for _, order, _, width, _, levels in scatter_plan(widths):
        for depth, (axis, extent, _) in enumerate(levels):
            slots = parts[axis] - 1
            copies += slots
            if depth == 0:
                loads += slots
                slots *= 2
            buffers += [pltpu.VMEM((*extent, rows, width), jnp.bfloat16)] * slots
    return pl.pallas_call(
        partial(scatter_kernel, widths),
        name="scatter_all",
        in_specs=[pl.BlockSpec(memory_space=pl.ANY)] * len(partials),
        out_specs=[pl.BlockSpec(memory_space=pltpu.VMEM)] * len(partials),
        out_shape=[jax.ShapeDtypeStruct((rows, width), jnp.float32) for width in widths],
        scratch_shapes=[
            pltpu.SemaphoreType.DMA((copies,)),
            pltpu.SemaphoreType.DMA((copies,)),
            pltpu.SemaphoreType.DMA((loads,)),
            *buffers,
        ],
        compiler_params=pltpu.CompilerParams(
            collective_id=1, has_side_effects=True, vmem_limit_bytes=67043328
        ),
    )(*[p.reshape(parts["z"], parts["x"], parts["y"], rows, p.shape[1]) for p in partials])


def adam_step(master, gradient, first, second, step_rate):
    first_new = beta_one * first + (1.0 - beta_one) * gradient
    second_new = beta_two * second + (1.0 - beta_two) * gradient * gradient
    direction = first_new / bias_one / (jnp.sqrt(second_new / bias_two) + adam_eps)
    return (master - step_rate * (direction + weight_decay * master), first_new, second_new)


def on_device(
    tokens,
    cotangent,
    segments,
    weight_qkv,
    weight_out,
    weight_ffn,
    vectors,
    first_qkv,
    first_out,
    first_ffn,
    first_vec,
    second_qkv,
    second_out,
    second_ffn,
    second_vec,
    outer_qkv,
    outer_out,
    outer_ffn,
    outer_vec,
):
    masters = (weight_qkv, weight_out, weight_ffn, vectors)
    lowered = [master.astype(jnp.bfloat16) for master in masters]
    width = weight_out.shape[1]
    entries = vectors.shape[0] // weight_out.shape[0]
    vector_block = jnp.pad(lowered[3].reshape(-1, entries), ((0, 0), (0, 128 - entries)))
    full_qkv, vector_rows, full_out, full_up, full_down = gather_all(
        [lowered[0], vector_block, lowered[1], lowered[2][0], lowered[2][1]],
        (False, True, False, False, False),
    )
    full_ffn = (full_up, full_down)
    full_vec = vector_rows[:, :entries].reshape(-1)
    vector_values = full_vec.astype(jnp.float32)
    pieces = [vector_values[position * width : (position + 1) * width] for position in range(8)]
    (
        bias_query,
        bias_value,
        bias_output,
        bias_second,
        gain_first,
        shift_first,
        gain_second,
        shift_second,
    ) = pieces
    bias_hidden = vector_values[8 * width :]
    token_rows = tokens[0]
    local_rows = token_rows.shape[0]
    side = lax.axis_index("seq")
    is_first = side == 0
    side_operand = jnp.reshape(side, (1,)).astype(jnp.int32)
    far_tokens = partner(jnp.where(is_first, token_rows[local_rows - W :], token_rows[:W]), "seq", 0)
    wide_tokens = jnp.where(
        is_first,
        jnp.concatenate([token_rows, far_tokens], axis=0),
        jnp.concatenate([far_tokens, token_rows], axis=0),
    )
    joined_bias = jnp.concatenate([bias_query, jnp.zeros_like(bias_query), bias_value])
    projected = (
        jnp.dot(wide_tokens, full_qkv, preferred_element_type=jnp.float32) + joined_bias
    ).astype(jnp.bfloat16)
    wide_ids = lax.dynamic_slice_in_dim(segments[0], side * (local_rows - W), local_rows + W, 0)
    ids_col = jnp.broadcast_to(wide_ids[:, None], (local_rows + W, 128))
    ids_row = jnp.broadcast_to(wide_ids[None, :], (8, local_rows + W))
    attended, attended_wide, logsum = attend(side_operand, ids_col, ids_row, projected)
    branch = jnp.dot(attended, full_out, preferred_element_type=jnp.float32) + bias_output
    residue_first = token_rows.astype(jnp.float32) + branch
    hidden_in, first_pullback = jax.vjp(layer_norm, residue_first, gain_first, shift_first)
    hidden_low = hidden_in.astype(jnp.bfloat16)
    inner = jnp.dot(hidden_low, full_ffn[0], preferred_element_type=jnp.float32) + bias_hidden
    activated, gelu_pullback = jax.vjp(partial(jax.nn.gelu, approximate=False), inner)
    activated_low = activated.astype(jnp.bfloat16)
    second_branch = (
        lax.dot_general(
            activated_low, full_ffn[1], (((1,), (1,)), ((), ())), preferred_element_type=jnp.float32
        )
        + bias_second
    )
    residue_second = hidden_in + second_branch
    result, second_pullback = jax.vjp(layer_norm, residue_second, gain_second, shift_second)
    upstream = cotangent[0].astype(jnp.float32)
    residue_second_grad, gain_second_grad, shift_second_grad = second_pullback(upstream)
    branch_two_low = residue_second_grad.astype(jnp.bfloat16)
    bias_second_grad = jnp.sum(branch_two_low.astype(jnp.float32), axis=0)
    down_grad = dot_tn(branch_two_low, activated_low).astype(jnp.bfloat16)
    activated_grad = jnp.dot(branch_two_low, full_ffn[1], preferred_element_type=jnp.float32)
    (inner_grad,) = gelu_pullback(activated_grad)
    inner_low = inner_grad.astype(jnp.bfloat16)
    bias_hidden_grad = jnp.sum(inner_low.astype(jnp.float32), axis=0)
    up_grad = dot_tn(hidden_low, inner_low).astype(jnp.bfloat16)
    hidden_grad = residue_second_grad + lax.dot_general(
        inner_low, full_ffn[0], (((1,), (1,)), ((), ())), preferred_element_type=jnp.float32
    )
    residue_first_grad, gain_first_grad, shift_first_grad = first_pullback(hidden_grad)
    branch_low = residue_first_grad.astype(jnp.bfloat16)
    bias_output_grad = jnp.sum(branch_low.astype(jnp.float32), axis=0)
    out_weight_grad = dot_tn(attended, branch_low).astype(jnp.bfloat16)
    mixed_grad = lax.dot_general(
        branch_low, full_out, (((1,), (1,)), ((), ())), preferred_element_type=jnp.float32
    ).astype(jnp.bfloat16)

    heads = width // HD
    head_of = jnp.arange(width, dtype=jnp.int32)[:, None] // HD
    collect = (head_of == jnp.arange(128, dtype=jnp.int32)[None, :]).astype(jnp.float32)
    inner_sums = jnp.dot(
        attended_wide * mixed_grad.astype(jnp.float32), collect, precision=lax.Precision.HIGHEST
    )

    def near_rows(x):
        return jnp.where(is_first, x[local_rows - W :], x[:W])

    far_stats = partner(
        jnp.concatenate([near_rows(logsum)[:, :heads], near_rows(inner_sums)[:, :heads]], axis=1),
        "seq",
        0,
    )
    far_outgrad = partner(near_rows(mixed_grad), "seq", 0)
    lane_pad = ((0, 0), (0, 128 - heads))
    far_logsum = jnp.pad(far_stats[:, :heads], lane_pad)
    far_inner = jnp.pad(far_stats[:, heads:], lane_pad)
    query_grad, key_near, value_near = attend_back(
        side_operand, ids_col, ids_row, projected, mixed_grad, logsum, inner_sums
    )
    key_grad, value_grad = attend_far(
        side_operand, ids_col, ids_row, projected, far_outgrad, far_logsum, far_inner, key_near, value_near
    )
    projected_grad = jnp.concatenate([query_grad, key_grad, value_grad], axis=1)
    qkv_weight_grad = dot_tn(token_rows, projected_grad).astype(jnp.bfloat16)
    projected_sums = jnp.sum(projected_grad.astype(jnp.float32), axis=0)
    input_grad = residue_first_grad + lax.dot_general(
        projected_grad, full_qkv, (((1,), (1,)), ((), ())), preferred_element_type=jnp.float32
    )
    vector_grad = jnp.concatenate(
        [
            projected_sums[:width],
            projected_sums[2 * width :],
            bias_output_grad,
            bias_second_grad,
            gain_first_grad,
            shift_first_grad,
            gain_second_grad,
            shift_second_grad,
            bias_hidden_grad,
        ]
    )
    small = jnp.pad(vector_grad.reshape(width, -1), ((0, 0), (0, 128 - entries))).astype(jnp.bfloat16)
    down_sum, up_sum, qkv_sum, small_sum, out_sum = scatter_all(
        [down_grad, up_grad, qkv_weight_grad, small, out_weight_grad]
    )
    summed = (qkv_sum, out_sum, jnp.stack([up_sum, down_sum]), small_sum[:, :entries].reshape(-1))
    firsts = (first_qkv[0], first_out[0], first_ffn[0], first_vec[0])
    seconds = (second_qkv[0], second_out[0], second_ffn[0], second_vec[0])
    outers = (outer_qkv, outer_out, outer_ffn, outer_vec)
    stepped = [
        adam_step(
            masters[member], summed[member], firsts[member], seconds[member], step_rates[member]
        )
        for member in range(4)
    ]
    changes = [masters[member] - stepped[member][0] for member in range(4)]
    lowered_changes = [change.astype(jnp.bfloat16) for change in changes]
    other_changes = [partner(change, "grp", 0) for change in lowered_changes]
    deltas = [
        (lowered_changes[member].astype(jnp.float32) + other_changes[member].astype(jnp.float32)) / 2
        for member in range(4)
    ]
    momenta = [outer_beta * outers[member] + deltas[member] for member in range(4)]
    renewed = [
        masters[member] - outer_rate * (deltas[member] + outer_beta * momenta[member])
        for member in range(4)
    ]
    return (
        result.astype(jnp.bfloat16)[None],
        input_grad[None],
        summed[0][None],
        summed[1][None],
        summed[2][None],
        summed[3][None],
        stepped[0][1][None],
        stepped[1][1][None],
        stepped[2][1][None],
        stepped[3][1][None],
        stepped[0][2][None],
        stepped[1][2][None],
        stepped[2][2][None],
        stepped[3][2][None],
        deltas[0],
        deltas[1],
        deltas[2],
        deltas[3],
        momenta[0],
        momenta[1],
        momenta[2],
        momenta[3],
        renewed[0],
        renewed[1],
        renewed[2],
        renewed[3],
    )


def solution(mesh):
    return jax.shard_map(
        on_device,
        mesh=mesh,
        in_specs=(
            P(("grp", "dp"), "seq", None),
            P(("grp", "dp"), "seq", None),
            P(("grp", "dp"), None),
            P(("dp", "seq"), None),
            P(("dp", "seq"), None),
            P(None, ("dp", "seq"), None),
            P(("dp", "seq")),
            P("grp", ("dp", "seq"), None),
            P("grp", ("dp", "seq"), None),
            P("grp", None, ("dp", "seq"), None),
            P("grp", ("dp", "seq")),
            P("grp", ("dp", "seq"), None),
            P("grp", ("dp", "seq"), None),
            P("grp", None, ("dp", "seq"), None),
            P("grp", ("dp", "seq")),
            P(("dp", "seq"), None),
            P(("dp", "seq"), None),
            P(None, ("dp", "seq"), None),
            P(("dp", "seq")),
        ),
        out_specs=(
            P(("grp", "dp"), "seq", None),
            P(("grp", "dp"), "seq", None),
            P("grp", ("dp", "seq"), None),
            P("grp", ("dp", "seq"), None),
            P("grp", None, ("dp", "seq"), None),
            P("grp", ("dp", "seq")),
            P("grp", ("dp", "seq"), None),
            P("grp", ("dp", "seq"), None),
            P("grp", None, ("dp", "seq"), None),
            P("grp", ("dp", "seq")),
            P("grp", ("dp", "seq"), None),
            P("grp", ("dp", "seq"), None),
            P("grp", None, ("dp", "seq"), None),
            P("grp", ("dp", "seq")),
            P(("dp", "seq"), None),
            P(("dp", "seq"), None),
            P(None, ("dp", "seq"), None),
            P(("dp", "seq")),
            P(("dp", "seq"), None),
            P(("dp", "seq"), None),
            P(None, ("dp", "seq"), None),
            P(("dp", "seq")),
            P(("dp", "seq"), None),
            P(("dp", "seq"), None),
            P(None, ("dp", "seq"), None),
            P(("dp", "seq")),
        ),
        check_vma=False,
    )
```

```python
from functools import partial

import jax
import jax.numpy as jnp
from jax import lax
from jax.experimental import pallas as pl
from jax.experimental.pallas import tpu as pltpu
from jax.sharding import PartitionSpec as P

HD = 64
W = 512


beta_one = 0.9
beta_two = 0.95
adam_eps = 1e-08
weight_decay = 0.1
bias_one = 1.0 - 0.9**10
bias_two = 1.0 - 0.95**10
step_rates = (0.01, 0.1, 0.005, 0.2)
outer_rate = 0.7
outer_beta = 0.9
norm_eps = 1e-05
score_fill = -1e30


def partner(x, axis, stride):
    return lax.ppermute(x, axis, [(i, i ^ 1 << stride) for i in range(lax.axis_size(axis))])


def layer_norm(residue, norm_gain, norm_shift):
    average = jnp.mean(residue, axis=-1, keepdims=True)
    centred = residue - average
    variance = jnp.mean(centred * centred, axis=-1, keepdims=True)
    return centred * lax.rsqrt(variance + norm_eps) * norm_gain + norm_shift


TILE = 256
LENGTHS = (3, 4, 5, 5)


def first_tile(side, j):
    return jnp.where(side == 0, jnp.maximum(j - 2, 0), 3 - j)


def query_tile(side, j):
    return jnp.where(side == 0, j, 5 - j)


def own_tile(side, j):
    return jnp.where(side == 0, j, 3 - j)


def dot_nt(a, b):
    return lax.dot_general(a, b, (((1,), (1,)), ((), ())), preferred_element_type=jnp.float32)


def dot_tn(a, b):
    return lax.dot_general(a, b, (((0,), (0,)), ((), ())), preferred_element_type=jnp.float32)


def dot_nn(a, b):
    return lax.dot_general(a, b, (((1,), (0,)), ((), ())), preferred_element_type=jnp.float32)


def mask_bias(query_start, key_start, query_ids, key_ids):
    rows, cols = query_ids.shape[0], key_ids.shape[1]
    relative = (
        lax.broadcasted_iota(jnp.int32, (rows, cols), 1)
        - lax.broadcasted_iota(jnp.int32, (rows, cols), 0)
        + (key_start - query_start)
    )
    allowed = (relative <= W) & (relative >= -W) & (query_ids == key_ids)
    return jnp.where(allowed, 0.0, score_fill)


def pair_split(x):
    lane = lax.broadcasted_iota(jnp.int32, x.shape, 1)
    zero = jnp.zeros_like(x)
    return jnp.where(lane < HD, x, zero), jnp.where(lane < HD, zero, x)


def pick_lane(x, index):
    lane = lax.broadcasted_iota(jnp.int32, x.shape, 1)
    return jnp.sum(jnp.where(lane == index, x, 0.0), axis=1, keepdims=True)


def attend_kernel(
    shared, ids_col_ref, ids_row_ref, q_ref, k_ref, v_ref, *refs
):
    count = len(shared)
    o_ref, wide_ref, lse_ref = refs[count : count + 3]
    wholes = refs[count + 3 : 2 * count + 3]
    bias_ref = refs[2 * count + 3]
    j, pair = pl.program_id(0), pl.program_id(1)
    side = lax.axis_index("seq")
    now = j * pl.num_programs(1) + pair
    slots = 32
    work = gather_steps(shared, refs[:count], wholes, *refs[2 * count + 4 :])
    spread(work, now, slots)

    def run(length):
        span = length * TILE
        start = pl.multiple_of(first_tile(side, j) * TILE, TILE)

        @pl.when(pair == 0)
        def _():
            bias_ref[:, :span] = mask_bias(
                query_tile(side, j) * TILE,
                start,
                ids_col_ref[:, :1],
                ids_row_ref[:1, pl.ds(start, span)],
            )
            lse_ref[...] = jnp.zeros_like(lse_ref)

        queries = pair_split(q_ref[...] * jnp.bfloat16(HD**-0.5))
        keys = k_ref[pl.ds(start, span), :]
        values = pair_split(v_ref[pl.ds(start, span), :])
        total = None
        lane = lax.broadcasted_iota(jnp.int32, lse_ref.shape, 1)
        for h in range(2):
            scores = dot_nt(queries[h], keys) + bias_ref[:, :span]
            maximum = jnp.max(scores, axis=1, keepdims=True)
            exponent = jnp.exp(scores - maximum)
            denominator = jnp.sum(exponent, axis=1, keepdims=True)
            weights = (exponent * (1.0 / denominator)).astype(jnp.bfloat16)
            part = dot_nn(weights, values[h])
            total = part if total is None else total + part
            logsum = maximum + jnp.log(denominator)
            lse_ref[...] = jnp.where(lane == 2 * pair + h, logsum, lse_ref[...])
        o_ref[...] = total.astype(jnp.bfloat16)
        wide_ref[...] = total

    for length in sorted(set(LENGTHS)):
        hits = [i for i in range(4) if LENGTHS[i] == length]

        @pl.when((j >= hits[0]) & (j <= hits[-1]))
        def _():
            run(length)

    @pl.when(now == slots - 1)
    def _():
        for step in work[-2:]:
            step()


def attend(ids_col, ids_row, qkv, shards):
    rows, width = qkv.shape[0], qkv.shape[1] // 3
    pairs = width // 128
    own = rows - W
    shared = (False,) * len(shards)
    got = pl.pallas_call(
        partial(attend_kernel, shared),
        name="attend",
        grid_spec=pltpu.PrefetchScalarGridSpec(
            num_scalar_prefetch=0,
            grid=(own // TILE, pairs),
            in_specs=[
                pl.BlockSpec((TILE, 128), lambda j, p: (query_tile(lax.axis_index("seq"), j), 0)),
                pl.BlockSpec((8, rows), lambda j, p: (0, 0)),
                pl.BlockSpec((TILE, 128), lambda j, p: (query_tile(lax.axis_index("seq"), j), p)),
                pl.BlockSpec((rows, 128), lambda j, p: (0, pairs + p)),
                pl.BlockSpec((rows, 128), lambda j, p: (0, 2 * pairs + p)),
                *[pl.BlockSpec(s.shape, lambda j, p: (0, 0)) for s in shards],
            ],
            out_specs=[
                pl.BlockSpec((TILE, 128), lambda j, p: (own_tile(lax.axis_index("seq"), j), p)),
                pl.BlockSpec((TILE, 128), lambda j, p: (own_tile(lax.axis_index("seq"), j), p)),
                pl.BlockSpec((TILE, 128), lambda j, p: (own_tile(lax.axis_index("seq"), j), 0)),
                *[pl.BlockSpec(memory_space=pl.ANY) for s in shards],
            ],
            scratch_shapes=[
                pltpu.VMEM((TILE, 5 * TILE), jnp.float32),
                *gather_scratch(shards, shared),
            ],
        ),
        out_shape=[
            jax.ShapeDtypeStruct((own, width), jnp.bfloat16),
            jax.ShapeDtypeStruct((own, width), jnp.float32),
            jax.ShapeDtypeStruct((own, 128), jnp.float32),
            *gather_shapes(shards),
        ],
        compiler_params=pltpu.CompilerParams(
            vmem_limit_bytes=48 << 20, collective_id=2, has_side_effects=True
        ),
        cost_estimate=pl.CostEstimate(
            flops=4 * 17 * TILE * TILE * width * 4, bytes_accessed=30 << 20, transcendentals=0
        ),
    )(ids_col, ids_row, qkv, qkv, qkv, *shards)
    return [*got[:3], *[w.reshape(-1, w.shape[-1]) for w in got[3:]]]


def attend_back_kernel(
    widths, ids_col_ref, ids_row_ref, q_ref, k_ref, v_ref, do_ref, lse_ref, inner_ref, *refs
):
    count = len(widths)
    dq_ref, dk_ref, dv_ref = refs[count : count + 3]
    sums = refs[count + 3 : 2 * count + 3]
    bias_ref, dkt_ref, dvt_ref = refs[2 * count + 3 : 2 * count + 6]
    pair, j = pl.program_id(0), pl.program_id(1)
    side = lax.axis_index("seq")
    own = dk_ref.shape[0]
    now, slots = pair * pl.num_programs(1) + j, 32
    work = scatter_steps(widths, refs[:count], sums, *refs[2 * count + 6 :])
    spread(work, now, slots)

    @pl.when(j == 0)
    def _():
        dkt_ref[...] = jnp.zeros_like(dkt_ref)
        dvt_ref[...] = jnp.zeros_like(dvt_ref)

    def run(length):
        span = length * TILE
        start = pl.multiple_of(first_tile(side, j) * TILE, TILE)

        @pl.when(pair == 0)
        def _():
            bias_ref[j, :, :span] = mask_bias(
                query_tile(side, j) * TILE,
                start,
                ids_col_ref[:, :1],
                ids_row_ref[:1, pl.ds(start, span)],
            )

        scaled = q_ref[...] * jnp.bfloat16(HD**-0.5)
        outgrad = do_ref[...]
        queries = pair_split(scaled)
        outgrads = pair_split(outgrad)
        turned_q = jnp.transpose(scaled.astype(jnp.float32)).astype(jnp.bfloat16)
        turned_do = jnp.transpose(outgrad.astype(jnp.float32)).astype(jnp.bfloat16)
        keys = k_ref[pl.ds(start, span), :]
        values = v_ref[pl.ds(start, span), :]
        key_parts = pair_split(keys)
        total = None
        for h in range(2):
            logsum = pick_lane(lse_ref[...], 2 * pair + h)
            inner = pick_lane(inner_ref[...], 2 * pair + h)
            scores = dot_nt(queries[h], keys) + bias_ref[j, :, :span]
            probs = jnp.exp(scores - logsum)
            prob_grad = dot_nt(outgrads[h], values)
            score_grad = (probs * (prob_grad - inner)).astype(jnp.bfloat16)
            part = dot_nn(score_grad, key_parts[h])
            total = part if total is None else total + part
            head = slice(h * HD, (h + 1) * HD)
            dvt_ref[head, pl.ds(start, span)] += dot_nn(turned_do[head], probs.astype(jnp.bfloat16))
            dkt_ref[head, pl.ds(start, span)] += dot_nn(turned_q[head], score_grad)
        dq_ref[...] = (total * HD**-0.5).astype(jnp.bfloat16)

    for length in sorted(set(LENGTHS)):
        hits = [i for i in range(4) if LENGTHS[i] == length]

        @pl.when((j >= hits[0]) & (j <= hits[-1]))
        def _():
            run(length)

    @pl.when(j == pl.num_programs(1) - 1)
    def _():
        at = pl.multiple_of(side * W, W)
        dk_ref[...] = jnp.transpose(dkt_ref[:, pl.ds(at, own)])
        dv_ref[...] = jnp.transpose(dvt_ref[:, pl.ds(at, own)])

    @pl.when(now == slots - 1)
    def _():
        for step in work[-2:]:
            step()


def attend_back(ids_col, ids_row, qkv, outgrad, lse, inner, partials):
    rows, width = qkv.shape[0], qkv.shape[1] // 3
    pairs = width // 128
    own = rows - W
    operands = scatter_operands(partials)
    widths = [p.shape[1] for p in partials]
    shard_rows = operands[0].shape[3]
    return pl.pallas_call(
        partial(attend_back_kernel, widths),
        name="attend_back",
        grid_spec=pltpu.PrefetchScalarGridSpec(
            num_scalar_prefetch=0,
            grid=(pairs, own // TILE),
            in_specs=[
                pl.BlockSpec((TILE, 128), lambda p, j: (query_tile(lax.axis_index("seq"), j), 0)),
                pl.BlockSpec((8, rows), lambda p, j: (0, 0)),
                pl.BlockSpec((TILE, 128), lambda p, j: (query_tile(lax.axis_index("seq"), j), p)),
                pl.BlockSpec((rows, 128), lambda p, j: (0, pairs + p)),
                pl.BlockSpec((rows, 128), lambda p, j: (0, 2 * pairs + p)),
                pl.BlockSpec((TILE, 128), lambda p, j: (own_tile(lax.axis_index("seq"), j), p)),
                pl.BlockSpec((TILE, 128), lambda p, j: (own_tile(lax.axis_index("seq"), j), 0)),
                pl.BlockSpec((TILE, 128), lambda p, j: (own_tile(lax.axis_index("seq"), j), 0)),
                *[pl.BlockSpec(memory_space=pl.ANY) for _ in widths],
            ],
            out_specs=[
                pl.BlockSpec((TILE, 128), lambda p, j: (own_tile(lax.axis_index("seq"), j), p)),
                pl.BlockSpec((own, 128), lambda p, j: (0, p)),
                pl.BlockSpec((own, 128), lambda p, j: (0, p)),
                *[pl.BlockSpec((shard_rows, w), lambda p, j: (0, 0)) for w in widths],
            ],
            scratch_shapes=[
                pltpu.VMEM((own // TILE, TILE, 5 * TILE), jnp.float32),
                pltpu.VMEM((128, rows), jnp.float32),
                pltpu.VMEM((128, rows), jnp.float32),
                *scatter_scratch(widths, shard_rows),
            ],
        ),
        out_shape=[
            jax.ShapeDtypeStruct((own, width), jnp.bfloat16),
            jax.ShapeDtypeStruct((own, width), jnp.float32),
            jax.ShapeDtypeStruct((own, width), jnp.float32),
            *[jax.ShapeDtypeStruct((shard_rows, w), jnp.float32) for w in widths],
        ],
        compiler_params=pltpu.CompilerParams(
            vmem_limit_bytes=67043328, collective_id=3, has_side_effects=True
        ),
        cost_estimate=pl.CostEstimate(
            flops=10 * 17 * TILE * TILE * width * 4, bytes_accessed=40 << 20, transcendentals=0
        ),
    )(ids_col, ids_row, qkv, qkv, qkv, outgrad, lse, inner, *operands)


def attend_far_kernel(
    side_ref, ids_col_ref, ids_row_ref, q_ref, k_ref, v_ref, do_ref, lse_ref, inner_ref,
    dk_in_ref, dv_in_ref, dk_ref, dv_ref, bias_ref,
):
    pair = pl.program_id(0)
    side = side_ref[0]

    @pl.when(pair == 0)
    def _():
        bias_ref[...] = mask_bias(
            jnp.where(side == 0, 2 * W, 0), W, ids_col_ref[:, :1], ids_row_ref[:1, W : 2 * W]
        )

    scaled = q_ref[...] * jnp.bfloat16(HD**-0.5)
    outgrad = do_ref[...]
    queries = pair_split(scaled)
    outgrads = pair_split(outgrad)
    turned_q = jnp.transpose(scaled.astype(jnp.float32)).astype(jnp.bfloat16)
    turned_do = jnp.transpose(outgrad.astype(jnp.float32)).astype(jnp.bfloat16)
    keys, values = k_ref[...], v_ref[...]
    dk_parts, dv_parts = [], []
    for h in range(2):
        logsum = pick_lane(lse_ref[...], 2 * pair + h)
        inner = pick_lane(inner_ref[...], 2 * pair + h)
        scores = dot_nt(queries[h], keys) + bias_ref[...]
        probs = jnp.exp(scores - logsum)
        prob_grad = dot_nt(outgrads[h], values)
        score_grad = (probs * (prob_grad - inner)).astype(jnp.bfloat16)
        head = slice(h * HD, (h + 1) * HD)
        dv_parts.append(dot_nn(turned_do[head], probs.astype(jnp.bfloat16)))
        dk_parts.append(dot_nn(turned_q[head], score_grad))
    dk_far = jnp.transpose(jnp.concatenate(dk_parts, axis=0))
    dv_far = jnp.transpose(jnp.concatenate(dv_parts, axis=0))
    near = pl.multiple_of(jnp.where(side == 0, W, 0), W)
    rest = pl.multiple_of(jnp.where(side == 0, 0, W), W)
    dk_ref[pl.ds(near, W), :] = (dk_in_ref[pl.ds(near, W), :] + dk_far).astype(jnp.bfloat16)
    dv_ref[pl.ds(near, W), :] = (dv_in_ref[pl.ds(near, W), :] + dv_far).astype(jnp.bfloat16)
    dk_ref[pl.ds(rest, W), :] = dk_in_ref[pl.ds(rest, W), :].astype(jnp.bfloat16)
    dv_ref[pl.ds(rest, W), :] = dv_in_ref[pl.ds(rest, W), :].astype(jnp.bfloat16)


def attend_far(side, ids_col, ids_row, qkv, far_outgrad, far_lse, far_inner, dk, dv):
    rows, width = qkv.shape[0], qkv.shape[1] // 3
    pairs = width // 128
    own = rows - W
    far = lambda p, s: (jnp.where(s[0] == 0, 2, 0), p)
    return pl.pallas_call(
        attend_far_kernel,
        name="attend_far",
        grid_spec=pltpu.PrefetchScalarGridSpec(
            num_scalar_prefetch=1,
            grid=(pairs,),
            in_specs=[
                pl.BlockSpec((W, 128), lambda p, s: (jnp.where(s[0] == 0, 2, 0), 0)),
                pl.BlockSpec((8, rows), lambda p, s: (0, 0)),
                pl.BlockSpec((W, 128), far),
                pl.BlockSpec((W, 128), lambda p, s: (1, pairs + p)),
                pl.BlockSpec((W, 128), lambda p, s: (1, 2 * pairs + p)),
                pl.BlockSpec((W, 128), lambda p, s: (0, p)),
                pl.BlockSpec((W, 128), lambda p, s: (0, 0)),
                pl.BlockSpec((W, 128), lambda p, s: (0, 0)),
                pl.BlockSpec((own, 128), lambda p, s: (0, p)),
                pl.BlockSpec((own, 128), lambda p, s: (0, p)),
            ],
            out_specs=[
                pl.BlockSpec((own, 128), lambda p, s: (0, p)),
                pl.BlockSpec((own, 128), lambda p, s: (0, p)),
            ],
            scratch_shapes=[pltpu.VMEM((W, W), jnp.float32)],
        ),
        out_shape=[jax.ShapeDtypeStruct((own, width), jnp.bfloat16)] * 2,
        compiler_params=pltpu.CompilerParams(vmem_limit_bytes=48 << 20),
        cost_estimate=pl.CostEstimate(
            flops=8 * 4 * TILE * TILE * width * 4, bytes_accessed=20 << 20, transcendentals=0
        ),
    )(side, ids_col, ids_row, qkv, qkv, qkv, far_outgrad, far_lse, far_inner, dk, dv)


AXES = ("z", "x", "y")
GATHER_ORDERS = ((("z", "x", "y"), 3), (("z", "y", "x"), 3), (("x", "y", "z"), 2))
SCATTER_ORDERS = ((("y", "x", "z"), 3), (("x", "y", "z"), 3), (("z", "y", "x"), 2))
PIECE = 512


def axis_parts():
    total = lax.axis_size("dp")
    inner = 2 ** ((total.bit_length() - 1) // 2)
    return {"z": total // inner, "x": inner, "y": lax.axis_size("seq")}


def places():
    inner = axis_parts()["x"]
    row = lax.axis_index("dp")
    return {"z": lax.div(row, inner), "x": lax.rem(row, inner), "y": lax.axis_index("seq")}


def neighbour(axis, step):
    parts, spots = axis_parts(), places()
    size = parts[axis]
    spots[axis] = lax.rem(spots[axis] + step + size, size)
    return (lax.axis_index("grp"), spots["z"] * parts["x"] + spots["x"], spots["y"])


def twin():
    return (1 - lax.axis_index("grp"), lax.axis_index("dp"), lax.axis_index("seq"))


def greet(peers):
    barrier = pltpu.get_barrier_semaphore()
    for peer in peers:
        pl.semaphore_signal(barrier, inc=1, device_id=peer, device_id_type=pl.DeviceIdType.MESH)
    pl.semaphore_wait(barrier, len(peers))


def ring_peers():
    return [neighbour(axis, step) for axis in AXES for step in (1, -1)]


def flows_of(widths, orders):
    flows = []
    for member, width in enumerate(widths):
        pieces = max(1, min(4, width // PIECE))
        for piece in range(pieces):
            tiles, begin = width // pieces // 128, piece * (width // pieces)
            if tiles < len(orders):
                flows.append((member, orders[0][0], begin, tiles * 128, piece))
                continue
            total = sum(share for _, share in orders)
            low, used = 0, 0
            for order, share in orders:
                used += share
                high = -(-used * tiles // total)
                flows.append((member, order, begin + low * 128, (high - low) * 128, piece))
                low = high
    return flows


def delays(flows, gap):
    seen, found = [], []
    for member, _, _, _, piece in flows:
        if (member, piece) not in seen:
            seen.append((member, piece))
        found.append((len(seen) - 1) * gap)
    return found


def gather_steps(shared, shards, wholes, send_sems, recv_sems, own_sems):
    count = len(shared)
    parts, spots = axis_parts(), places()
    core = lax.axis_index("grp")
    spans = [s.shape[1] if shared[m] else s.shape[1] // 2 for m, s in enumerate(shards)]

    def columns(member, begin, width):
        if shared[member]:
            return pl.ds(begin, width)
        return pl.ds(pl.multiple_of(core * spans[member] + begin, 128), width)

    def own(member):
        cut = columns(member, 0, spans[member])
        return pltpu.make_async_copy(
            shards[member].at[:, cut],
            wholes[member].at[spots["z"], spots["x"], spots["y"], :, cut],
            own_sems.at[member],
        )

    flows = flows_of(spans, GATHER_ORDERS)
    chains, first = [], []
    for member, order, begin, width, _ in flows:
        cut = columns(member, begin, width)
        steps, done = [], []
        for axis in order:
            for turn in range(parts[axis] - 1):
                select = []
                for a in AXES:
                    if a == axis:
                        select.append(pl.ds(lax.rem(spots[a] + parts[a] - turn, parts[a]), 1))
                    elif a in done:
                        select.append(pl.ds(0, parts[a]))
                    else:
                        select.append(pl.ds(spots[a], 1))
                steps.append((wholes[member].at[(*select, slice(None), cut)], neighbour(axis, 1)))
            done.append(axis)
        if not shared[member]:
            steps.append((wholes[member].at[:, :, :, :, cut], twin()))
        first.append(sum(len(c) for c in chains))
        chains.append(steps)

    def remote(i, at):
        block, peer = chains[i][at]
        return pltpu.make_async_remote_copy(
            src_ref=block,
            dst_ref=block,
            send_sem=send_sems.at[first[i] + at],
            recv_sem=recv_sems.at[first[i] + at],
            device_id=peer,
            device_id_type=pl.DeviceIdType.MESH,
        )

    late = delays(flows, 1)
    length = max(late[i] + len(chains[i]) for i in range(len(flows)))

    def begin():
        greet(ring_peers() + [twin()])
        for member in range(count):
            own(member).start()
        for member in range(count):
            own(member).wait()

    def tick(time):
        for i, steps in enumerate(chains):
            at = time - late[i]
            if 1 <= at <= len(steps):
                remote(i, at - 1).wait_recv()
            if 0 <= at < len(steps):
                remote(i, at).start()

    def finish():
        for i, steps in enumerate(chains):
            for at in range(len(steps)):
                remote(i, at).wait_send()

    return [begin] + [partial(tick, time) for time in range(length + 1)] + [finish]


def gather_kernel(shared, *refs):
    count = len(shared)
    for step in gather_steps(shared, refs[:count], refs[count : 2 * count], *refs[2 * count :]):
        step()


def gather_scratch(shards, shared):
    parts = axis_parts()
    hops = sum(size - 1 for size in parts.values()) + 1
    spans = [s.shape[1] if shared[m] else s.shape[1] // 2 for m, s in enumerate(shards)]
    copies = hops * len(flows_of(spans, GATHER_ORDERS))
    return [
        pltpu.SemaphoreType.DMA((copies,)),
        pltpu.SemaphoreType.DMA((copies,)),
        pltpu.SemaphoreType.DMA((len(shards),)),
    ]


def gather_shapes(shards):
    parts = axis_parts()
    return [jax.ShapeDtypeStruct((parts["z"], parts["x"], parts["y"], *s.shape), s.dtype) for s in shards]


def gather_all(shards, shared):
    wholes = pl.pallas_call(
        partial(gather_kernel, shared),
        name="gather_all",
        in_specs=[pl.BlockSpec(memory_space=pltpu.VMEM)] * len(shards),
        out_specs=[pl.BlockSpec(memory_space=pl.ANY)] * len(shards),
        out_shape=gather_shapes(shards),
        scratch_shapes=gather_scratch(shards, shared),
        compiler_params=pltpu.CompilerParams(collective_id=0, has_side_effects=True),
    )(*shards)
    return [w.reshape(-1, w.shape[-1]) for w in wholes]


def scatter_plan(widths):
    parts = axis_parts()
    plan = []
    for member, order, begin, width, piece in flows_of(widths, SCATTER_ORDERS):
        left, levels = list(AXES), []
        for axis in order:
            left.remove(axis)
            levels.append((axis, tuple(parts[a] for a in left), [a for a in left]))
        plan.append((member, order, begin, width, piece, levels))
    return plan


def scatter_steps(widths, partials, sums, send_sems, recv_sems, load_sems, *buffers):
    plan = scatter_plan(widths)
    buffers = list(buffers)
    parts, spots = axis_parts(), places()
    chains, copies = [], []
    for member, order, begin, width, _, levels in plan:
        cut = pl.ds(begin, width)
        chain = []
        source, before = partials[member], list(AXES)
        for depth, (axis, extent, left) in enumerate(levels):
            size = parts[axis]
            inbox = [buffers.pop(0) for _ in range(size - 1)]
            terms = []
            for turn in range(size):
                index = lax.rem(spots[axis] + 2 * size - 1 - turn, size)
                select = tuple(index if a == axis else slice(None) for a in before)
                if depth:
                    terms.append(source.at[select])
                else:
                    terms.append(source.at[(*select, slice(None), cut)])
            ready = []
            if depth == 0:
                for turn in range(1, size):
                    local = buffers.pop(0)
                    copies.append((terms[turn], local))
                    ready.append(len(copies) - 1)
                    terms[turn] = local
            chain.append((axis, extent, inbox, terms, ready))
            source, before = inbox[-1], left
        chains.append(chain)

    def accumulate(target, term, extent):
        total = 1
        for size in extent:
            total *= size

        def body(index, carry):
            where, left = [], index
            for size in reversed(extent):
                where.insert(0, lax.rem(left, size))
                left = lax.div(left, size)
            where = tuple(where)
            target[where] = (
                target[where].astype(jnp.float32) + term[where].astype(jnp.float32)
            ).astype(jnp.bfloat16)
            return carry

        lax.fori_loop(0, total, body, 0)

    flat, first = [], []
    for chain in chains:
        steps = []
        for depth, (axis, extent, inbox, terms, ready) in enumerate(chain):
            for turn in range(parts[axis] - 1):
                steps.append((depth, axis, turn))
        first.append(sum(len(f) for f in flat))
        flat.append(steps)
    late = delays([p[:5] for p in plan], 1)
    length = max(late[i] + len(flat[i]) for i in range(len(plan)))

    def load(index):
        return pltpu.make_async_copy(*copies[index], load_sems.at[index])

    def remote(i, at):
        depth, axis, turn = flat[i][at]
        _, extent, inbox, terms, ready = chains[i][depth]
        return pltpu.make_async_remote_copy(
            src_ref=inbox[turn - 1] if turn else terms[0],
            dst_ref=inbox[turn],
            send_sem=send_sems.at[first[i] + at],
            recv_sem=recv_sems.at[first[i] + at],
            device_id=neighbour(axis, 1),
            device_id_type=pl.DeviceIdType.MESH,
        )

    def begin():
        greet(ring_peers())
        for index in range(len(copies)):
            load(index).start()

    def tick(time):
        for i, steps in enumerate(flat):
            at = time - late[i]
            if 1 <= at <= len(steps):
                remote(i, at - 1).wait_recv()
                depth, axis, turn = steps[at - 1]
                _, extent, inbox, terms, ready = chains[i][depth]
                if ready:
                    load(ready[turn]).wait()
                if at < len(steps):
                    accumulate(inbox[turn], terms[turn + 1], extent)
                else:
                    member, _, begin, width = plan[i][:4]
                    sums[member][:, begin : begin + width] = inbox[turn][...].astype(
                        jnp.float32
                    ) + terms[turn + 1][...].astype(jnp.float32)
            if 0 <= at < len(steps):
                remote(i, at).start()

    def finish():
        for i, steps in enumerate(flat):
            for at in range(len(steps)):
                remote(i, at).wait_send()

    return [begin] + [partial(tick, time) for time in range(length + 1)] + [finish]


def scatter_kernel(widths, *refs):
    count = len(widths)
    for step in scatter_steps(widths, refs[:count], refs[count : 2 * count], *refs[2 * count :]):
        step()


def scatter_scratch(widths, rows):
    parts = axis_parts()
    buffers, copies, loads = [], 0, 0
    for _, order, _, width, _, levels in scatter_plan(widths):
        for depth, (axis, extent, _) in enumerate(levels):
            slots = parts[axis] - 1
            copies += slots
            if depth == 0:
                loads += slots
                slots *= 2
            buffers += [pltpu.VMEM((*extent, rows, width), jnp.bfloat16)] * slots
    return [
        pltpu.SemaphoreType.DMA((copies,)),
        pltpu.SemaphoreType.DMA((copies,)),
        pltpu.SemaphoreType.DMA((loads,)),
        *buffers,
    ]


def scatter_operands(partials):
    parts = axis_parts()
    return [p.reshape(parts["z"], parts["x"], parts["y"], -1, p.shape[1]) for p in partials]


def spread(work, now, slots):
    for order, step in enumerate(work[:-2]):
        slot = 0 if order < 2 else min(slots - 1, (order - 1) * (slots - 1) // (len(work) - 2))
        pl.when(now == slot)(step)


def scatter_all(partials):
    operands = scatter_operands(partials)
    widths = [p.shape[1] for p in partials]
    rows = operands[0].shape[3]
    return pl.pallas_call(
        partial(scatter_kernel, widths),
        name="scatter_all",
        in_specs=[pl.BlockSpec(memory_space=pl.ANY)] * len(partials),
        out_specs=[pl.BlockSpec(memory_space=pltpu.VMEM)] * len(partials),
        out_shape=[jax.ShapeDtypeStruct((rows, width), jnp.float32) for width in widths],
        scratch_shapes=scatter_scratch(widths, rows),
        compiler_params=pltpu.CompilerParams(
            collective_id=1, has_side_effects=True, vmem_limit_bytes=67043328
        ),
    )(*operands)


def ffn_up_kernel(shared, x_ref, w_ref, bias_ref, *refs):
    count = len(shared)
    active_ref, slope_ref = refs[count : count + 2]
    wholes = refs[count + 2 : 2 * count + 2]
    work = gather_steps(shared, refs[:count], wholes, *refs[2 * count + 2 :])
    now, slots = pl.program_id(0), 16
    spread(work, now, slots)
    rows = 256
    for begin in range(0, x_ref.shape[0], rows):
        block = slice(begin, begin + rows)
        u = dot_nn(x_ref[block, :], w_ref[...]) + bias_ref[:1, :]
        share = 0.5 + 0.5 * lax.erf(u * 0.5**0.5)
        density = (0.5 / jnp.pi) ** 0.5 * jnp.exp(-0.5 * u * u)
        active_ref[block, :] = (u * share).astype(jnp.bfloat16)
        slope_ref[block, :] = (share + u * density).astype(jnp.bfloat16)

    @pl.when(now == slots - 1)
    def _():
        for step in work[-2:]:
            step()


def ffn_up(x, weight, bias, shards):
    rows, depth = x.shape
    width = weight.shape[1]
    tile = width // 16
    shared = (False,) * len(shards)
    got = pl.pallas_call(
        partial(ffn_up_kernel, shared),
        name="ffn_up",
        grid=(16,),
        in_specs=[
            pl.BlockSpec((rows, depth), lambda i: (0, 0)),
            pl.BlockSpec((depth, tile), lambda i: (0, i)),
            pl.BlockSpec((8, tile), lambda i: (0, i)),
            *[pl.BlockSpec(s.shape, lambda i: (0, 0)) for s in shards],
        ],
        out_specs=[
            pl.BlockSpec((rows, tile), lambda i: (0, i)),
            pl.BlockSpec((rows, tile), lambda i: (0, i)),
            *[pl.BlockSpec(memory_space=pl.ANY) for s in shards],
        ],
        out_shape=[
            jax.ShapeDtypeStruct((rows, width), jnp.bfloat16),
            jax.ShapeDtypeStruct((rows, width), jnp.bfloat16),
            *gather_shapes(shards),
        ],
        scratch_shapes=gather_scratch(shards, shared),
        compiler_params=pltpu.CompilerParams(
            vmem_limit_bytes=48 << 20, collective_id=4, has_side_effects=True
        ),
        cost_estimate=pl.CostEstimate(
            flops=2 * rows * depth * width, bytes_accessed=40 << 20, transcendentals=0
        ),
    )(x, weight, jnp.broadcast_to(bias[None, :], (8, width)), *shards)
    return [*got[:2], *[w.reshape(-1, w.shape[-1]) for w in got[2:]]]


def adam_step(master, gradient, first, second, step_rate):
    first_new = beta_one * first + (1.0 - beta_one) * gradient
    second_new = beta_two * second + (1.0 - beta_two) * gradient * gradient
    direction = first_new / bias_one / (jnp.sqrt(second_new / bias_two) + adam_eps)
    return (master - step_rate * (direction + weight_decay * master), first_new, second_new)


def on_device(
    tokens,
    cotangent,
    segments,
    weight_qkv,
    weight_out,
    weight_ffn,
    vectors,
    first_qkv,
    first_out,
    first_ffn,
    first_vec,
    second_qkv,
    second_out,
    second_ffn,
    second_vec,
    outer_qkv,
    outer_out,
    outer_ffn,
    outer_vec,
):
    masters = (weight_qkv, weight_out, weight_ffn, vectors)
    lowered = [master.astype(jnp.bfloat16) for master in masters]
    width = weight_out.shape[1]
    entries = vectors.shape[0] // weight_out.shape[0]
    vector_block = jnp.pad(lowered[3].reshape(-1, entries), ((0, 0), (0, 128 - entries)))
    full_qkv, vector_rows = gather_all([lowered[0], vector_block], (False, True))
    full_vec = vector_rows[:, :entries].reshape(-1)
    vector_values = full_vec.astype(jnp.float32)
    pieces = [vector_values[position * width : (position + 1) * width] for position in range(8)]
    (
        bias_query,
        bias_value,
        bias_output,
        bias_second,
        gain_first,
        shift_first,
        gain_second,
        shift_second,
    ) = pieces
    bias_hidden = vector_values[8 * width :]
    token_rows = tokens[0]
    local_rows = token_rows.shape[0]
    side = lax.axis_index("seq")
    is_first = side == 0
    side_operand = jnp.reshape(side, (1,)).astype(jnp.int32)
    far_tokens = partner(jnp.where(is_first, token_rows[local_rows - W :], token_rows[:W]), "seq", 0)
    wide_tokens = jnp.where(
        is_first,
        jnp.concatenate([token_rows, far_tokens], axis=0),
        jnp.concatenate([far_tokens, token_rows], axis=0),
    )
    joined_bias = jnp.concatenate([bias_query, jnp.zeros_like(bias_query), bias_value])
    projected = (
        jnp.dot(wide_tokens, full_qkv, preferred_element_type=jnp.float32) + joined_bias
    ).astype(jnp.bfloat16)
    wide_ids = lax.dynamic_slice_in_dim(segments[0], side * (local_rows - W), local_rows + W, 0)
    ids_col = jnp.broadcast_to(wide_ids[:, None], (local_rows + W, 128))
    ids_row = jnp.broadcast_to(wide_ids[None, :], (8, local_rows + W))
    attended, attended_wide, logsum, full_out, full_up = attend(
        ids_col, ids_row, projected, [lowered[1], lowered[2][0]]
    )
    branch = jnp.dot(attended, full_out, preferred_element_type=jnp.float32) + bias_output
    residue_first = token_rows.astype(jnp.float32) + branch
    hidden_in, first_pullback = jax.vjp(layer_norm, residue_first, gain_first, shift_first)
    hidden_low = hidden_in.astype(jnp.bfloat16)
    activated_low, slope, full_down = ffn_up(hidden_low, full_up, bias_hidden, [lowered[2][1]])
    full_ffn = (full_up, full_down)
    second_branch = (
        lax.dot_general(
            activated_low, full_ffn[1], (((1,), (1,)), ((), ())), preferred_element_type=jnp.float32
        )
        + bias_second
    )
    residue_second = hidden_in + second_branch
    result, second_pullback = jax.vjp(layer_norm, residue_second, gain_second, shift_second)
    upstream = cotangent[0].astype(jnp.float32)
    residue_second_grad, gain_second_grad, shift_second_grad = second_pullback(upstream)
    branch_two_low = residue_second_grad.astype(jnp.bfloat16)
    bias_second_grad = jnp.sum(branch_two_low.astype(jnp.float32), axis=0)
    down_grad = dot_tn(branch_two_low, activated_low).astype(jnp.bfloat16)
    activated_grad = jnp.dot(branch_two_low, full_ffn[1], preferred_element_type=jnp.float32)
    inner_low = (activated_grad * slope.astype(jnp.float32)).astype(jnp.bfloat16)
    bias_hidden_grad = jnp.sum(inner_low.astype(jnp.float32), axis=0)
    up_grad = dot_tn(hidden_low, inner_low).astype(jnp.bfloat16)
    hidden_grad = residue_second_grad + lax.dot_general(
        inner_low, full_ffn[0], (((1,), (1,)), ((), ())), preferred_element_type=jnp.float32
    )
    residue_first_grad, gain_first_grad, shift_first_grad = first_pullback(hidden_grad)
    branch_low = residue_first_grad.astype(jnp.bfloat16)
    bias_output_grad = jnp.sum(branch_low.astype(jnp.float32), axis=0)
    out_weight_grad = dot_tn(attended, branch_low).astype(jnp.bfloat16)
    mixed_grad = lax.dot_general(
        branch_low, full_out, (((1,), (1,)), ((), ())), preferred_element_type=jnp.float32
    ).astype(jnp.bfloat16)

    heads = width // HD
    head_of = jnp.arange(width, dtype=jnp.int32)[:, None] // HD
    collect = (head_of == jnp.arange(128, dtype=jnp.int32)[None, :]).astype(jnp.float32)
    inner_sums = jnp.dot(
        attended_wide * mixed_grad.astype(jnp.float32), collect, precision=lax.Precision.HIGHEST
    )

    def near_rows(x):
        return jnp.where(is_first, x[local_rows - W :], x[:W])

    far_stats = partner(
        jnp.concatenate([near_rows(logsum)[:, :heads], near_rows(inner_sums)[:, :heads]], axis=1),
        "seq",
        0,
    )
    far_outgrad = partner(near_rows(mixed_grad), "seq", 0)
    lane_pad = ((0, 0), (0, 128 - heads))
    far_logsum = jnp.pad(far_stats[:, :heads], lane_pad)
    far_inner = jnp.pad(far_stats[:, heads:], lane_pad)
    query_grad, key_near, value_near, down_sum, up_sum = attend_back(
        ids_col, ids_row, projected, mixed_grad, logsum, inner_sums, [down_grad, up_grad]
    )
    key_grad, value_grad = attend_far(
        side_operand, ids_col, ids_row, projected, far_outgrad, far_logsum, far_inner, key_near, value_near
    )
    projected_grad = jnp.concatenate([query_grad, key_grad, value_grad], axis=1)
    qkv_weight_grad = dot_tn(token_rows, projected_grad).astype(jnp.bfloat16)
    projected_sums = jnp.sum(projected_grad.astype(jnp.float32), axis=0)
    input_grad = residue_first_grad + lax.dot_general(
        projected_grad, full_qkv, (((1,), (1,)), ((), ())), preferred_element_type=jnp.float32
    )
    vector_grad = jnp.concatenate(
        [
            projected_sums[:width],
            projected_sums[2 * width :],
            bias_output_grad,
            bias_second_grad,
            gain_first_grad,
            shift_first_grad,
            gain_second_grad,
            shift_second_grad,
            bias_hidden_grad,
        ]
    )
    small = jnp.pad(vector_grad.reshape(width, -1), ((0, 0), (0, 128 - entries))).astype(jnp.bfloat16)
    qkv_sum, small_sum, out_sum = scatter_all([qkv_weight_grad, small, out_weight_grad])
    summed = (qkv_sum, out_sum, jnp.stack([up_sum, down_sum]), small_sum[:, :entries].reshape(-1))
    firsts = (first_qkv[0], first_out[0], first_ffn[0], first_vec[0])
    seconds = (second_qkv[0], second_out[0], second_ffn[0], second_vec[0])
    outers = (outer_qkv, outer_out, outer_ffn, outer_vec)
    stepped = [
        adam_step(
            masters[member], summed[member], firsts[member], seconds[member], step_rates[member]
        )
        for member in range(4)
    ]
    changes = [masters[member] - stepped[member][0] for member in range(4)]
    lowered_changes = [change.astype(jnp.bfloat16) for change in changes]
    other_changes = [partner(change, "grp", 0) for change in lowered_changes]
    deltas = [
        (lowered_changes[member].astype(jnp.float32) + other_changes[member].astype(jnp.float32)) / 2
        for member in range(4)
    ]
    momenta = [outer_beta * outers[member] + deltas[member] for member in range(4)]
    renewed = [
        masters[member] - outer_rate * (deltas[member] + outer_beta * momenta[member])
        for member in range(4)
    ]
    return (
        result.astype(jnp.bfloat16)[None],
        input_grad[None],
        summed[0][None],
        summed[1][None],
        summed[2][None],
        summed[3][None],
        stepped[0][1][None],
        stepped[1][1][None],
        stepped[2][1][None],
        stepped[3][1][None],
        stepped[0][2][None],
        stepped[1][2][None],
        stepped[2][2][None],
        stepped[3][2][None],
        deltas[0],
        deltas[1],
        deltas[2],
        deltas[3],
        momenta[0],
        momenta[1],
        momenta[2],
        momenta[3],
        renewed[0],
        renewed[1],
        renewed[2],
        renewed[3],
    )


def solution(mesh):
    return jax.shard_map(
        on_device,
        mesh=mesh,
        in_specs=(
            P(("grp", "dp"), "seq", None),
            P(("grp", "dp"), "seq", None),
            P(("grp", "dp"), None),
            P(("dp", "seq"), None),
            P(("dp", "seq"), None),
            P(None, ("dp", "seq"), None),
            P(("dp", "seq")),
            P("grp", ("dp", "seq"), None),
            P("grp", ("dp", "seq"), None),
            P("grp", None, ("dp", "seq"), None),
            P("grp", ("dp", "seq")),
            P("grp", ("dp", "seq"), None),
            P("grp", ("dp", "seq"), None),
            P("grp", None, ("dp", "seq"), None),
            P("grp", ("dp", "seq")),
            P(("dp", "seq"), None),
            P(("dp", "seq"), None),
            P(None, ("dp", "seq"), None),
            P(("dp", "seq")),
        ),
        out_specs=(
            P(("grp", "dp"), "seq", None),
            P(("grp", "dp"), "seq", None),
            P("grp", ("dp", "seq"), None),
            P("grp", ("dp", "seq"), None),
            P("grp", None, ("dp", "seq"), None),
            P("grp", ("dp", "seq")),
            P("grp", ("dp", "seq"), None),
            P("grp", ("dp", "seq"), None),
            P("grp", None, ("dp", "seq"), None),
            P("grp", ("dp", "seq")),
            P("grp", ("dp", "seq"), None),
            P("grp", ("dp", "seq"), None),
            P("grp", None, ("dp", "seq"), None),
            P("grp", ("dp", "seq")),
            P(("dp", "seq"), None),
            P(("dp", "seq"), None),
            P(None, ("dp", "seq"), None),
            P(("dp", "seq")),
            P(("dp", "seq"), None),
            P(("dp", "seq"), None),
            P(None, ("dp", "seq"), None),
            P(("dp", "seq")),
            P(("dp", "seq"), None),
            P(("dp", "seq"), None),
            P(None, ("dp", "seq"), None),
            P(("dp", "seq")),
        ),
        check_vma=False,
    )
```

```python
from functools import partial

import jax
import jax.numpy as jnp
from jax import lax
from jax.experimental import pallas as pl
from jax.experimental.pallas import tpu as pltpu
from jax.sharding import PartitionSpec as P

HD = 64
W = 512


beta_one = 0.9
beta_two = 0.95
adam_eps = 1e-08
weight_decay = 0.1
bias_one = 1.0 - 0.9**10
bias_two = 1.0 - 0.95**10
step_rates = (0.01, 0.1, 0.005, 0.2)
outer_rate = 0.7
outer_beta = 0.9
norm_eps = 1e-05
score_fill = -1e30


def partner(x, axis, stride):
    return lax.ppermute(x, axis, [(i, i ^ 1 << stride) for i in range(lax.axis_size(axis))])


def layer_norm(residue, norm_gain, norm_shift):
    average = jnp.mean(residue, axis=-1, keepdims=True)
    centred = residue - average
    variance = jnp.mean(centred * centred, axis=-1, keepdims=True)
    return centred * lax.rsqrt(variance + norm_eps) * norm_gain + norm_shift


TILE = 256
LENGTHS = (3, 4, 5, 5)


def first_tile(side, j):
    return jnp.where(side == 0, jnp.maximum(j - 2, 0), 3 - j)


def query_tile(side, j):
    return jnp.where(side == 0, j, 5 - j)


def own_tile(side, j):
    return jnp.where(side == 0, j, 3 - j)


def dot_nt(a, b):
    return lax.dot_general(a, b, (((1,), (1,)), ((), ())), preferred_element_type=jnp.float32)


def dot_tn(a, b):
    return lax.dot_general(a, b, (((0,), (0,)), ((), ())), preferred_element_type=jnp.float32)


def dot_nn(a, b):
    return lax.dot_general(a, b, (((1,), (0,)), ((), ())), preferred_element_type=jnp.float32)


def mask_bias(query_start, key_start, query_ids, key_ids):
    rows, cols = query_ids.shape[0], key_ids.shape[1]
    relative = (
        lax.broadcasted_iota(jnp.int32, (rows, cols), 1)
        - lax.broadcasted_iota(jnp.int32, (rows, cols), 0)
        + (key_start - query_start)
    )
    allowed = (relative <= W) & (relative >= -W) & (query_ids == key_ids)
    return jnp.where(allowed, 0.0, score_fill)


def pair_split(x):
    lane = lax.broadcasted_iota(jnp.int32, x.shape, 1)
    zero = jnp.zeros_like(x)
    return jnp.where(lane < HD, x, zero), jnp.where(lane < HD, zero, x)


def pick_lane(x, index):
    lane = lax.broadcasted_iota(jnp.int32, x.shape, 1)
    return jnp.sum(jnp.where(lane == index, x, 0.0), axis=1, keepdims=True)


def attend_kernel(
    shared, ids_col_ref, ids_row_ref, q_ref, k_ref, v_ref, *refs
):
    count = len(shared)
    o_ref, wide_ref, lse_ref = refs[count : count + 3]
    wholes = refs[count + 3 : 2 * count + 3]
    bias_ref = refs[2 * count + 3]
    j, pair = pl.program_id(0), pl.program_id(1)
    side = lax.axis_index("seq")
    now = j * pl.num_programs(1) + pair
    slots = 32
    work = gather_steps(shared, refs[:count], wholes, *refs[2 * count + 4 :])
    spread(work, now, slots, 0)

    def run(length):
        span = length * TILE
        start = pl.multiple_of(first_tile(side, j) * TILE, TILE)

        @pl.when(pair == 0)
        def _():
            bias_ref[:, :span] = mask_bias(
                query_tile(side, j) * TILE,
                start,
                ids_col_ref[:, :1],
                ids_row_ref[:1, pl.ds(start, span)],
            )
            lse_ref[...] = jnp.zeros_like(lse_ref)

        queries = pair_split(q_ref[...] * jnp.bfloat16(HD**-0.5))
        keys = k_ref[pl.ds(start, span), :]
        values = pair_split(v_ref[pl.ds(start, span), :])
        total = None
        lane = lax.broadcasted_iota(jnp.int32, lse_ref.shape, 1)
        for h in range(2):
            scores = dot_nt(queries[h], keys) + bias_ref[:, :span]
            maximum = jnp.max(scores, axis=1, keepdims=True)
            exponent = jnp.exp(scores - maximum)
            denominator = jnp.sum(exponent, axis=1, keepdims=True)
            weights = (exponent * (1.0 / denominator)).astype(jnp.bfloat16)
            part = dot_nn(weights, values[h])
            total = part if total is None else total + part
            logsum = maximum + jnp.log(denominator)
            lse_ref[...] = jnp.where(lane == 2 * pair + h, logsum, lse_ref[...])
        o_ref[...] = total.astype(jnp.bfloat16)
        wide_ref[...] = total

    for length in sorted(set(LENGTHS)):
        hits = [i for i in range(4) if LENGTHS[i] == length]

        @pl.when((j >= hits[0]) & (j <= hits[-1]))
        def _():
            run(length)

    @pl.when(now == slots - 1)
    def _():
        for step in work[-2:]:
            step()


def attend(ids_col, ids_row, qkv, shards):
    rows, width = qkv.shape[0], qkv.shape[1] // 3
    pairs = width // 128
    own = rows - W
    shared = (False,) * len(shards)
    got = pl.pallas_call(
        partial(attend_kernel, shared),
        name="attend",
        grid_spec=pltpu.PrefetchScalarGridSpec(
            num_scalar_prefetch=0,
            grid=(own // TILE, pairs),
            in_specs=[
                pl.BlockSpec((TILE, 128), lambda j, p: (query_tile(lax.axis_index("seq"), j), 0)),
                pl.BlockSpec((8, rows), lambda j, p: (0, 0)),
                pl.BlockSpec((TILE, 128), lambda j, p: (query_tile(lax.axis_index("seq"), j), p)),
                pl.BlockSpec((rows, 128), lambda j, p: (0, pairs + p)),
                pl.BlockSpec((rows, 128), lambda j, p: (0, 2 * pairs + p)),
                *[pl.BlockSpec(s.shape, lambda j, p: (0, 0)) for s in shards],
            ],
            out_specs=[
                pl.BlockSpec((TILE, 128), lambda j, p: (own_tile(lax.axis_index("seq"), j), p)),
                pl.BlockSpec((TILE, 128), lambda j, p: (own_tile(lax.axis_index("seq"), j), p)),
                pl.BlockSpec((TILE, 128), lambda j, p: (own_tile(lax.axis_index("seq"), j), 0)),
                *[pl.BlockSpec(memory_space=pl.ANY) for s in shards],
            ],
            scratch_shapes=[
                pltpu.VMEM((TILE, 5 * TILE), jnp.float32),
                *gather_scratch(shards, shared),
            ],
        ),
        out_shape=[
            jax.ShapeDtypeStruct((own, width), jnp.bfloat16),
            jax.ShapeDtypeStruct((own, width), jnp.float32),
            jax.ShapeDtypeStruct((own, 128), jnp.float32),
            *gather_shapes(shards),
        ],
        compiler_params=pltpu.CompilerParams(
            vmem_limit_bytes=48 << 20, collective_id=2, has_side_effects=True
        ),
        cost_estimate=pl.CostEstimate(
            flops=4 * 17 * TILE * TILE * width * 4, bytes_accessed=30 << 20, transcendentals=0
        ),
    )(ids_col, ids_row, qkv, qkv, qkv, *shards)
    return [*got[:3], *[w.reshape(-1, w.shape[-1]) for w in got[3:]]]


def attend_back_kernel(
    widths, ids_col_ref, ids_row_ref, q_ref, k_ref, v_ref, do_ref, lse_ref, inner_ref, *refs
):
    count = len(widths)
    dq_ref, dk_ref, dv_ref = refs[count : count + 3]
    sums = refs[count + 3 : 2 * count + 3]
    bias_ref, dkt_ref, dvt_ref = refs[2 * count + 3 : 2 * count + 6]
    pair, j = pl.program_id(0), pl.program_id(1)
    side = lax.axis_index("seq")
    own = dk_ref.shape[0]
    now, slots = pair * pl.num_programs(1) + j, 32
    work = scatter_steps(widths, refs[:count], sums, *refs[2 * count + 6 :])
    spread(work, now, slots, chunks(widths))

    @pl.when(j == 0)
    def _():
        dkt_ref[...] = jnp.zeros_like(dkt_ref)
        dvt_ref[...] = jnp.zeros_like(dvt_ref)

    def run(length):
        span = length * TILE
        start = pl.multiple_of(first_tile(side, j) * TILE, TILE)

        @pl.when(pair == 0)
        def _():
            bias_ref[j, :, :span] = mask_bias(
                query_tile(side, j) * TILE,
                start,
                ids_col_ref[:, :1],
                ids_row_ref[:1, pl.ds(start, span)],
            )

        scaled = q_ref[...] * jnp.bfloat16(HD**-0.5)
        outgrad = do_ref[...]
        queries = pair_split(scaled)
        outgrads = pair_split(outgrad)
        turned_q = jnp.transpose(scaled.astype(jnp.float32)).astype(jnp.bfloat16)
        turned_do = jnp.transpose(outgrad.astype(jnp.float32)).astype(jnp.bfloat16)
        keys = k_ref[pl.ds(start, span), :]
        values = v_ref[pl.ds(start, span), :]
        key_parts = pair_split(keys)
        total = None
        for h in range(2):
            logsum = pick_lane(lse_ref[...], 2 * pair + h)
            inner = pick_lane(inner_ref[...], 2 * pair + h)
            scores = dot_nt(queries[h], keys) + bias_ref[j, :, :span]
            probs = jnp.exp(scores - logsum)
            prob_grad = dot_nt(outgrads[h], values)
            score_grad = (probs * (prob_grad - inner)).astype(jnp.bfloat16)
            part = dot_nn(score_grad, key_parts[h])
            total = part if total is None else total + part
            head = slice(h * HD, (h + 1) * HD)
            dvt_ref[head, pl.ds(start, span)] += dot_nn(turned_do[head], probs.astype(jnp.bfloat16))
            dkt_ref[head, pl.ds(start, span)] += dot_nn(turned_q[head], score_grad)
        dq_ref[...] = (total * HD**-0.5).astype(jnp.bfloat16)

    for length in sorted(set(LENGTHS)):
        hits = [i for i in range(4) if LENGTHS[i] == length]

        @pl.when((j >= hits[0]) & (j <= hits[-1]))
        def _():
            run(length)

    @pl.when(j == pl.num_programs(1) - 1)
    def _():
        at = pl.multiple_of(side * W, W)
        dk_ref[...] = jnp.transpose(dkt_ref[:, pl.ds(at, own)])
        dv_ref[...] = jnp.transpose(dvt_ref[:, pl.ds(at, own)])

    @pl.when(now == slots - 1)
    def _():
        for step in work[-2:]:
            step()


def attend_back(ids_col, ids_row, qkv, outgrad, lse, inner, partials):
    rows, width = qkv.shape[0], qkv.shape[1] // 3
    pairs = width // 128
    own = rows - W
    operands = scatter_operands(partials)
    widths = [p.shape[1] for p in partials]
    shard_rows = operands[0].shape[3]
    return pl.pallas_call(
        partial(attend_back_kernel, widths),
        name="attend_back",
        grid_spec=pltpu.PrefetchScalarGridSpec(
            num_scalar_prefetch=0,
            grid=(pairs, own // TILE),
            in_specs=[
                pl.BlockSpec((TILE, 128), lambda p, j: (query_tile(lax.axis_index("seq"), j), 0)),
                pl.BlockSpec((8, rows), lambda p, j: (0, 0)),
                pl.BlockSpec((TILE, 128), lambda p, j: (query_tile(lax.axis_index("seq"), j), p)),
                pl.BlockSpec((rows, 128), lambda p, j: (0, pairs + p)),
                pl.BlockSpec((rows, 128), lambda p, j: (0, 2 * pairs + p)),
                pl.BlockSpec((TILE, 128), lambda p, j: (own_tile(lax.axis_index("seq"), j), p)),
                pl.BlockSpec((TILE, 128), lambda p, j: (own_tile(lax.axis_index("seq"), j), 0)),
                pl.BlockSpec((TILE, 128), lambda p, j: (own_tile(lax.axis_index("seq"), j), 0)),
                *[pl.BlockSpec(memory_space=pl.ANY) for _ in widths],
            ],
            out_specs=[
                pl.BlockSpec((TILE, 128), lambda p, j: (own_tile(lax.axis_index("seq"), j), p)),
                pl.BlockSpec((own, 128), lambda p, j: (0, p)),
                pl.BlockSpec((own, 128), lambda p, j: (0, p)),
                *[pl.BlockSpec((shard_rows, w), lambda p, j: (0, 0)) for w in widths],
            ],
            scratch_shapes=[
                pltpu.VMEM((own // TILE, TILE, 5 * TILE), jnp.float32),
                pltpu.VMEM((128, rows), jnp.float32),
                pltpu.VMEM((128, rows), jnp.float32),
                *scatter_scratch(widths, shard_rows),
            ],
        ),
        out_shape=[
            jax.ShapeDtypeStruct((own, width), jnp.bfloat16),
            jax.ShapeDtypeStruct((own, width), jnp.float32),
            jax.ShapeDtypeStruct((own, width), jnp.float32),
            *[jax.ShapeDtypeStruct((shard_rows, w), jnp.float32) for w in widths],
        ],
        compiler_params=pltpu.CompilerParams(
            vmem_limit_bytes=67043328, collective_id=3, has_side_effects=True
        ),
        cost_estimate=pl.CostEstimate(
            flops=10 * 17 * TILE * TILE * width * 4, bytes_accessed=40 << 20, transcendentals=0
        ),
    )(ids_col, ids_row, qkv, qkv, qkv, outgrad, lse, inner, *operands)


def attend_far_kernel(
    side_ref, ids_col_ref, ids_row_ref, q_ref, k_ref, v_ref, do_ref, lse_ref, inner_ref,
    dk_in_ref, dv_in_ref, dk_ref, dv_ref, bias_ref,
):
    pair = pl.program_id(0)
    side = side_ref[0]

    @pl.when(pair == 0)
    def _():
        bias_ref[...] = mask_bias(
            jnp.where(side == 0, 2 * W, 0), W, ids_col_ref[:, :1], ids_row_ref[:1, W : 2 * W]
        )

    scaled = q_ref[...] * jnp.bfloat16(HD**-0.5)
    outgrad = do_ref[...]
    queries = pair_split(scaled)
    outgrads = pair_split(outgrad)
    turned_q = jnp.transpose(scaled.astype(jnp.float32)).astype(jnp.bfloat16)
    turned_do = jnp.transpose(outgrad.astype(jnp.float32)).astype(jnp.bfloat16)
    keys, values = k_ref[...], v_ref[...]
    dk_parts, dv_parts = [], []
    for h in range(2):
        logsum = pick_lane(lse_ref[...], 2 * pair + h)
        inner = pick_lane(inner_ref[...], 2 * pair + h)
        scores = dot_nt(queries[h], keys) + bias_ref[...]
        probs = jnp.exp(scores - logsum)
        prob_grad = dot_nt(outgrads[h], values)
        score_grad = (probs * (prob_grad - inner)).astype(jnp.bfloat16)
        head = slice(h * HD, (h + 1) * HD)
        dv_parts.append(dot_nn(turned_do[head], probs.astype(jnp.bfloat16)))
        dk_parts.append(dot_nn(turned_q[head], score_grad))
    dk_far = jnp.transpose(jnp.concatenate(dk_parts, axis=0))
    dv_far = jnp.transpose(jnp.concatenate(dv_parts, axis=0))
    near = pl.multiple_of(jnp.where(side == 0, W, 0), W)
    rest = pl.multiple_of(jnp.where(side == 0, 0, W), W)
    dk_ref[pl.ds(near, W), :] = (dk_in_ref[pl.ds(near, W), :] + dk_far).astype(jnp.bfloat16)
    dv_ref[pl.ds(near, W), :] = (dv_in_ref[pl.ds(near, W), :] + dv_far).astype(jnp.bfloat16)
    dk_ref[pl.ds(rest, W), :] = dk_in_ref[pl.ds(rest, W), :].astype(jnp.bfloat16)
    dv_ref[pl.ds(rest, W), :] = dv_in_ref[pl.ds(rest, W), :].astype(jnp.bfloat16)


def attend_far(side, ids_col, ids_row, qkv, far_outgrad, far_lse, far_inner, dk, dv):
    rows, width = qkv.shape[0], qkv.shape[1] // 3
    pairs = width // 128
    own = rows - W
    far = lambda p, s: (jnp.where(s[0] == 0, 2, 0), p)
    return pl.pallas_call(
        attend_far_kernel,
        name="attend_far",
        grid_spec=pltpu.PrefetchScalarGridSpec(
            num_scalar_prefetch=1,
            grid=(pairs,),
            in_specs=[
                pl.BlockSpec((W, 128), lambda p, s: (jnp.where(s[0] == 0, 2, 0), 0)),
                pl.BlockSpec((8, rows), lambda p, s: (0, 0)),
                pl.BlockSpec((W, 128), far),
                pl.BlockSpec((W, 128), lambda p, s: (1, pairs + p)),
                pl.BlockSpec((W, 128), lambda p, s: (1, 2 * pairs + p)),
                pl.BlockSpec((W, 128), lambda p, s: (0, p)),
                pl.BlockSpec((W, 128), lambda p, s: (0, 0)),
                pl.BlockSpec((W, 128), lambda p, s: (0, 0)),
                pl.BlockSpec((own, 128), lambda p, s: (0, p)),
                pl.BlockSpec((own, 128), lambda p, s: (0, p)),
            ],
            out_specs=[
                pl.BlockSpec((own, 128), lambda p, s: (0, p)),
                pl.BlockSpec((own, 128), lambda p, s: (0, p)),
            ],
            scratch_shapes=[pltpu.VMEM((W, W), jnp.float32)],
        ),
        out_shape=[jax.ShapeDtypeStruct((own, width), jnp.bfloat16)] * 2,
        compiler_params=pltpu.CompilerParams(vmem_limit_bytes=48 << 20),
        cost_estimate=pl.CostEstimate(
            flops=8 * 4 * TILE * TILE * width * 4, bytes_accessed=20 << 20, transcendentals=0
        ),
    )(side, ids_col, ids_row, qkv, qkv, qkv, far_outgrad, far_lse, far_inner, dk, dv)


AXES = ("z", "x", "y")
GATHER_ORDERS = ((("z", "x", "y"), 3), (("z", "y", "x"), 3), (("x", "y", "z"), 2))
SCATTER_ORDERS = ((("y", "x", "z"), 3), (("x", "y", "z"), 3), (("z", "y", "x"), 2))
PIECE = 512


def axis_parts():
    total = lax.axis_size("dp")
    inner = 2 ** ((total.bit_length() - 1) // 2)
    return {"z": total // inner, "x": inner, "y": lax.axis_size("seq")}


def places():
    inner = axis_parts()["x"]
    row = lax.axis_index("dp")
    return {"z": lax.div(row, inner), "x": lax.rem(row, inner), "y": lax.axis_index("seq")}


def neighbour(axis, step):
    parts, spots = axis_parts(), places()
    size = parts[axis]
    spots[axis] = lax.rem(spots[axis] + step + size, size)
    return (lax.axis_index("grp"), spots["z"] * parts["x"] + spots["x"], spots["y"])


def twin():
    return (1 - lax.axis_index("grp"), lax.axis_index("dp"), lax.axis_index("seq"))


def greet(peers):
    barrier = pltpu.get_barrier_semaphore()
    for peer in peers:
        pl.semaphore_signal(barrier, inc=1, device_id=peer, device_id_type=pl.DeviceIdType.MESH)
    pl.semaphore_wait(barrier, len(peers))


def ring_peers():
    return [neighbour(axis, step) for axis in AXES for step in (1, -1)]


def flows_of(widths, orders):
    flows = []
    for member, width in enumerate(widths):
        pieces = chunks([width])
        for piece in range(pieces):
            tiles, begin = width // pieces // 128, piece * (width // pieces)
            if tiles < len(orders):
                flows.append((member, orders[0][0], begin, tiles * 128, piece))
                continue
            total = sum(share for _, share in orders)
            low, used = 0, 0
            for order, share in orders:
                used += share
                high = -(-used * tiles // total)
                flows.append((member, order, begin + low * 128, (high - low) * 128, piece))
                low = high
    return flows


def delays(flows, gap):
    seen, found = [], []
    for member, _, _, _, piece in flows:
        if (member, piece) not in seen:
            seen.append((member, piece))
        found.append((len(seen) - 1) * gap)
    return found


def gather_steps(shared, shards, wholes, send_sems, recv_sems, own_sems):
    count = len(shared)
    parts, spots = axis_parts(), places()
    core = lax.axis_index("grp")
    spans = [s.shape[1] if shared[m] else s.shape[1] // 2 for m, s in enumerate(shards)]

    def columns(member, begin, width):
        if shared[member]:
            return pl.ds(begin, width)
        return pl.ds(pl.multiple_of(core * spans[member] + begin, 128), width)

    def own(member):
        cut = columns(member, 0, spans[member])
        return pltpu.make_async_copy(
            shards[member].at[:, cut],
            wholes[member].at[spots["z"], spots["x"], spots["y"], :, cut],
            own_sems.at[member],
        )

    flows = flows_of(spans, GATHER_ORDERS)
    chains, first = [], []
    for member, order, begin, width, _ in flows:
        cut = columns(member, begin, width)
        steps, done = [], []
        for axis in order:
            for turn in range(parts[axis] - 1):
                select = []
                for a in AXES:
                    if a == axis:
                        select.append(pl.ds(lax.rem(spots[a] + parts[a] - turn, parts[a]), 1))
                    elif a in done:
                        select.append(pl.ds(0, parts[a]))
                    else:
                        select.append(pl.ds(spots[a], 1))
                steps.append((wholes[member].at[(*select, slice(None), cut)], neighbour(axis, 1)))
            done.append(axis)
        if not shared[member]:
            steps.append((wholes[member].at[:, :, :, :, cut], twin()))
        first.append(sum(len(c) for c in chains))
        chains.append(steps)

    def remote(i, at):
        block, peer = chains[i][at]
        return pltpu.make_async_remote_copy(
            src_ref=block,
            dst_ref=block,
            send_sem=send_sems.at[first[i] + at],
            recv_sem=recv_sems.at[first[i] + at],
            device_id=peer,
            device_id_type=pl.DeviceIdType.MESH,
        )

    late = delays(flows, 1)
    length = max(late[i] + len(chains[i]) for i in range(len(flows)))

    def begin():
        greet(ring_peers() + [twin()])
        for member in range(count):
            own(member).start()
        for member in range(count):
            own(member).wait()

    def tick(time):
        for i, steps in enumerate(chains):
            at = time - late[i]
            if 1 <= at <= len(steps):
                remote(i, at - 1).wait_recv()
            if 0 <= at < len(steps):
                remote(i, at).start()

    def finish():
        for i, steps in enumerate(chains):
            for at in range(len(steps)):
                remote(i, at).wait_send()

    return [begin] + [partial(tick, time) for time in range(length + 1)] + [finish]


def gather_kernel(shared, *refs):
    count = len(shared)
    for step in gather_steps(shared, refs[:count], refs[count : 2 * count], *refs[2 * count :]):
        step()


def gather_scratch(shards, shared):
    parts = axis_parts()
    hops = sum(size - 1 for size in parts.values()) + 1
    spans = [s.shape[1] if shared[m] else s.shape[1] // 2 for m, s in enumerate(shards)]
    copies = hops * len(flows_of(spans, GATHER_ORDERS))
    return [
        pltpu.SemaphoreType.DMA((copies,)),
        pltpu.SemaphoreType.DMA((copies,)),
        pltpu.SemaphoreType.DMA((len(shards),)),
    ]


def gather_shapes(shards):
    parts = axis_parts()
    return [jax.ShapeDtypeStruct((parts["z"], parts["x"], parts["y"], *s.shape), s.dtype) for s in shards]


def gather_all(shards, shared):
    wholes = pl.pallas_call(
        partial(gather_kernel, shared),
        name="gather_all",
        in_specs=[pl.BlockSpec(memory_space=pltpu.VMEM)] * len(shards),
        out_specs=[pl.BlockSpec(memory_space=pl.ANY)] * len(shards),
        out_shape=gather_shapes(shards),
        scratch_shapes=gather_scratch(shards, shared),
        compiler_params=pltpu.CompilerParams(collective_id=0, has_side_effects=True),
    )(*shards)
    return [w.reshape(-1, w.shape[-1]) for w in wholes]


def scatter_plan(widths):
    parts = axis_parts()
    plan = []
    for member, order, begin, width, piece in flows_of(widths, SCATTER_ORDERS):
        left, levels = list(AXES), []
        for axis in order:
            left.remove(axis)
            levels.append((axis, tuple(parts[a] for a in left), [a for a in left]))
        plan.append((member, order, begin, width, piece, levels))
    return plan


def scatter_steps(widths, partials, sums, send_sems, recv_sems, load_sems, *buffers):
    plan = scatter_plan(widths)
    buffers = list(buffers)
    parts, spots = axis_parts(), places()
    chains, copies = [], []
    for member, order, begin, width, _, levels in plan:
        cut = pl.ds(begin, width)
        chain = []
        source, before = partials[member], list(AXES)
        for depth, (axis, extent, left) in enumerate(levels):
            size = parts[axis]
            inbox = [buffers.pop(0) for _ in range(size - 1)]
            terms = []
            for turn in range(size):
                index = lax.rem(spots[axis] + 2 * size - 1 - turn, size)
                select = tuple(index if a == axis else slice(None) for a in before)
                if depth:
                    terms.append(source.at[select])
                else:
                    terms.append(source.at[(*select, slice(None), cut)])
            ready = []
            if depth == 0:
                for turn in range(1, size):
                    local = buffers.pop(0)
                    copies.append((terms[turn], local))
                    ready.append(len(copies) - 1)
                    terms[turn] = local
            chain.append((axis, extent, inbox, terms, ready))
            source, before = inbox[-1], left
        chains.append(chain)

    def accumulate(target, term, extent):
        total = 1
        for size in extent:
            total *= size

        def body(index, carry):
            where, left = [], index
            for size in reversed(extent):
                where.insert(0, lax.rem(left, size))
                left = lax.div(left, size)
            where = tuple(where)
            target[where] = (
                target[where].astype(jnp.float32) + term[where].astype(jnp.float32)
            ).astype(jnp.bfloat16)
            return carry

        lax.fori_loop(0, total, body, 0)

    flat, first = [], []
    for chain in chains:
        steps = []
        for depth, (axis, extent, inbox, terms, ready) in enumerate(chain):
            for turn in range(parts[axis] - 1):
                steps.append((depth, axis, turn))
        first.append(sum(len(f) for f in flat))
        flat.append(steps)
    late = delays([p[:5] for p in plan], 1)
    length = max(late[i] + len(flat[i]) for i in range(len(plan)))

    def load(index):
        return pltpu.make_async_copy(*copies[index], load_sems.at[index])

    def remote(i, at):
        depth, axis, turn = flat[i][at]
        _, extent, inbox, terms, ready = chains[i][depth]
        return pltpu.make_async_remote_copy(
            src_ref=inbox[turn - 1] if turn else terms[0],
            dst_ref=inbox[turn],
            send_sem=send_sems.at[first[i] + at],
            recv_sem=recv_sems.at[first[i] + at],
            device_id=neighbour(axis, 1),
            device_id_type=pl.DeviceIdType.MESH,
        )

    def begin():
        greet(ring_peers())
        for index in range(len(copies)):
            load(index).start()

    def tick(time):
        for i, steps in enumerate(flat):
            at = time - late[i]
            if 1 <= at <= len(steps):
                remote(i, at - 1).wait_recv()
                depth, axis, turn = steps[at - 1]
                _, extent, inbox, terms, ready = chains[i][depth]
                if ready:
                    load(ready[turn]).wait()
                if at < len(steps):
                    accumulate(inbox[turn], terms[turn + 1], extent)
                else:
                    member, _, begin, width = plan[i][:4]
                    sums[member][:, begin : begin + width] = inbox[turn][...].astype(
                        jnp.float32
                    ) + terms[turn + 1][...].astype(jnp.float32)
            if 0 <= at < len(steps):
                remote(i, at).start()

    def finish():
        for i, steps in enumerate(flat):
            for at in range(len(steps)):
                remote(i, at).wait_send()

    return [begin] + [partial(tick, time) for time in range(length + 1)] + [finish]


def scatter_scratch(widths, rows):
    parts = axis_parts()
    buffers, copies, loads = [], 0, 0
    for _, order, _, width, _, levels in scatter_plan(widths):
        for depth, (axis, extent, _) in enumerate(levels):
            slots = parts[axis] - 1
            copies += slots
            if depth == 0:
                loads += slots
                slots *= 2
            buffers += [pltpu.VMEM((*extent, rows, width), jnp.bfloat16)] * slots
    return [
        pltpu.SemaphoreType.DMA((copies,)),
        pltpu.SemaphoreType.DMA((copies,)),
        pltpu.SemaphoreType.DMA((loads,)),
        *buffers,
    ]


def scatter_operands(partials):
    parts = axis_parts()
    return [p.reshape(parts["z"], parts["x"], parts["y"], -1, p.shape[1]) for p in partials]


def spread(work, now, slots, busy):
    ticks = len(work) - 3
    for order, step in enumerate(work[:-2]):
        time = max(0, order - 1)
        if busy:
            slot = min(slots - 1, time * slots // busy)
        elif time < 4:
            slot = time
        else:
            slot = 3 + (time - 3) * (slots - 4) // (ticks - 3)
        pl.when(now == slot)(step)


def chunks(widths):
    return sum(max(1, min(4, width // PIECE)) for width in widths)


def ffn_up_kernel(shared, x_ref, w_ref, bias_ref, *refs):
    count = len(shared)
    active_ref, slope_ref = refs[count : count + 2]
    wholes = refs[count + 2 : 2 * count + 2]
    work = gather_steps(shared, refs[:count], wholes, *refs[2 * count + 2 :])
    now, slots = pl.program_id(0), 16
    spread(work, now, slots, 0)
    rows = 256
    for begin in range(0, x_ref.shape[0], rows):
        block = slice(begin, begin + rows)
        u = dot_nn(x_ref[block, :], w_ref[...]) + bias_ref[:1, :]
        share = 0.5 + 0.5 * lax.erf(u * 0.5**0.5)
        density = (0.5 / jnp.pi) ** 0.5 * jnp.exp(-0.5 * u * u)
        active_ref[block, :] = (u * share).astype(jnp.bfloat16)
        slope_ref[block, :] = (share + u * density).astype(jnp.bfloat16)

    @pl.when(now == slots - 1)
    def _():
        for step in work[-2:]:
            step()


def ffn_up(x, weight, bias, shards):
    rows, depth = x.shape
    width = weight.shape[1]
    tile = width // 16
    shared = (False,) * len(shards)
    got = pl.pallas_call(
        partial(ffn_up_kernel, shared),
        name="ffn_up",
        grid=(16,),
        in_specs=[
            pl.BlockSpec((rows, depth), lambda i: (0, 0)),
            pl.BlockSpec((depth, tile), lambda i: (0, i)),
            pl.BlockSpec((8, tile), lambda i: (0, i)),
            *[pl.BlockSpec(s.shape, lambda i: (0, 0)) for s in shards],
        ],
        out_specs=[
            pl.BlockSpec((rows, tile), lambda i: (0, i)),
            pl.BlockSpec((rows, tile), lambda i: (0, i)),
            *[pl.BlockSpec(memory_space=pl.ANY) for s in shards],
        ],
        out_shape=[
            jax.ShapeDtypeStruct((rows, width), jnp.bfloat16),
            jax.ShapeDtypeStruct((rows, width), jnp.bfloat16),
            *gather_shapes(shards),
        ],
        scratch_shapes=gather_scratch(shards, shared),
        compiler_params=pltpu.CompilerParams(
            vmem_limit_bytes=48 << 20, collective_id=4, has_side_effects=True
        ),
        cost_estimate=pl.CostEstimate(
            flops=2 * rows * depth * width, bytes_accessed=40 << 20, transcendentals=0
        ),
    )(x, weight, jnp.broadcast_to(bias[None, :], (8, width)), *shards)
    return [*got[:2], *[w.reshape(-1, w.shape[-1]) for w in got[2:]]]


def ffn_back_kernel(widths, dz_ref, down_ref, slope_ref, turned_ref, up_ref, *refs):
    count = len(widths)
    up_grad_ref, bias_ref, total_ref = refs[count : count + 3]
    sums = refs[count + 3 : 2 * count + 3]
    work = scatter_steps(widths, refs[:count], sums, *refs[2 * count + 3 :])
    now, slots = pl.program_id(0), 16
    spread(work, now, slots, chunks(widths))

    @pl.when(now == 0)
    def _():
        total_ref[...] = jnp.zeros_like(total_ref)

    inner = (dot_nn(dz_ref[...], down_ref[...]) * slope_ref[...].astype(jnp.float32)).astype(jnp.bfloat16)
    column = jnp.sum(inner.astype(jnp.float32), axis=0, keepdims=True)
    bias_ref[...] = jnp.broadcast_to(column, bias_ref.shape)
    up_grad_ref[...] = dot_nn(turned_ref[...], inner).astype(jnp.bfloat16)
    total_ref[...] += dot_nt(inner, up_ref[...])

    @pl.when(now == slots - 1)
    def _():
        for step in work[-2:]:
            step()


def ffn_back(dz, weight_down, slope, turned, weight_up, partials):
    rows, depth = dz.shape
    width = weight_up.shape[1]
    tile = width // 16
    operands = scatter_operands(partials)
    widths = [p.shape[1] for p in partials]
    shard_rows = operands[0].shape[3]
    whole = pl.BlockSpec((rows, depth), lambda i: (0, 0))
    return pl.pallas_call(
        partial(ffn_back_kernel, widths),
        name="ffn_back",
        grid=(16,),
        in_specs=[
            whole,
            pl.BlockSpec((depth, tile), lambda i: (0, i)),
            pl.BlockSpec((rows, tile), lambda i: (0, i)),
            pl.BlockSpec((depth, rows), lambda i: (0, 0)),
            pl.BlockSpec((depth, tile), lambda i: (0, i)),
            *[pl.BlockSpec(memory_space=pl.ANY) for _ in widths],
        ],
        out_specs=[
            pl.BlockSpec((depth, tile), lambda i: (0, i)),
            pl.BlockSpec((8, tile), lambda i: (0, i)),
            whole,
            *[pl.BlockSpec((shard_rows, w), lambda i: (0, 0)) for w in widths],
        ],
        out_shape=[
            jax.ShapeDtypeStruct((depth, width), jnp.bfloat16),
            jax.ShapeDtypeStruct((8, width), jnp.float32),
            jax.ShapeDtypeStruct((rows, depth), jnp.float32),
            *[jax.ShapeDtypeStruct((shard_rows, w), jnp.float32) for w in widths],
        ],
        scratch_shapes=scatter_scratch(widths, shard_rows),
        compiler_params=pltpu.CompilerParams(
            vmem_limit_bytes=67043328, collective_id=5, has_side_effects=True
        ),
        cost_estimate=pl.CostEstimate(
            flops=6 * rows * depth * width, bytes_accessed=60 << 20, transcendentals=0
        ),
    )(dz, weight_down, slope, turned, weight_up, *operands)


def finish_kernel(widths, base_ref, grad_ref, weight_ref, *refs):
    count = len(widths)
    out_ref = refs[count]
    sums = refs[count + 1 : 2 * count + 1]
    work = scatter_steps(widths, refs[:count], sums, *refs[2 * count + 1 :])
    now, slots = pl.program_id(0), 16
    spread(work, now, slots, chunks(widths))
    out_ref[...] = base_ref[...] + dot_nt(grad_ref[...], weight_ref[...])

    @pl.when(now == slots - 1)
    def _():
        for step in work[-2:]:
            step()


def finish(base, grad, weight, partials):
    rows, depth = base.shape
    width = grad.shape[1]
    tile = rows // 16
    operands = scatter_operands(partials)
    widths = [p.shape[1] for p in partials]
    shard_rows = operands[0].shape[3]
    return pl.pallas_call(
        partial(finish_kernel, widths),
        name="finish",
        grid=(16,),
        in_specs=[
            pl.BlockSpec((tile, depth), lambda i: (i, 0)),
            pl.BlockSpec((tile, width), lambda i: (i, 0)),
            pl.BlockSpec((depth, width), lambda i: (0, 0)),
            *[pl.BlockSpec(memory_space=pl.ANY) for _ in widths],
        ],
        out_specs=[
            pl.BlockSpec((tile, depth), lambda i: (i, 0)),
            *[pl.BlockSpec((shard_rows, w), lambda i: (0, 0)) for w in widths],
        ],
        out_shape=[
            jax.ShapeDtypeStruct((rows, depth), jnp.float32),
            *[jax.ShapeDtypeStruct((shard_rows, w), jnp.float32) for w in widths],
        ],
        scratch_shapes=scatter_scratch(widths, shard_rows),
        compiler_params=pltpu.CompilerParams(
            vmem_limit_bytes=67043328, collective_id=1, has_side_effects=True
        ),
        cost_estimate=pl.CostEstimate(
            flops=2 * rows * depth * width, bytes_accessed=30 << 20, transcendentals=0
        ),
    )(base, grad, weight, *operands)


def adam_step(master, gradient, first, second, step_rate):
    first_new = beta_one * first + (1.0 - beta_one) * gradient
    second_new = beta_two * second + (1.0 - beta_two) * gradient * gradient
    direction = first_new / bias_one / (jnp.sqrt(second_new / bias_two) + adam_eps)
    return (master - step_rate * (direction + weight_decay * master), first_new, second_new)


def on_device(
    tokens,
    cotangent,
    segments,
    weight_qkv,
    weight_out,
    weight_ffn,
    vectors,
    first_qkv,
    first_out,
    first_ffn,
    first_vec,
    second_qkv,
    second_out,
    second_ffn,
    second_vec,
    outer_qkv,
    outer_out,
    outer_ffn,
    outer_vec,
):
    masters = (weight_qkv, weight_out, weight_ffn, vectors)
    lowered = [master.astype(jnp.bfloat16) for master in masters]
    width = weight_out.shape[1]
    entries = vectors.shape[0] // weight_out.shape[0]
    vector_block = jnp.pad(lowered[3].reshape(-1, entries), ((0, 0), (0, 128 - entries)))
    full_qkv, vector_rows = gather_all([lowered[0], vector_block], (False, True))
    full_vec = vector_rows[:, :entries].reshape(-1)
    vector_values = full_vec.astype(jnp.float32)
    pieces = [vector_values[position * width : (position + 1) * width] for position in range(8)]
    (
        bias_query,
        bias_value,
        bias_output,
        bias_second,
        gain_first,
        shift_first,
        gain_second,
        shift_second,
    ) = pieces
    bias_hidden = vector_values[8 * width :]
    token_rows = tokens[0]
    local_rows = token_rows.shape[0]
    side = lax.axis_index("seq")
    is_first = side == 0
    side_operand = jnp.reshape(side, (1,)).astype(jnp.int32)
    far_tokens = partner(jnp.where(is_first, token_rows[local_rows - W :], token_rows[:W]), "seq", 0)
    wide_tokens = jnp.where(
        is_first,
        jnp.concatenate([token_rows, far_tokens], axis=0),
        jnp.concatenate([far_tokens, token_rows], axis=0),
    )
    joined_bias = jnp.concatenate([bias_query, jnp.zeros_like(bias_query), bias_value])
    projected = (
        jnp.dot(wide_tokens, full_qkv, preferred_element_type=jnp.float32) + joined_bias
    ).astype(jnp.bfloat16)
    wide_ids = lax.dynamic_slice_in_dim(segments[0], side * (local_rows - W), local_rows + W, 0)
    ids_col = jnp.broadcast_to(wide_ids[:, None], (local_rows + W, 128))
    ids_row = jnp.broadcast_to(wide_ids[None, :], (8, local_rows + W))
    attended, attended_wide, logsum, full_out, full_up = attend(
        ids_col, ids_row, projected, [lowered[1], lowered[2][0]]
    )
    branch = jnp.dot(attended, full_out, preferred_element_type=jnp.float32) + bias_output
    residue_first = token_rows.astype(jnp.float32) + branch
    hidden_in, first_pullback = jax.vjp(layer_norm, residue_first, gain_first, shift_first)
    hidden_low = hidden_in.astype(jnp.bfloat16)
    activated_low, slope, full_down = ffn_up(hidden_low, full_up, bias_hidden, [lowered[2][1]])
    second_branch = (
        lax.dot_general(
            activated_low, full_down, (((1,), (1,)), ((), ())), preferred_element_type=jnp.float32
        )
        + bias_second
    )
    residue_second = hidden_in + second_branch
    result, second_pullback = jax.vjp(layer_norm, residue_second, gain_second, shift_second)
    upstream = cotangent[0].astype(jnp.float32)
    residue_second_grad, gain_second_grad, shift_second_grad = second_pullback(upstream)
    branch_two_low = residue_second_grad.astype(jnp.bfloat16)
    bias_second_grad = jnp.sum(branch_two_low.astype(jnp.float32), axis=0)
    down_grad = dot_tn(branch_two_low, activated_low).astype(jnp.bfloat16)
    up_grad, bias_rows, hidden_total, down_sum = ffn_back(
        branch_two_low, full_down, slope, jnp.transpose(hidden_low), full_up, [down_grad]
    )
    bias_hidden_grad = bias_rows[0]
    hidden_grad = residue_second_grad + hidden_total
    residue_first_grad, gain_first_grad, shift_first_grad = first_pullback(hidden_grad)
    branch_low = residue_first_grad.astype(jnp.bfloat16)
    bias_output_grad = jnp.sum(branch_low.astype(jnp.float32), axis=0)
    out_weight_grad = dot_tn(attended, branch_low).astype(jnp.bfloat16)
    mixed_grad = lax.dot_general(
        branch_low, full_out, (((1,), (1,)), ((), ())), preferred_element_type=jnp.float32
    ).astype(jnp.bfloat16)

    heads = width // HD
    head_of = jnp.arange(width, dtype=jnp.int32)[:, None] // HD
    collect = (head_of == jnp.arange(128, dtype=jnp.int32)[None, :]).astype(jnp.float32)
    inner_sums = jnp.dot(
        attended_wide * mixed_grad.astype(jnp.float32), collect, precision=lax.Precision.HIGHEST
    )

    def near_rows(x):
        return jnp.where(is_first, x[local_rows - W :], x[:W])

    far_stats = partner(
        jnp.concatenate([near_rows(logsum)[:, :heads], near_rows(inner_sums)[:, :heads]], axis=1),
        "seq",
        0,
    )
    far_outgrad = partner(near_rows(mixed_grad), "seq", 0)
    lane_pad = ((0, 0), (0, 128 - heads))
    far_logsum = jnp.pad(far_stats[:, :heads], lane_pad)
    far_inner = jnp.pad(far_stats[:, heads:], lane_pad)
    query_grad, key_near, value_near, up_sum = attend_back(
        ids_col, ids_row, projected, mixed_grad, logsum, inner_sums, [up_grad]
    )
    key_grad, value_grad = attend_far(
        side_operand, ids_col, ids_row, projected, far_outgrad, far_logsum, far_inner, key_near, value_near
    )
    projected_grad = jnp.concatenate([query_grad, key_grad, value_grad], axis=1)
    qkv_weight_grad = dot_tn(token_rows, projected_grad).astype(jnp.bfloat16)
    projected_sums = jnp.sum(projected_grad.astype(jnp.float32), axis=0)
    vector_grad = jnp.concatenate(
        [
            projected_sums[:width],
            projected_sums[2 * width :],
            bias_output_grad,
            bias_second_grad,
            gain_first_grad,
            shift_first_grad,
            gain_second_grad,
            shift_second_grad,
            bias_hidden_grad,
        ]
    )
    small = jnp.pad(vector_grad.reshape(width, -1), ((0, 0), (0, 128 - entries))).astype(jnp.bfloat16)
    input_grad, qkv_sum, small_sum, out_sum = finish(
        residue_first_grad, projected_grad, full_qkv, [qkv_weight_grad, small, out_weight_grad]
    )
    summed = (qkv_sum, out_sum, jnp.stack([up_sum, down_sum]), small_sum[:, :entries].reshape(-1))
    firsts = (first_qkv[0], first_out[0], first_ffn[0], first_vec[0])
    seconds = (second_qkv[0], second_out[0], second_ffn[0], second_vec[0])
    outers = (outer_qkv, outer_out, outer_ffn, outer_vec)
    stepped = [
        adam_step(
            masters[member], summed[member], firsts[member], seconds[member], step_rates[member]
        )
        for member in range(4)
    ]
    changes = [masters[member] - stepped[member][0] for member in range(4)]
    lowered_changes = [change.astype(jnp.bfloat16) for change in changes]
    other_changes = [partner(change, "grp", 0) for change in lowered_changes]
    deltas = [
        (lowered_changes[member].astype(jnp.float32) + other_changes[member].astype(jnp.float32)) / 2
        for member in range(4)
    ]
    momenta = [outer_beta * outers[member] + deltas[member] for member in range(4)]
    renewed = [
        masters[member] - outer_rate * (deltas[member] + outer_beta * momenta[member])
        for member in range(4)
    ]
    return (
        result.astype(jnp.bfloat16)[None],
        input_grad[None],
        summed[0][None],
        summed[1][None],
        summed[2][None],
        summed[3][None],
        stepped[0][1][None],
        stepped[1][1][None],
        stepped[2][1][None],
        stepped[3][1][None],
        stepped[0][2][None],
        stepped[1][2][None],
        stepped[2][2][None],
        stepped[3][2][None],
        deltas[0],
        deltas[1],
        deltas[2],
        deltas[3],
        momenta[0],
        momenta[1],
        momenta[2],
        momenta[3],
        renewed[0],
        renewed[1],
        renewed[2],
        renewed[3],
    )


def solution(mesh):
    return jax.shard_map(
        on_device,
        mesh=mesh,
        in_specs=(
            P(("grp", "dp"), "seq", None),
            P(("grp", "dp"), "seq", None),
            P(("grp", "dp"), None),
            P(("dp", "seq"), None),
            P(("dp", "seq"), None),
            P(None, ("dp", "seq"), None),
            P(("dp", "seq")),
            P("grp", ("dp", "seq"), None),
            P("grp", ("dp", "seq"), None),
            P("grp", None, ("dp", "seq"), None),
            P("grp", ("dp", "seq")),
            P("grp", ("dp", "seq"), None),
            P("grp", ("dp", "seq"), None),
            P("grp", None, ("dp", "seq"), None),
            P("grp", ("dp", "seq")),
            P(("dp", "seq"), None),
            P(("dp", "seq"), None),
            P(None, ("dp", "seq"), None),
            P(("dp", "seq")),
        ),
        out_specs=(
            P(("grp", "dp"), "seq", None),
            P(("grp", "dp"), "seq", None),
            P("grp", ("dp", "seq"), None),
            P("grp", ("dp", "seq"), None),
            P("grp", None, ("dp", "seq"), None),
            P("grp", ("dp", "seq")),
            P("grp", ("dp", "seq"), None),
            P("grp", ("dp", "seq"), None),
            P("grp", None, ("dp", "seq"), None),
            P("grp", ("dp", "seq")),
            P("grp", ("dp", "seq"), None),
            P("grp", ("dp", "seq"), None),
            P("grp", None, ("dp", "seq"), None),
            P("grp", ("dp", "seq")),
            P(("dp", "seq"), None),
            P(("dp", "seq"), None),
            P(None, ("dp", "seq"), None),
            P(("dp", "seq")),
            P(("dp", "seq"), None),
            P(("dp", "seq"), None),
            P(None, ("dp", "seq"), None),
            P(("dp", "seq")),
            P(("dp", "seq"), None),
            P(("dp", "seq"), None),
            P(None, ("dp", "seq"), None),
            P(("dp", "seq")),
        ),
        check_vma=False,
    )
```

```python
from functools import partial

import jax
import jax.numpy as jnp
from jax import lax
from jax.experimental import pallas as pl
from jax.experimental.pallas import tpu as pltpu
from jax.sharding import PartitionSpec as P

HD = 64
W = 512


beta_one = 0.9
beta_two = 0.95
adam_eps = 1e-08
weight_decay = 0.1
bias_one = 1.0 - 0.9**10
bias_two = 1.0 - 0.95**10
step_rates = (0.01, 0.1, 0.005, 0.2)
outer_rate = 0.7
outer_beta = 0.9
norm_eps = 1e-05
score_fill = -1e30


def partner(x, axis, stride):
    return lax.ppermute(x, axis, [(i, i ^ 1 << stride) for i in range(lax.axis_size(axis))])


def layer_norm(residue, norm_gain, norm_shift):
    average = jnp.mean(residue, axis=-1, keepdims=True)
    centred = residue - average
    variance = jnp.mean(centred * centred, axis=-1, keepdims=True)
    return centred * lax.rsqrt(variance + norm_eps) * norm_gain + norm_shift


TILE = 256
LENGTHS = (3, 4, 5, 5)


def first_tile(side, j):
    return jnp.where(side == 0, jnp.maximum(j - 2, 0), 3 - j)


def query_tile(side, j):
    return jnp.where(side == 0, j, 5 - j)


def own_tile(side, j):
    return jnp.where(side == 0, j, 3 - j)


def dot_nt(a, b):
    return lax.dot_general(a, b, (((1,), (1,)), ((), ())), preferred_element_type=jnp.float32)


def dot_tn(a, b):
    return lax.dot_general(a, b, (((0,), (0,)), ((), ())), preferred_element_type=jnp.float32)


def dot_nn(a, b):
    return lax.dot_general(a, b, (((1,), (0,)), ((), ())), preferred_element_type=jnp.float32)


def mask_bias(query_start, key_start, query_ids, key_ids):
    rows, cols = query_ids.shape[0], key_ids.shape[1]
    relative = (
        lax.broadcasted_iota(jnp.int32, (rows, cols), 1)
        - lax.broadcasted_iota(jnp.int32, (rows, cols), 0)
        + (key_start - query_start)
    )
    allowed = (relative <= W) & (relative >= -W) & (query_ids == key_ids)
    return jnp.where(allowed, 0.0, score_fill)


def pair_split(x):
    lane = lax.broadcasted_iota(jnp.int32, x.shape, 1)
    zero = jnp.zeros_like(x)
    return jnp.where(lane < HD, x, zero), jnp.where(lane < HD, zero, x)


def pick_lane(x, index):
    lane = lax.broadcasted_iota(jnp.int32, x.shape, 1)
    return jnp.sum(jnp.where(lane == index, x, 0.0), axis=1, keepdims=True)


def attend_kernel(
    shared, ids_col_ref, ids_row_ref, q_ref, k_ref, v_ref, *refs
):
    count = len(shared)
    o_ref, wide_ref, lse_ref = refs[count : count + 3]
    wholes = refs[count + 3 : 2 * count + 3]
    bias_ref = refs[2 * count + 3]
    j, pair = pl.program_id(0), pl.program_id(1)
    side = lax.axis_index("seq")
    now = j * pl.num_programs(1) + pair
    slots = 32
    work = gather_steps(shared, refs[:count], wholes, *refs[2 * count + 4 :])
    spread(work, now, slots, 0)

    def run(length):
        span = length * TILE
        start = pl.multiple_of(first_tile(side, j) * TILE, TILE)

        @pl.when(pair == 0)
        def _():
            bias_ref[:, :span] = mask_bias(
                query_tile(side, j) * TILE,
                start,
                ids_col_ref[:, :1],
                ids_row_ref[:1, pl.ds(start, span)],
            )
            lse_ref[...] = jnp.zeros_like(lse_ref)

        queries = pair_split(q_ref[...] * jnp.bfloat16(HD**-0.5))
        keys = k_ref[pl.ds(start, span), :]
        values = pair_split(v_ref[pl.ds(start, span), :])
        total = None
        lane = lax.broadcasted_iota(jnp.int32, lse_ref.shape, 1)
        for h in range(2):
            scores = dot_nt(queries[h], keys) + bias_ref[:, :span]
            maximum = jnp.max(scores, axis=1, keepdims=True)
            exponent = jnp.exp(scores - maximum)
            denominator = jnp.sum(exponent, axis=1, keepdims=True)
            weights = (exponent * (1.0 / denominator)).astype(jnp.bfloat16)
            part = dot_nn(weights, values[h])
            total = part if total is None else total + part
            logsum = maximum + jnp.log(denominator)
            lse_ref[...] = jnp.where(lane == 2 * pair + h, logsum, lse_ref[...])
        o_ref[...] = total.astype(jnp.bfloat16)
        wide_ref[...] = total

    for length in sorted(set(LENGTHS)):
        hits = [i for i in range(4) if LENGTHS[i] == length]

        @pl.when((j >= hits[0]) & (j <= hits[-1]))
        def _():
            run(length)

    @pl.when(now == slots - 1)
    def _():
        for step in work[-2:]:
            step()


def attend(ids_col, ids_row, qkv, shards):
    rows, width = qkv.shape[0], qkv.shape[1] // 3
    pairs = width // 128
    own = rows - W
    shared = (False,) * len(shards)
    got = pl.pallas_call(
        partial(attend_kernel, shared),
        name="attend",
        grid_spec=pltpu.PrefetchScalarGridSpec(
            num_scalar_prefetch=0,
            grid=(own // TILE, pairs),
            in_specs=[
                pl.BlockSpec((TILE, 128), lambda j, p: (query_tile(lax.axis_index("seq"), j), 0)),
                pl.BlockSpec((8, rows), lambda j, p: (0, 0)),
                pl.BlockSpec((TILE, 128), lambda j, p: (query_tile(lax.axis_index("seq"), j), p)),
                pl.BlockSpec((rows, 128), lambda j, p: (0, pairs + p)),
                pl.BlockSpec((rows, 128), lambda j, p: (0, 2 * pairs + p)),
                *[pl.BlockSpec(s.shape, lambda j, p: (0, 0)) for s in shards],
            ],
            out_specs=[
                pl.BlockSpec((TILE, 128), lambda j, p: (own_tile(lax.axis_index("seq"), j), p)),
                pl.BlockSpec((TILE, 128), lambda j, p: (own_tile(lax.axis_index("seq"), j), p)),
                pl.BlockSpec((TILE, 128), lambda j, p: (own_tile(lax.axis_index("seq"), j), 0)),
                *[pl.BlockSpec(memory_space=pl.ANY) for s in shards],
            ],
            scratch_shapes=[
                pltpu.VMEM((TILE, 5 * TILE), jnp.float32),
                *gather_scratch(shards, shared),
            ],
        ),
        out_shape=[
            jax.ShapeDtypeStruct((own, width), jnp.bfloat16),
            jax.ShapeDtypeStruct((own, width), jnp.float32),
            jax.ShapeDtypeStruct((own, 128), jnp.float32),
            *gather_shapes(shards),
        ],
        compiler_params=pltpu.CompilerParams(
            vmem_limit_bytes=48 << 20, collective_id=2, has_side_effects=True
        ),
        cost_estimate=pl.CostEstimate(
            flops=4 * 17 * TILE * TILE * width * 4, bytes_accessed=30 << 20, transcendentals=0
        ),
    )(ids_col, ids_row, qkv, qkv, qkv, *shards)
    return [*got[:3], *[w.reshape(-1, w.shape[-1]) for w in got[3:]]]


def attend_back_kernel(
    widths, ids_col_ref, ids_row_ref, q_ref, k_ref, v_ref, do_ref, lse_ref, inner_ref, *refs
):
    count = len(widths)
    dq_ref, dk_ref, dv_ref = refs[count : count + 3]
    sums = refs[count + 3 : 2 * count + 3]
    bias_ref, dkt_ref, dvt_ref = refs[2 * count + 3 : 2 * count + 6]
    pair, j = pl.program_id(0), pl.program_id(1)
    side = lax.axis_index("seq")
    own = dk_ref.shape[0]
    now, slots = pair * pl.num_programs(1) + j, 32
    work = scatter_steps(widths, refs[:count], sums, *refs[2 * count + 6 :])
    spread(work, now, slots, chunks(widths))

    @pl.when(j == 0)
    def _():
        dkt_ref[...] = jnp.zeros_like(dkt_ref)
        dvt_ref[...] = jnp.zeros_like(dvt_ref)

    def run(length):
        span = length * TILE
        start = pl.multiple_of(first_tile(side, j) * TILE, TILE)

        @pl.when(pair == 0)
        def _():
            bias_ref[j, :, :span] = mask_bias(
                query_tile(side, j) * TILE,
                start,
                ids_col_ref[:, :1],
                ids_row_ref[:1, pl.ds(start, span)],
            )

        scaled = q_ref[...] * jnp.bfloat16(HD**-0.5)
        outgrad = do_ref[...]
        queries = pair_split(scaled)
        outgrads = pair_split(outgrad)
        turned_q = jnp.transpose(scaled.astype(jnp.float32)).astype(jnp.bfloat16)
        turned_do = jnp.transpose(outgrad.astype(jnp.float32)).astype(jnp.bfloat16)
        keys = k_ref[pl.ds(start, span), :]
        values = v_ref[pl.ds(start, span), :]
        key_parts = pair_split(keys)
        total = None
        for h in range(2):
            logsum = pick_lane(lse_ref[...], 2 * pair + h)
            inner = pick_lane(inner_ref[...], 2 * pair + h)
            scores = dot_nt(queries[h], keys) + bias_ref[j, :, :span]
            probs = jnp.exp(scores - logsum)
            prob_grad = dot_nt(outgrads[h], values)
            score_grad = (probs * (prob_grad - inner)).astype(jnp.bfloat16)
            part = dot_nn(score_grad, key_parts[h])
            total = part if total is None else total + part
            head = slice(h * HD, (h + 1) * HD)
            dvt_ref[head, pl.ds(start, span)] += dot_nn(turned_do[head], probs.astype(jnp.bfloat16))
            dkt_ref[head, pl.ds(start, span)] += dot_nn(turned_q[head], score_grad)
        dq_ref[...] = (total * HD**-0.5).astype(jnp.bfloat16)

    for length in sorted(set(LENGTHS)):
        hits = [i for i in range(4) if LENGTHS[i] == length]

        @pl.when((j >= hits[0]) & (j <= hits[-1]))
        def _():
            run(length)

    @pl.when(j == pl.num_programs(1) - 1)
    def _():
        at = pl.multiple_of(side * W, W)
        dk_ref[...] = jnp.transpose(dkt_ref[:, pl.ds(at, own)])
        dv_ref[...] = jnp.transpose(dvt_ref[:, pl.ds(at, own)])

    @pl.when(now == slots - 1)
    def _():
        for step in work[-2:]:
            step()


def attend_back(ids_col, ids_row, qkv, outgrad, lse, inner, partials):
    rows, width = qkv.shape[0], qkv.shape[1] // 3
    pairs = width // 128
    own = rows - W
    operands = scatter_operands(partials)
    widths = [p.shape[1] for p in partials]
    shard_rows = operands[0].shape[3]
    return pl.pallas_call(
        partial(attend_back_kernel, widths),
        name="attend_back",
        grid_spec=pltpu.PrefetchScalarGridSpec(
            num_scalar_prefetch=0,
            grid=(pairs, own // TILE),
            in_specs=[
                pl.BlockSpec((TILE, 128), lambda p, j: (query_tile(lax.axis_index("seq"), j), 0)),
                pl.BlockSpec((8, rows), lambda p, j: (0, 0)),
                pl.BlockSpec((TILE, 128), lambda p, j: (query_tile(lax.axis_index("seq"), j), p)),
                pl.BlockSpec((rows, 128), lambda p, j: (0, pairs + p)),
                pl.BlockSpec((rows, 128), lambda p, j: (0, 2 * pairs + p)),
                pl.BlockSpec((TILE, 128), lambda p, j: (own_tile(lax.axis_index("seq"), j), p)),
                pl.BlockSpec((TILE, 128), lambda p, j: (own_tile(lax.axis_index("seq"), j), 0)),
                pl.BlockSpec((TILE, 128), lambda p, j: (own_tile(lax.axis_index("seq"), j), 0)),
                *[pl.BlockSpec(memory_space=pl.ANY) for _ in widths],
            ],
            out_specs=[
                pl.BlockSpec((TILE, 128), lambda p, j: (own_tile(lax.axis_index("seq"), j), p)),
                pl.BlockSpec((own, 128), lambda p, j: (0, p)),
                pl.BlockSpec((own, 128), lambda p, j: (0, p)),
                *[pl.BlockSpec((shard_rows, w), lambda p, j: (0, 0)) for w in widths],
            ],
            scratch_shapes=[
                pltpu.VMEM((own // TILE, TILE, 5 * TILE), jnp.float32),
                pltpu.VMEM((128, rows), jnp.float32),
                pltpu.VMEM((128, rows), jnp.float32),
                *scatter_scratch(widths, shard_rows),
            ],
        ),
        out_shape=[
            jax.ShapeDtypeStruct((own, width), jnp.bfloat16),
            jax.ShapeDtypeStruct((own, width), jnp.float32),
            jax.ShapeDtypeStruct((own, width), jnp.float32),
            *[jax.ShapeDtypeStruct((shard_rows, w), jnp.float32) for w in widths],
        ],
        compiler_params=pltpu.CompilerParams(
            vmem_limit_bytes=67043328, collective_id=3, has_side_effects=True
        ),
        cost_estimate=pl.CostEstimate(
            flops=10 * 17 * TILE * TILE * width * 4, bytes_accessed=40 << 20, transcendentals=0
        ),
    )(ids_col, ids_row, qkv, qkv, qkv, outgrad, lse, inner, *operands)


def attend_far_kernel(
    side_ref, ids_col_ref, ids_row_ref, q_ref, k_ref, v_ref, do_ref, lse_ref, inner_ref,
    dk_in_ref, dv_in_ref, dk_ref, dv_ref, bias_ref,
):
    pair = pl.program_id(0)
    side = side_ref[0]

    @pl.when(pair == 0)
    def _():
        bias_ref[...] = mask_bias(
            jnp.where(side == 0, 2 * W, 0), W, ids_col_ref[:, :1], ids_row_ref[:1, W : 2 * W]
        )

    scaled = q_ref[...] * jnp.bfloat16(HD**-0.5)
    outgrad = do_ref[...]
    queries = pair_split(scaled)
    outgrads = pair_split(outgrad)
    turned_q = jnp.transpose(scaled.astype(jnp.float32)).astype(jnp.bfloat16)
    turned_do = jnp.transpose(outgrad.astype(jnp.float32)).astype(jnp.bfloat16)
    keys, values = k_ref[...], v_ref[...]
    dk_parts, dv_parts = [], []
    for h in range(2):
        logsum = pick_lane(lse_ref[...], 2 * pair + h)
        inner = pick_lane(inner_ref[...], 2 * pair + h)
        scores = dot_nt(queries[h], keys) + bias_ref[...]
        probs = jnp.exp(scores - logsum)
        prob_grad = dot_nt(outgrads[h], values)
        score_grad = (probs * (prob_grad - inner)).astype(jnp.bfloat16)
        head = slice(h * HD, (h + 1) * HD)
        dv_parts.append(dot_nn(turned_do[head], probs.astype(jnp.bfloat16)))
        dk_parts.append(dot_nn(turned_q[head], score_grad))
    dk_far = jnp.transpose(jnp.concatenate(dk_parts, axis=0))
    dv_far = jnp.transpose(jnp.concatenate(dv_parts, axis=0))
    near = pl.multiple_of(jnp.where(side == 0, W, 0), W)
    rest = pl.multiple_of(jnp.where(side == 0, 0, W), W)
    dk_ref[pl.ds(near, W), :] = (dk_in_ref[pl.ds(near, W), :] + dk_far).astype(jnp.bfloat16)
    dv_ref[pl.ds(near, W), :] = (dv_in_ref[pl.ds(near, W), :] + dv_far).astype(jnp.bfloat16)
    dk_ref[pl.ds(rest, W), :] = dk_in_ref[pl.ds(rest, W), :].astype(jnp.bfloat16)
    dv_ref[pl.ds(rest, W), :] = dv_in_ref[pl.ds(rest, W), :].astype(jnp.bfloat16)


def attend_far(side, ids_col, ids_row, qkv, far_outgrad, far_lse, far_inner, dk, dv):
    rows, width = qkv.shape[0], qkv.shape[1] // 3
    pairs = width // 128
    own = rows - W
    far = lambda p, s: (jnp.where(s[0] == 0, 2, 0), p)
    return pl.pallas_call(
        attend_far_kernel,
        name="attend_far",
        grid_spec=pltpu.PrefetchScalarGridSpec(
            num_scalar_prefetch=1,
            grid=(pairs,),
            in_specs=[
                pl.BlockSpec((W, 128), lambda p, s: (jnp.where(s[0] == 0, 2, 0), 0)),
                pl.BlockSpec((8, rows), lambda p, s: (0, 0)),
                pl.BlockSpec((W, 128), far),
                pl.BlockSpec((W, 128), lambda p, s: (1, pairs + p)),
                pl.BlockSpec((W, 128), lambda p, s: (1, 2 * pairs + p)),
                pl.BlockSpec((W, 128), lambda p, s: (0, p)),
                pl.BlockSpec((W, 128), lambda p, s: (0, 0)),
                pl.BlockSpec((W, 128), lambda p, s: (0, 0)),
                pl.BlockSpec((own, 128), lambda p, s: (0, p)),
                pl.BlockSpec((own, 128), lambda p, s: (0, p)),
            ],
            out_specs=[
                pl.BlockSpec((own, 128), lambda p, s: (0, p)),
                pl.BlockSpec((own, 128), lambda p, s: (0, p)),
            ],
            scratch_shapes=[pltpu.VMEM((W, W), jnp.float32)],
        ),
        out_shape=[jax.ShapeDtypeStruct((own, width), jnp.bfloat16)] * 2,
        compiler_params=pltpu.CompilerParams(vmem_limit_bytes=48 << 20),
        cost_estimate=pl.CostEstimate(
            flops=8 * 4 * TILE * TILE * width * 4, bytes_accessed=20 << 20, transcendentals=0
        ),
    )(side, ids_col, ids_row, qkv, qkv, qkv, far_outgrad, far_lse, far_inner, dk, dv)


AXES = ("z", "x", "y")
GATHER_ORDERS = ((("z", "x", "y"), 3), (("z", "y", "x"), 3), (("x", "y", "z"), 2))
SCATTER_ORDERS = ((("y", "x", "z"), 3), (("x", "y", "z"), 3), (("z", "y", "x"), 2))
PIECE = 1024


def axis_parts():
    total = lax.axis_size("dp")
    inner = 2 ** ((total.bit_length() - 1) // 2)
    return {"z": total // inner, "x": inner, "y": lax.axis_size("seq")}


def places():
    inner = axis_parts()["x"]
    row = lax.axis_index("dp")
    return {"z": lax.div(row, inner), "x": lax.rem(row, inner), "y": lax.axis_index("seq")}


def neighbour(axis, step):
    parts, spots = axis_parts(), places()
    size = parts[axis]
    spots[axis] = lax.rem(spots[axis] + step + size, size)
    return (lax.axis_index("grp"), spots["z"] * parts["x"] + spots["x"], spots["y"])


def twin():
    return (1 - lax.axis_index("grp"), lax.axis_index("dp"), lax.axis_index("seq"))


def greet(peers):
    barrier = pltpu.get_barrier_semaphore()
    for peer in peers:
        pl.semaphore_signal(barrier, inc=1, device_id=peer, device_id_type=pl.DeviceIdType.MESH)
    pl.semaphore_wait(barrier, len(peers))


def ring_peers():
    return [neighbour(axis, step) for axis in AXES for step in (1, -1)]


def flows_of(widths, orders):
    flows = []
    for member, width in enumerate(widths):
        pieces = chunks([width])
        for piece in range(pieces):
            tiles, begin = width // pieces // 128, piece * (width // pieces)
            if tiles < len(orders):
                flows.append((member, orders[0][0], begin, tiles * 128, piece))
                continue
            total = sum(share for _, share in orders)
            low, used = 0, 0
            for order, share in orders:
                used += share
                high = -(-used * tiles // total)
                flows.append((member, order, begin + low * 128, (high - low) * 128, piece))
                low = high
    return flows


def delays(flows, gap):
    seen, found = [], []
    for member, _, _, _, piece in flows:
        if (member, piece) not in seen:
            seen.append((member, piece))
        found.append((len(seen) - 1) * gap)
    return found


def gather_steps(shared, shards, wholes, send_sems, recv_sems, own_sems):
    count = len(shared)
    parts, spots = axis_parts(), places()
    core = lax.axis_index("grp")
    spans = [s.shape[1] if shared[m] else s.shape[1] // 2 for m, s in enumerate(shards)]

    def columns(member, begin, width):
        if shared[member]:
            return pl.ds(begin, width)
        return pl.ds(pl.multiple_of(core * spans[member] + begin, 128), width)

    def own(member):
        cut = columns(member, 0, spans[member])
        return pltpu.make_async_copy(
            shards[member].at[:, cut],
            wholes[member].at[spots["z"], spots["x"], spots["y"], :, cut],
            own_sems.at[member],
        )

    flows = flows_of(spans, GATHER_ORDERS)
    chains, first = [], []
    for member, order, begin, width, _ in flows:
        cut = columns(member, begin, width)
        steps, done = [], []
        for axis in order:
            for turn in range(parts[axis] - 1):
                select = []
                for a in AXES:
                    if a == axis:
                        select.append(pl.ds(lax.rem(spots[a] + parts[a] - turn, parts[a]), 1))
                    elif a in done:
                        select.append(pl.ds(0, parts[a]))
                    else:
                        select.append(pl.ds(spots[a], 1))
                steps.append((wholes[member].at[(*select, slice(None), cut)], neighbour(axis, 1)))
            done.append(axis)
        if not shared[member]:
            steps.append((wholes[member].at[:, :, :, :, cut], twin()))
        first.append(sum(len(c) for c in chains))
        chains.append(steps)

    def remote(i, at):
        block, peer = chains[i][at]
        return pltpu.make_async_remote_copy(
            src_ref=block,
            dst_ref=block,
            send_sem=send_sems.at[first[i] + at],
            recv_sem=recv_sems.at[first[i] + at],
            device_id=peer,
            device_id_type=pl.DeviceIdType.MESH,
        )

    late = delays(flows, 1)
    length = max(late[i] + len(chains[i]) for i in range(len(flows)))

    def begin():
        greet(ring_peers() + [twin()])
        for member in range(count):
            own(member).start()
        for member in range(count):
            own(member).wait()

    def tick(time):
        for i, steps in enumerate(chains):
            at = time - late[i]
            if 1 <= at <= len(steps):
                remote(i, at - 1).wait_recv()
            if 0 <= at < len(steps):
                remote(i, at).start()

    def finish():
        for i, steps in enumerate(chains):
            for at in range(len(steps)):
                remote(i, at).wait_send()

    return [begin] + [partial(tick, time) for time in range(length + 1)] + [finish]


def gather_kernel(shared, *refs):
    count = len(shared)
    for step in gather_steps(shared, refs[:count], refs[count : 2 * count], *refs[2 * count :]):
        step()


def gather_scratch(shards, shared):
    parts = axis_parts()
    hops = sum(size - 1 for size in parts.values()) + 1
    spans = [s.shape[1] if shared[m] else s.shape[1] // 2 for m, s in enumerate(shards)]
    copies = hops * len(flows_of(spans, GATHER_ORDERS))
    return [
        pltpu.SemaphoreType.DMA((copies,)),
        pltpu.SemaphoreType.DMA((copies,)),
        pltpu.SemaphoreType.DMA((len(shards),)),
    ]


def gather_shapes(shards):
    parts = axis_parts()
    return [jax.ShapeDtypeStruct((parts["z"], parts["x"], parts["y"], *s.shape), s.dtype) for s in shards]


def gather_all(shards, shared):
    wholes = pl.pallas_call(
        partial(gather_kernel, shared),
        name="gather_all",
        in_specs=[pl.BlockSpec(memory_space=pltpu.VMEM)] * len(shards),
        out_specs=[pl.BlockSpec(memory_space=pl.ANY)] * len(shards),
        out_shape=gather_shapes(shards),
        scratch_shapes=gather_scratch(shards, shared),
        compiler_params=pltpu.CompilerParams(collective_id=0, has_side_effects=True),
    )(*shards)
    return [w.reshape(-1, w.shape[-1]) for w in wholes]


def scatter_plan(widths):
    parts = axis_parts()
    plan = []
    for member, order, begin, width, piece in flows_of(widths, SCATTER_ORDERS):
        left, levels = list(AXES), []
        for axis in order:
            left.remove(axis)
            levels.append((axis, tuple(parts[a] for a in left), [a for a in left]))
        plan.append((member, order, begin, width, piece, levels))
    return plan


def scatter_steps(widths, partials, sums, send_sems, recv_sems, load_sems, *buffers):
    plan = scatter_plan(widths)
    buffers = list(buffers)
    parts, spots = axis_parts(), places()
    chains, copies = [], []
    for member, order, begin, width, _, levels in plan:
        cut = pl.ds(begin, width)
        chain = []
        source, before = partials[member], list(AXES)
        for depth, (axis, extent, left) in enumerate(levels):
            size = parts[axis]
            inbox = [buffers.pop(0) for _ in range(size - 1)]
            terms = []
            for turn in range(size):
                index = lax.rem(spots[axis] + 2 * size - 1 - turn, size)
                select = tuple(index if a == axis else slice(None) for a in before)
                if depth:
                    terms.append(source.at[select])
                else:
                    terms.append(source.at[(*select, slice(None), cut)])
            ready = []
            if depth == 0:
                for turn in range(1, size):
                    local = buffers.pop(0)
                    copies.append((terms[turn], local))
                    ready.append(len(copies) - 1)
                    terms[turn] = local
            chain.append((axis, extent, inbox, terms, ready))
            source, before = inbox[-1], left
        chains.append(chain)

    def accumulate(target, term, extent):
        total = 1
        for size in extent:
            total *= size

        def body(index, carry):
            where, left = [], index
            for size in reversed(extent):
                where.insert(0, lax.rem(left, size))
                left = lax.div(left, size)
            where = tuple(where)
            target[where] = (
                target[where].astype(jnp.float32) + term[where].astype(jnp.float32)
            ).astype(jnp.bfloat16)
            return carry

        lax.fori_loop(0, total, body, 0)

    flat, first = [], []
    for chain in chains:
        steps = []
        for depth, (axis, extent, inbox, terms, ready) in enumerate(chain):
            for turn in range(parts[axis] - 1):
                steps.append((depth, axis, turn))
        first.append(sum(len(f) for f in flat))
        flat.append(steps)
    late = delays([p[:5] for p in plan], 1)
    length = max(late[i] + len(flat[i]) for i in range(len(plan)))

    def load(index):
        return pltpu.make_async_copy(*copies[index], load_sems.at[index])

    def remote(i, at):
        depth, axis, turn = flat[i][at]
        _, extent, inbox, terms, ready = chains[i][depth]
        return pltpu.make_async_remote_copy(
            src_ref=inbox[turn - 1] if turn else terms[0],
            dst_ref=inbox[turn],
            send_sem=send_sems.at[first[i] + at],
            recv_sem=recv_sems.at[first[i] + at],
            device_id=neighbour(axis, 1),
            device_id_type=pl.DeviceIdType.MESH,
        )

    def begin():
        greet(ring_peers())
        for index in range(len(copies)):
            load(index).start()

    def tick(time):
        for i, steps in enumerate(flat):
            at = time - late[i]
            if 1 <= at <= len(steps):
                remote(i, at - 1).wait_recv()
                depth, axis, turn = steps[at - 1]
                _, extent, inbox, terms, ready = chains[i][depth]
                if ready:
                    load(ready[turn]).wait()
                if at < len(steps):
                    accumulate(inbox[turn], terms[turn + 1], extent)
                else:
                    member, _, begin, width = plan[i][:4]
                    sums[member][:, begin : begin + width] = inbox[turn][...].astype(
                        jnp.float32
                    ) + terms[turn + 1][...].astype(jnp.float32)
            if 0 <= at < len(steps):
                remote(i, at).start()

    def finish():
        for i, steps in enumerate(flat):
            for at in range(len(steps)):
                remote(i, at).wait_send()

    return [begin] + [partial(tick, time) for time in range(length + 1)] + [finish]


def scatter_scratch(widths, rows):
    parts = axis_parts()
    buffers, copies, loads = [], 0, 0
    for _, order, _, width, _, levels in scatter_plan(widths):
        for depth, (axis, extent, _) in enumerate(levels):
            slots = parts[axis] - 1
            copies += slots
            if depth == 0:
                loads += slots
                slots *= 2
            buffers += [pltpu.VMEM((*extent, rows, width), jnp.bfloat16)] * slots
    return [
        pltpu.SemaphoreType.DMA((copies,)),
        pltpu.SemaphoreType.DMA((copies,)),
        pltpu.SemaphoreType.DMA((loads,)),
        *buffers,
    ]


def scatter_operands(partials):
    parts = axis_parts()
    return [p.reshape(parts["z"], parts["x"], parts["y"], -1, p.shape[1]) for p in partials]


def spread(work, now, slots, busy):
    ticks = len(work) - 3
    for order, step in enumerate(work[:-2]):
        time = max(0, order - 1)
        if busy:
            slot = min(slots - 1, time * slots // busy)
        elif time < 4:
            slot = time
        else:
            slot = 3 + (time - 3) * (slots - 4) // (ticks - 3)
        pl.when(now == slot)(step)


def chunks(widths):
    return sum(max(1, min(4, width // PIECE)) for width in widths)


def ffn_up_kernel(shared, x_ref, w_ref, bias_ref, *refs):
    count = len(shared)
    active_ref, slope_ref = refs[count : count + 2]
    wholes = refs[count + 2 : 2 * count + 2]
    work = gather_steps(shared, refs[:count], wholes, *refs[2 * count + 2 :])
    now, slots = pl.program_id(0), 16
    spread(work, now, slots, 0)
    rows = 256
    for begin in range(0, x_ref.shape[0], rows):
        block = slice(begin, begin + rows)
        u = dot_nn(x_ref[block, :], w_ref[...]) + bias_ref[:1, :]
        share = 0.5 + 0.5 * lax.erf(u * 0.5**0.5)
        density = (0.5 / jnp.pi) ** 0.5 * jnp.exp(-0.5 * u * u)
        active_ref[block, :] = (u * share).astype(jnp.bfloat16)
        slope_ref[block, :] = (share + u * density).astype(jnp.bfloat16)

    @pl.when(now == slots - 1)
    def _():
        for step in work[-2:]:
            step()


def ffn_up(x, weight, bias, shards):
    rows, depth = x.shape
    width = weight.shape[1]
    tile = width // 16
    shared = (False,) * len(shards)
    got = pl.pallas_call(
        partial(ffn_up_kernel, shared),
        name="ffn_up",
        grid=(16,),
        in_specs=[
            pl.BlockSpec((rows, depth), lambda i: (0, 0)),
            pl.BlockSpec((depth, tile), lambda i: (0, i)),
            pl.BlockSpec((8, tile), lambda i: (0, i)),
            *[pl.BlockSpec(s.shape, lambda i: (0, 0)) for s in shards],
        ],
        out_specs=[
            pl.BlockSpec((rows, tile), lambda i: (0, i)),
            pl.BlockSpec((rows, tile), lambda i: (0, i)),
            *[pl.BlockSpec(memory_space=pl.ANY) for s in shards],
        ],
        out_shape=[
            jax.ShapeDtypeStruct((rows, width), jnp.bfloat16),
            jax.ShapeDtypeStruct((rows, width), jnp.bfloat16),
            *gather_shapes(shards),
        ],
        scratch_shapes=gather_scratch(shards, shared),
        compiler_params=pltpu.CompilerParams(
            vmem_limit_bytes=48 << 20, collective_id=4, has_side_effects=True
        ),
        cost_estimate=pl.CostEstimate(
            flops=2 * rows * depth * width, bytes_accessed=40 << 20, transcendentals=0
        ),
    )(x, weight, jnp.broadcast_to(bias[None, :], (8, width)), *shards)
    return [*got[:2], *[w.reshape(-1, w.shape[-1]) for w in got[2:]]]


def ffn_back_kernel(widths, dz_ref, down_ref, slope_ref, x_ref, up_ref, *refs):
    count = len(widths)
    turned_ref, *refs = refs[2 * count + 3], *refs[: 2 * count + 3], *refs[2 * count + 4 :]
    up_grad_ref, bias_ref, total_ref = refs[count : count + 3]
    sums = refs[count + 3 : 2 * count + 3]
    work = scatter_steps(widths, refs[:count], sums, *refs[2 * count + 3 :])
    now, slots = pl.program_id(0), 16
    spread(work, now, slots, chunks(widths))

    @pl.when(now == 0)
    def _():
        total_ref[...] = jnp.zeros_like(total_ref)
        for begin in range(0, x_ref.shape[0], TILE):
            block = slice(begin, begin + TILE)
            turned_ref[:, block] = jnp.transpose(x_ref[block, :].astype(jnp.float32)).astype(jnp.bfloat16)

    inner = (dot_nn(dz_ref[...], down_ref[...]) * slope_ref[...].astype(jnp.float32)).astype(jnp.bfloat16)
    column = jnp.sum(inner.astype(jnp.float32), axis=0, keepdims=True)
    bias_ref[...] = jnp.broadcast_to(column, bias_ref.shape)
    up_grad_ref[...] = dot_nn(turned_ref[...], inner).astype(jnp.bfloat16)
    total_ref[...] += dot_nt(inner, up_ref[...])

    @pl.when(now == slots - 1)
    def _():
        for step in work[-2:]:
            step()


def ffn_back(dz, weight_down, slope, x, weight_up, partials):
    rows, depth = dz.shape
    width = weight_up.shape[1]
    tile = width // 16
    operands = scatter_operands(partials)
    widths = [p.shape[1] for p in partials]
    shard_rows = operands[0].shape[3]
    whole = pl.BlockSpec((rows, depth), lambda i: (0, 0))
    return pl.pallas_call(
        partial(ffn_back_kernel, widths),
        name="ffn_back",
        grid=(16,),
        in_specs=[
            whole,
            pl.BlockSpec((depth, tile), lambda i: (0, i)),
            pl.BlockSpec((rows, tile), lambda i: (0, i)),
            whole,
            pl.BlockSpec((depth, tile), lambda i: (0, i)),
            *[pl.BlockSpec(memory_space=pl.ANY) for _ in widths],
        ],
        out_specs=[
            pl.BlockSpec((depth, tile), lambda i: (0, i)),
            pl.BlockSpec((8, tile), lambda i: (0, i)),
            whole,
            *[pl.BlockSpec((shard_rows, w), lambda i: (0, 0)) for w in widths],
        ],
        out_shape=[
            jax.ShapeDtypeStruct((depth, width), jnp.bfloat16),
            jax.ShapeDtypeStruct((8, width), jnp.float32),
            jax.ShapeDtypeStruct((rows, depth), jnp.float32),
            *[jax.ShapeDtypeStruct((shard_rows, w), jnp.float32) for w in widths],
        ],
        scratch_shapes=[pltpu.VMEM((depth, rows), jnp.bfloat16), *scatter_scratch(widths, shard_rows)],
        compiler_params=pltpu.CompilerParams(
            vmem_limit_bytes=67043328, collective_id=5, has_side_effects=True
        ),
        cost_estimate=pl.CostEstimate(
            flops=6 * rows * depth * width, bytes_accessed=60 << 20, transcendentals=0
        ),
    )(dz, weight_down, slope, x, weight_up, *operands)


def finish_kernel(widths, base_ref, grad_ref, weight_ref, *refs):
    count = len(widths)
    out_ref = refs[count]
    sums = refs[count + 1 : 2 * count + 1]
    work = scatter_steps(widths, refs[:count], sums, *refs[2 * count + 1 :])
    now, slots = pl.program_id(0), 16
    spread(work, now, slots, chunks(widths))
    out_ref[...] = base_ref[...] + dot_nt(grad_ref[...], weight_ref[...])

    @pl.when(now == slots - 1)
    def _():
        for step in work[-2:]:
            step()


def finish(base, grad, weight, partials):
    rows, depth = base.shape
    width = grad.shape[1]
    tile = rows // 16
    operands = scatter_operands(partials)
    widths = [p.shape[1] for p in partials]
    shard_rows = operands[0].shape[3]
    return pl.pallas_call(
        partial(finish_kernel, widths),
        name="finish",
        grid=(16,),
        in_specs=[
            pl.BlockSpec((tile, depth), lambda i: (i, 0)),
            pl.BlockSpec((tile, width), lambda i: (i, 0)),
            pl.BlockSpec((depth, width), lambda i: (0, 0)),
            *[pl.BlockSpec(memory_space=pl.ANY) for _ in widths],
        ],
        out_specs=[
            pl.BlockSpec((tile, depth), lambda i: (i, 0)),
            *[pl.BlockSpec((shard_rows, w), lambda i: (0, 0)) for w in widths],
        ],
        out_shape=[
            jax.ShapeDtypeStruct((rows, depth), jnp.float32),
            *[jax.ShapeDtypeStruct((shard_rows, w), jnp.float32) for w in widths],
        ],
        scratch_shapes=scatter_scratch(widths, shard_rows),
        compiler_params=pltpu.CompilerParams(
            vmem_limit_bytes=67043328, collective_id=1, has_side_effects=True
        ),
        cost_estimate=pl.CostEstimate(
            flops=2 * rows * depth * width, bytes_accessed=30 << 20, transcendentals=0
        ),
    )(base, grad, weight, *operands)


def adam_step(master, gradient, first, second, step_rate):
    first_new = beta_one * first + (1.0 - beta_one) * gradient
    second_new = beta_two * second + (1.0 - beta_two) * gradient * gradient
    direction = first_new / bias_one / (jnp.sqrt(second_new / bias_two) + adam_eps)
    return (master - step_rate * (direction + weight_decay * master), first_new, second_new)


def on_device(
    tokens,
    cotangent,
    segments,
    weight_qkv,
    weight_out,
    weight_ffn,
    vectors,
    first_qkv,
    first_out,
    first_ffn,
    first_vec,
    second_qkv,
    second_out,
    second_ffn,
    second_vec,
    outer_qkv,
    outer_out,
    outer_ffn,
    outer_vec,
):
    masters = (weight_qkv, weight_out, weight_ffn, vectors)
    lowered = [master.astype(jnp.bfloat16) for master in masters]
    width = weight_out.shape[1]
    entries = vectors.shape[0] // weight_out.shape[0]
    vector_block = jnp.pad(lowered[3].reshape(-1, entries), ((0, 0), (0, 128 - entries)))
    full_qkv, vector_rows = gather_all([lowered[0], vector_block], (False, True))
    full_vec = vector_rows[:, :entries].reshape(-1)
    vector_values = full_vec.astype(jnp.float32)
    pieces = [vector_values[position * width : (position + 1) * width] for position in range(8)]
    (
        bias_query,
        bias_value,
        bias_output,
        bias_second,
        gain_first,
        shift_first,
        gain_second,
        shift_second,
    ) = pieces
    bias_hidden = vector_values[8 * width :]
    token_rows = tokens[0]
    local_rows = token_rows.shape[0]
    side = lax.axis_index("seq")
    is_first = side == 0
    side_operand = jnp.reshape(side, (1,)).astype(jnp.int32)
    far_tokens = partner(jnp.where(is_first, token_rows[local_rows - W :], token_rows[:W]), "seq", 0)
    wide_tokens = jnp.where(
        is_first,
        jnp.concatenate([token_rows, far_tokens], axis=0),
        jnp.concatenate([far_tokens, token_rows], axis=0),
    )
    joined_bias = jnp.concatenate([bias_query, jnp.zeros_like(bias_query), bias_value])
    projected = (
        jnp.dot(wide_tokens, full_qkv, preferred_element_type=jnp.float32) + joined_bias
    ).astype(jnp.bfloat16)
    wide_ids = lax.dynamic_slice_in_dim(segments[0], side * (local_rows - W), local_rows + W, 0)
    ids_col = jnp.broadcast_to(wide_ids[:, None], (local_rows + W, 128))
    ids_row = jnp.broadcast_to(wide_ids[None, :], (8, local_rows + W))
    attended, attended_wide, logsum, full_out, full_up = attend(
        ids_col, ids_row, projected, [lowered[1], lowered[2][0]]
    )
    branch = jnp.dot(attended, full_out, preferred_element_type=jnp.float32) + bias_output
    residue_first = token_rows.astype(jnp.float32) + branch
    hidden_in, first_pullback = jax.vjp(layer_norm, residue_first, gain_first, shift_first)
    hidden_low = hidden_in.astype(jnp.bfloat16)
    activated_low, slope, full_down = ffn_up(hidden_low, full_up, bias_hidden, [lowered[2][1]])
    second_branch = (
        lax.dot_general(
            activated_low, full_down, (((1,), (1,)), ((), ())), preferred_element_type=jnp.float32
        )
        + bias_second
    )
    residue_second = hidden_in + second_branch
    result, second_pullback = jax.vjp(layer_norm, residue_second, gain_second, shift_second)
    upstream = cotangent[0].astype(jnp.float32)
    residue_second_grad, gain_second_grad, shift_second_grad = second_pullback(upstream)
    branch_two_low = residue_second_grad.astype(jnp.bfloat16)
    bias_second_grad = jnp.sum(branch_two_low.astype(jnp.float32), axis=0)
    down_grad = dot_tn(branch_two_low, activated_low).astype(jnp.bfloat16)
    up_grad, bias_rows, hidden_total, down_sum = ffn_back(
        branch_two_low, full_down, slope, hidden_low, full_up, [down_grad]
    )
    bias_hidden_grad = bias_rows[0]
    hidden_grad = residue_second_grad + hidden_total
    residue_first_grad, gain_first_grad, shift_first_grad = first_pullback(hidden_grad)
    branch_low = residue_first_grad.astype(jnp.bfloat16)
    bias_output_grad = jnp.sum(branch_low.astype(jnp.float32), axis=0)
    out_weight_grad = dot_tn(attended, branch_low).astype(jnp.bfloat16)
    mixed_grad = lax.dot_general(
        branch_low, full_out, (((1,), (1,)), ((), ())), preferred_element_type=jnp.float32
    ).astype(jnp.bfloat16)

    heads = width // HD
    head_of = jnp.arange(width, dtype=jnp.int32)[:, None] // HD
    collect = (head_of == jnp.arange(128, dtype=jnp.int32)[None, :]).astype(jnp.float32)
    inner_sums = jnp.dot(
        attended_wide * mixed_grad.astype(jnp.float32), collect, precision=lax.Precision.HIGHEST
    )

    def near_rows(x):
        return jnp.where(is_first, x[local_rows - W :], x[:W])

    far_stats = partner(
        jnp.concatenate([near_rows(logsum)[:, :heads], near_rows(inner_sums)[:, :heads]], axis=1),
        "seq",
        0,
    )
    far_outgrad = partner(near_rows(mixed_grad), "seq", 0)
    lane_pad = ((0, 0), (0, 128 - heads))
    far_logsum = jnp.pad(far_stats[:, :heads], lane_pad)
    far_inner = jnp.pad(far_stats[:, heads:], lane_pad)
    query_grad, key_near, value_near, up_sum = attend_back(
        ids_col, ids_row, projected, mixed_grad, logsum, inner_sums, [up_grad]
    )
    key_grad, value_grad = attend_far(
        side_operand, ids_col, ids_row, projected, far_outgrad, far_logsum, far_inner, key_near, value_near
    )
    projected_grad = jnp.concatenate([query_grad, key_grad, value_grad], axis=1)
    qkv_weight_grad = dot_tn(token_rows, projected_grad).astype(jnp.bfloat16)
    projected_sums = jnp.sum(projected_grad.astype(jnp.float32), axis=0)
    vector_grad = jnp.concatenate(
        [
            projected_sums[:width],
            projected_sums[2 * width :],
            bias_output_grad,
            bias_second_grad,
            gain_first_grad,
            shift_first_grad,
            gain_second_grad,
            shift_second_grad,
            bias_hidden_grad,
        ]
    )
    small = jnp.pad(vector_grad.reshape(width, -1), ((0, 0), (0, 128 - entries))).astype(jnp.bfloat16)
    input_grad, qkv_sum, small_sum, out_sum = finish(
        residue_first_grad, projected_grad, full_qkv, [qkv_weight_grad, small, out_weight_grad]
    )
    summed = (qkv_sum, out_sum, jnp.stack([up_sum, down_sum]), small_sum[:, :entries].reshape(-1))
    firsts = (first_qkv[0], first_out[0], first_ffn[0], first_vec[0])
    seconds = (second_qkv[0], second_out[0], second_ffn[0], second_vec[0])
    outers = (outer_qkv, outer_out, outer_ffn, outer_vec)
    stepped = [
        adam_step(
            masters[member], summed[member], firsts[member], seconds[member], step_rates[member]
        )
        for member in range(4)
    ]
    changes = [masters[member] - stepped[member][0] for member in range(4)]
    lowered_changes = [change.astype(jnp.bfloat16) for change in changes]
    other_changes = [partner(change, "grp", 0) for change in lowered_changes]
    deltas = [
        (lowered_changes[member].astype(jnp.float32) + other_changes[member].astype(jnp.float32)) / 2
        for member in range(4)
    ]
    momenta = [outer_beta * outers[member] + deltas[member] for member in range(4)]
    renewed = [
        masters[member] - outer_rate * (deltas[member] + outer_beta * momenta[member])
        for member in range(4)
    ]
    return (
        result.astype(jnp.bfloat16)[None],
        input_grad[None],
        summed[0][None],
        summed[1][None],
        summed[2][None],
        summed[3][None],
        stepped[0][1][None],
        stepped[1][1][None],
        stepped[2][1][None],
        stepped[3][1][None],
        stepped[0][2][None],
        stepped[1][2][None],
        stepped[2][2][None],
        stepped[3][2][None],
        deltas[0],
        deltas[1],
        deltas[2],
        deltas[3],
        momenta[0],
        momenta[1],
        momenta[2],
        momenta[3],
        renewed[0],
        renewed[1],
        renewed[2],
        renewed[3],
    )


def solution(mesh):
    return jax.shard_map(
        on_device,
        mesh=mesh,
        in_specs=(
            P(("grp", "dp"), "seq", None),
            P(("grp", "dp"), "seq", None),
            P(("grp", "dp"), None),
            P(("dp", "seq"), None),
            P(("dp", "seq"), None),
            P(None, ("dp", "seq"), None),
            P(("dp", "seq")),
            P("grp", ("dp", "seq"), None),
            P("grp", ("dp", "seq"), None),
            P("grp", None, ("dp", "seq"), None),
            P("grp", ("dp", "seq")),
            P("grp", ("dp", "seq"), None),
            P("grp", ("dp", "seq"), None),
            P("grp", None, ("dp", "seq"), None),
            P("grp", ("dp", "seq")),
            P(("dp", "seq"), None),
            P(("dp", "seq"), None),
            P(None, ("dp", "seq"), None),
            P(("dp", "seq")),
        ),
        out_specs=(
            P(("grp", "dp"), "seq", None),
            P(("grp", "dp"), "seq", None),
            P("grp", ("dp", "seq"), None),
            P("grp", ("dp", "seq"), None),
            P("grp", None, ("dp", "seq"), None),
            P("grp", ("dp", "seq")),
            P("grp", ("dp", "seq"), None),
            P("grp", ("dp", "seq"), None),
            P("grp", None, ("dp", "seq"), None),
            P("grp", ("dp", "seq")),
            P("grp", ("dp", "seq"), None),
            P("grp", ("dp", "seq"), None),
            P("grp", None, ("dp", "seq"), None),
            P("grp", ("dp", "seq")),
            P(("dp", "seq"), None),
            P(("dp", "seq"), None),
            P(None, ("dp", "seq"), None),
            P(("dp", "seq")),
            P(("dp", "seq"), None),
            P(("dp", "seq"), None),
            P(None, ("dp", "seq"), None),
            P(("dp", "seq")),
            P(("dp", "seq"), None),
            P(("dp", "seq"), None),
            P(None, ("dp", "seq"), None),
            P(("dp", "seq")),
        ),
        check_vma=False,
    )
```

```python
from functools import partial

import jax
import jax.numpy as jnp
from jax import lax
from jax.experimental import pallas as pl
from jax.experimental.pallas import tpu as pltpu
from jax.sharding import PartitionSpec as P

HD = 64
W = 512


beta_one = 0.9
beta_two = 0.95
adam_eps = 1e-08
weight_decay = 0.1
bias_one = 1.0 - 0.9**10
bias_two = 1.0 - 0.95**10
step_rates = (0.01, 0.1, 0.005, 0.2)
outer_rate = 0.7
outer_beta = 0.9
norm_eps = 1e-05
score_fill = -1e30


def partner(x, axis, stride):
    return lax.ppermute(x, axis, [(i, i ^ 1 << stride) for i in range(lax.axis_size(axis))])


def layer_norm(residue, norm_gain, norm_shift):
    average = jnp.mean(residue, axis=-1, keepdims=True)
    centred = residue - average
    variance = jnp.mean(centred * centred, axis=-1, keepdims=True)
    return centred * lax.rsqrt(variance + norm_eps) * norm_gain + norm_shift


TILE = 256
LENGTHS = (3, 4, 5, 5)


def first_tile(side, j):
    return jnp.where(side == 0, jnp.maximum(j - 2, 0), 3 - j)


def query_tile(side, j):
    return jnp.where(side == 0, j, 5 - j)


def own_tile(side, j):
    return jnp.where(side == 0, j, 3 - j)


def dot_nt(a, b):
    return lax.dot_general(a, b, (((1,), (1,)), ((), ())), preferred_element_type=jnp.float32)


def dot_tn(a, b):
    return lax.dot_general(a, b, (((0,), (0,)), ((), ())), preferred_element_type=jnp.float32)


def dot_nn(a, b):
    return lax.dot_general(a, b, (((1,), (0,)), ((), ())), preferred_element_type=jnp.float32)


def mask_bias(query_start, key_start, query_ids, key_ids):
    rows, cols = query_ids.shape[0], key_ids.shape[1]
    relative = (
        lax.broadcasted_iota(jnp.int32, (rows, cols), 1)
        - lax.broadcasted_iota(jnp.int32, (rows, cols), 0)
        + (key_start - query_start)
    )
    allowed = (relative <= W) & (relative >= -W) & (query_ids == key_ids)
    return jnp.where(allowed, 0.0, score_fill)


def pair_split(x):
    lane = lax.broadcasted_iota(jnp.int32, x.shape, 1)
    zero = jnp.zeros_like(x)
    return jnp.where(lane < HD, x, zero), jnp.where(lane < HD, zero, x)


def pick_lane(x, index):
    lane = lax.broadcasted_iota(jnp.int32, x.shape, 1)
    return jnp.sum(jnp.where(lane == index, x, 0.0), axis=1, keepdims=True)


def attend_kernel(
    shared, ids_col_ref, ids_row_ref, q_ref, k_ref, v_ref, *refs
):
    count = len(shared)
    o_ref, wide_ref, lse_ref = refs[count : count + 3]
    wholes = refs[count + 3 : 2 * count + 3]
    bias_ref = refs[2 * count + 3]
    j, pair = pl.program_id(0), pl.program_id(1)
    side = lax.axis_index("seq")
    now = j * pl.num_programs(1) + pair
    slots = 32
    work = gather_steps(shared, refs[:count], wholes, *refs[2 * count + 4 :])
    spread(work, now, slots, 0)

    def run(length):
        span = length * TILE
        start = pl.multiple_of(first_tile(side, j) * TILE, TILE)

        @pl.when(pair == 0)
        def _():
            bias_ref[:, :span] = mask_bias(
                query_tile(side, j) * TILE,
                start,
                ids_col_ref[:, :1],
                ids_row_ref[:1, pl.ds(start, span)],
            )
            lse_ref[...] = jnp.zeros_like(lse_ref)

        queries = pair_split(q_ref[...] * jnp.bfloat16(HD**-0.5))
        keys = k_ref[pl.ds(start, span), :]
        values = pair_split(v_ref[pl.ds(start, span), :])
        total = None
        lane = lax.broadcasted_iota(jnp.int32, lse_ref.shape, 1)
        for h in range(2):
            scores = dot_nt(queries[h], keys) + bias_ref[:, :span]
            maximum = jnp.max(scores, axis=1, keepdims=True)
            exponent = jnp.exp(scores - maximum)
            denominator = jnp.sum(exponent, axis=1, keepdims=True)
            weights = (exponent * (1.0 / denominator)).astype(jnp.bfloat16)
            part = dot_nn(weights, values[h])
            total = part if total is None else total + part
            logsum = maximum + jnp.log(denominator)
            lse_ref[...] = jnp.where(lane == 2 * pair + h, logsum, lse_ref[...])
        o_ref[...] = total.astype(jnp.bfloat16)
        wide_ref[...] = total

    for length in sorted(set(LENGTHS)):
        hits = [i for i in range(4) if LENGTHS[i] == length]

        @pl.when((j >= hits[0]) & (j <= hits[-1]))
        def _():
            run(length)

    @pl.when(now == slots - 1)
    def _():
        for step in work[-2:]:
            step()


def attend(ids_col, ids_row, qkv, shards):
    rows, width = qkv.shape[0], qkv.shape[1] // 3
    pairs = width // 128
    own = rows - W
    shared = (False,) * len(shards)
    got = pl.pallas_call(
        partial(attend_kernel, shared),
        name="attend",
        grid_spec=pltpu.PrefetchScalarGridSpec(
            num_scalar_prefetch=0,
            grid=(own // TILE, pairs),
            in_specs=[
                pl.BlockSpec((TILE, 128), lambda j, p: (query_tile(lax.axis_index("seq"), j), 0)),
                pl.BlockSpec((8, rows), lambda j, p: (0, 0)),
                pl.BlockSpec((TILE, 128), lambda j, p: (query_tile(lax.axis_index("seq"), j), p)),
                pl.BlockSpec((rows, 128), lambda j, p: (0, pairs + p)),
                pl.BlockSpec((rows, 128), lambda j, p: (0, 2 * pairs + p)),
                *[pl.BlockSpec(s.shape, lambda j, p: (0, 0)) for s in shards],
            ],
            out_specs=[
                pl.BlockSpec((TILE, 128), lambda j, p: (own_tile(lax.axis_index("seq"), j), p)),
                pl.BlockSpec((TILE, 128), lambda j, p: (own_tile(lax.axis_index("seq"), j), p)),
                pl.BlockSpec((TILE, 128), lambda j, p: (own_tile(lax.axis_index("seq"), j), 0)),
                *[pl.BlockSpec(memory_space=pl.ANY) for s in shards],
            ],
            scratch_shapes=[
                pltpu.VMEM((TILE, 5 * TILE), jnp.float32),
                *gather_scratch(shards, shared),
            ],
        ),
        out_shape=[
            jax.ShapeDtypeStruct((own, width), jnp.bfloat16),
            jax.ShapeDtypeStruct((own, width), jnp.float32),
            jax.ShapeDtypeStruct((own, 128), jnp.float32),
            *gather_shapes(shards),
        ],
        compiler_params=pltpu.CompilerParams(
            vmem_limit_bytes=48 << 20, collective_id=2, has_side_effects=True
        ),
        cost_estimate=pl.CostEstimate(
            flops=4 * 17 * TILE * TILE * width * 4, bytes_accessed=30 << 20, transcendentals=0
        ),
    )(ids_col, ids_row, qkv, qkv, qkv, *shards)
    return [*got[:3], *[w.reshape(-1, w.shape[-1]) for w in got[3:]]]


def attend_back_kernel(
    widths, ids_col_ref, ids_row_ref, q_ref, k_ref, v_ref, do_ref, lse_ref, inner_ref, *refs
):
    count = len(widths)
    dq_ref, dk_ref, dv_ref = refs[count : count + 3]
    sums = refs[count + 3 : 2 * count + 3]
    bias_ref, dkt_ref, dvt_ref = refs[2 * count + 3 : 2 * count + 6]
    pair, j = pl.program_id(0), pl.program_id(1)
    side = lax.axis_index("seq")
    own = dk_ref.shape[0]
    now, slots = pair * pl.num_programs(1) + j, 32
    work = scatter_steps(widths, refs[:count], sums, *refs[2 * count + 6 :])
    spread(work, now, slots, chunks(widths))

    @pl.when(j == 0)
    def _():
        dkt_ref[...] = jnp.zeros_like(dkt_ref)
        dvt_ref[...] = jnp.zeros_like(dvt_ref)

    def run(length):
        span = length * TILE
        start = pl.multiple_of(first_tile(side, j) * TILE, TILE)

        @pl.when(pair == 0)
        def _():
            bias_ref[j, :, :span] = mask_bias(
                query_tile(side, j) * TILE,
                start,
                ids_col_ref[:, :1],
                ids_row_ref[:1, pl.ds(start, span)],
            )

        scaled = q_ref[...] * jnp.bfloat16(HD**-0.5)
        outgrad = do_ref[...]
        queries = pair_split(scaled)
        outgrads = pair_split(outgrad)
        turned_q = jnp.transpose(scaled.astype(jnp.float32)).astype(jnp.bfloat16)
        turned_do = jnp.transpose(outgrad.astype(jnp.float32)).astype(jnp.bfloat16)
        keys = k_ref[pl.ds(start, span), :]
        values = v_ref[pl.ds(start, span), :]
        key_parts = pair_split(keys)
        total = None
        for h in range(2):
            logsum = pick_lane(lse_ref[...], 2 * pair + h)
            inner = pick_lane(inner_ref[...], 2 * pair + h)
            scores = dot_nt(queries[h], keys) + bias_ref[j, :, :span]
            probs = jnp.exp(scores - logsum)
            prob_grad = dot_nt(outgrads[h], values)
            score_grad = (probs * (prob_grad - inner)).astype(jnp.bfloat16)
            part = dot_nn(score_grad, key_parts[h])
            total = part if total is None else total + part
            head = slice(h * HD, (h + 1) * HD)
            dvt_ref[head, pl.ds(start, span)] += dot_nn(turned_do[head], probs.astype(jnp.bfloat16))
            dkt_ref[head, pl.ds(start, span)] += dot_nn(turned_q[head], score_grad)
        dq_ref[...] = (total * HD**-0.5).astype(jnp.bfloat16)

    for length in sorted(set(LENGTHS)):
        hits = [i for i in range(4) if LENGTHS[i] == length]

        @pl.when((j >= hits[0]) & (j <= hits[-1]))
        def _():
            run(length)

    @pl.when(j == pl.num_programs(1) - 1)
    def _():
        at = pl.multiple_of(side * W, W)
        dk_ref[...] = jnp.transpose(dkt_ref[:, pl.ds(at, own)])
        dv_ref[...] = jnp.transpose(dvt_ref[:, pl.ds(at, own)])

    @pl.when(now == slots - 1)
    def _():
        for step in work[-2:]:
            step()


def attend_back(ids_col, ids_row, qkv, outgrad, lse, inner, partials):
    rows, width = qkv.shape[0], qkv.shape[1] // 3
    pairs = width // 128
    own = rows - W
    operands = scatter_operands(partials)
    widths = [p.shape[1] for p in partials]
    shard_rows = operands[0].shape[3]
    return pl.pallas_call(
        partial(attend_back_kernel, widths),
        name="attend_back",
        grid_spec=pltpu.PrefetchScalarGridSpec(
            num_scalar_prefetch=0,
            grid=(pairs, own // TILE),
            in_specs=[
                pl.BlockSpec((TILE, 128), lambda p, j: (query_tile(lax.axis_index("seq"), j), 0)),
                pl.BlockSpec((8, rows), lambda p, j: (0, 0)),
                pl.BlockSpec((TILE, 128), lambda p, j: (query_tile(lax.axis_index("seq"), j), p)),
                pl.BlockSpec((rows, 128), lambda p, j: (0, pairs + p)),
                pl.BlockSpec((rows, 128), lambda p, j: (0, 2 * pairs + p)),
                pl.BlockSpec((TILE, 128), lambda p, j: (own_tile(lax.axis_index("seq"), j), p)),
                pl.BlockSpec((TILE, 128), lambda p, j: (own_tile(lax.axis_index("seq"), j), 0)),
                pl.BlockSpec((TILE, 128), lambda p, j: (own_tile(lax.axis_index("seq"), j), 0)),
                *[pl.BlockSpec(memory_space=pl.ANY) for _ in widths],
            ],
            out_specs=[
                pl.BlockSpec((TILE, 128), lambda p, j: (own_tile(lax.axis_index("seq"), j), p)),
                pl.BlockSpec((own, 128), lambda p, j: (0, p)),
                pl.BlockSpec((own, 128), lambda p, j: (0, p)),
                *[pl.BlockSpec((shard_rows, w), lambda p, j: (0, 0)) for w in widths],
            ],
            scratch_shapes=[
                pltpu.VMEM((own // TILE, TILE, 5 * TILE), jnp.float32),
                pltpu.VMEM((128, rows), jnp.float32),
                pltpu.VMEM((128, rows), jnp.float32),
                *scatter_scratch(widths, shard_rows),
            ],
        ),
        out_shape=[
            jax.ShapeDtypeStruct((own, width), jnp.bfloat16),
            jax.ShapeDtypeStruct((own, width), jnp.float32),
            jax.ShapeDtypeStruct((own, width), jnp.float32),
            *[jax.ShapeDtypeStruct((shard_rows, w), jnp.float32) for w in widths],
        ],
        compiler_params=pltpu.CompilerParams(
            vmem_limit_bytes=67043328, collective_id=3, has_side_effects=True
        ),
        cost_estimate=pl.CostEstimate(
            flops=10 * 17 * TILE * TILE * width * 4, bytes_accessed=40 << 20, transcendentals=0
        ),
    )(ids_col, ids_row, qkv, qkv, qkv, outgrad, lse, inner, *operands)


def attend_far_kernel(
    side_ref, ids_col_ref, ids_row_ref, q_ref, k_ref, v_ref, do_ref, lse_ref, inner_ref,
    dk_in_ref, dv_in_ref, dk_ref, dv_ref, bias_ref,
):
    pair = pl.program_id(0)
    side = side_ref[0]

    @pl.when(pair == 0)
    def _():
        bias_ref[...] = mask_bias(
            jnp.where(side == 0, 2 * W, 0), W, ids_col_ref[:, :1], ids_row_ref[:1, W : 2 * W]
        )

    scaled = q_ref[...] * jnp.bfloat16(HD**-0.5)
    outgrad = do_ref[...]
    queries = pair_split(scaled)
    outgrads = pair_split(outgrad)
    turned_q = jnp.transpose(scaled.astype(jnp.float32)).astype(jnp.bfloat16)
    turned_do = jnp.transpose(outgrad.astype(jnp.float32)).astype(jnp.bfloat16)
    keys, values = k_ref[...], v_ref[...]
    dk_parts, dv_parts = [], []
    for h in range(2):
        logsum = pick_lane(lse_ref[...], 2 * pair + h)
        inner = pick_lane(inner_ref[...], 2 * pair + h)
        scores = dot_nt(queries[h], keys) + bias_ref[...]
        probs = jnp.exp(scores - logsum)
        prob_grad = dot_nt(outgrads[h], values)
        score_grad = (probs * (prob_grad - inner)).astype(jnp.bfloat16)
        head = slice(h * HD, (h + 1) * HD)
        dv_parts.append(dot_nn(turned_do[head], probs.astype(jnp.bfloat16)))
        dk_parts.append(dot_nn(turned_q[head], score_grad))
    dk_far = jnp.transpose(jnp.concatenate(dk_parts, axis=0))
    dv_far = jnp.transpose(jnp.concatenate(dv_parts, axis=0))
    near = pl.multiple_of(jnp.where(side == 0, W, 0), W)
    rest = pl.multiple_of(jnp.where(side == 0, 0, W), W)
    dk_ref[pl.ds(near, W), :] = (dk_in_ref[pl.ds(near, W), :] + dk_far).astype(jnp.bfloat16)
    dv_ref[pl.ds(near, W), :] = (dv_in_ref[pl.ds(near, W), :] + dv_far).astype(jnp.bfloat16)
    dk_ref[pl.ds(rest, W), :] = dk_in_ref[pl.ds(rest, W), :].astype(jnp.bfloat16)
    dv_ref[pl.ds(rest, W), :] = dv_in_ref[pl.ds(rest, W), :].astype(jnp.bfloat16)


def attend_far(side, ids_col, ids_row, qkv, far_outgrad, far_lse, far_inner, dk, dv):
    rows, width = qkv.shape[0], qkv.shape[1] // 3
    pairs = width // 128
    own = rows - W
    far = lambda p, s: (jnp.where(s[0] == 0, 2, 0), p)
    return pl.pallas_call(
        attend_far_kernel,
        name="attend_far",
        grid_spec=pltpu.PrefetchScalarGridSpec(
            num_scalar_prefetch=1,
            grid=(pairs,),
            in_specs=[
                pl.BlockSpec((W, 128), lambda p, s: (jnp.where(s[0] == 0, 2, 0), 0)),
                pl.BlockSpec((8, rows), lambda p, s: (0, 0)),
                pl.BlockSpec((W, 128), far),
                pl.BlockSpec((W, 128), lambda p, s: (1, pairs + p)),
                pl.BlockSpec((W, 128), lambda p, s: (1, 2 * pairs + p)),
                pl.BlockSpec((W, 128), lambda p, s: (0, p)),
                pl.BlockSpec((W, 128), lambda p, s: (0, 0)),
                pl.BlockSpec((W, 128), lambda p, s: (0, 0)),
                pl.BlockSpec((own, 128), lambda p, s: (0, p)),
                pl.BlockSpec((own, 128), lambda p, s: (0, p)),
            ],
            out_specs=[
                pl.BlockSpec((own, 128), lambda p, s: (0, p)),
                pl.BlockSpec((own, 128), lambda p, s: (0, p)),
            ],
            scratch_shapes=[pltpu.VMEM((W, W), jnp.float32)],
        ),
        out_shape=[jax.ShapeDtypeStruct((own, width), jnp.bfloat16)] * 2,
        compiler_params=pltpu.CompilerParams(vmem_limit_bytes=48 << 20),
        cost_estimate=pl.CostEstimate(
            flops=8 * 4 * TILE * TILE * width * 4, bytes_accessed=20 << 20, transcendentals=0
        ),
    )(side, ids_col, ids_row, qkv, qkv, qkv, far_outgrad, far_lse, far_inner, dk, dv)


AXES = ("z", "x", "y")
GATHER_ORDERS = ((("z", "x", "y"), 3), (("z", "y", "x"), 3), (("x", "y", "z"), 2))
SCATTER_ORDERS = ((("y", "x", "z"), 3), (("x", "y", "z"), 3), (("z", "y", "x"), 2))
PIECE = 1024


def axis_parts():
    total = lax.axis_size("dp")
    inner = 2 ** ((total.bit_length() - 1) // 2)
    return {"z": total // inner, "x": inner, "y": lax.axis_size("seq")}


def places():
    inner = axis_parts()["x"]
    row = lax.axis_index("dp")
    return {"z": lax.div(row, inner), "x": lax.rem(row, inner), "y": lax.axis_index("seq")}


def neighbour(axis, step):
    parts, spots = axis_parts(), places()
    size = parts[axis]
    spots[axis] = lax.rem(spots[axis] + step + size, size)
    return (lax.axis_index("grp"), spots["z"] * parts["x"] + spots["x"], spots["y"])


def twin():
    return (1 - lax.axis_index("grp"), lax.axis_index("dp"), lax.axis_index("seq"))


def greet(peers):
    barrier = pltpu.get_barrier_semaphore()
    for peer in peers:
        pl.semaphore_signal(barrier, inc=1, device_id=peer, device_id_type=pl.DeviceIdType.MESH)
    pl.semaphore_wait(barrier, len(peers))


def ring_peers():
    return [neighbour(axis, step) for axis in AXES for step in (1, -1)]


def flows_of(widths, orders):
    flows = []
    for member, width in enumerate(widths):
        pieces = chunks([width])
        for piece in range(pieces):
            tiles, begin = width // pieces // 128, piece * (width // pieces)
            if tiles < len(orders):
                flows.append((member, orders[0][0], begin, tiles * 128, piece))
                continue
            total = sum(share for _, share in orders)
            low, used = 0, 0
            for order, share in orders:
                used += share
                high = -(-used * tiles // total)
                flows.append((member, order, begin + low * 128, (high - low) * 128, piece))
                low = high
    return flows


def delays(flows, gap):
    seen, found = [], []
    for member, _, _, _, piece in flows:
        if (member, piece) not in seen:
            seen.append((member, piece))
        found.append((len(seen) - 1) * gap)
    return found


def gather_steps(shared, shards, wholes, send_sems, recv_sems, own_sems):
    count = len(shared)
    parts, spots = axis_parts(), places()
    core = lax.axis_index("grp")
    spans = [s.shape[1] if shared[m] else s.shape[1] // 2 for m, s in enumerate(shards)]

    def columns(member, begin, width):
        if shared[member]:
            return pl.ds(begin, width)
        return pl.ds(pl.multiple_of(core * spans[member] + begin, 128), width)

    def own(member):
        cut = columns(member, 0, spans[member])
        return pltpu.make_async_copy(
            shards[member].at[:, cut],
            wholes[member].at[spots["z"], spots["x"], spots["y"], :, cut],
            own_sems.at[member],
        )

    flows = flows_of(spans, GATHER_ORDERS)
    chains, first = [], []
    for member, order, begin, width, _ in flows:
        cut = columns(member, begin, width)
        steps, done = [], []
        for axis in order:
            for turn in range(parts[axis] - 1):
                select = []
                for a in AXES:
                    if a == axis:
                        select.append(pl.ds(lax.rem(spots[a] + parts[a] - turn, parts[a]), 1))
                    elif a in done:
                        select.append(pl.ds(0, parts[a]))
                    else:
                        select.append(pl.ds(spots[a], 1))
                steps.append((wholes[member].at[(*select, slice(None), cut)], neighbour(axis, 1)))
            done.append(axis)
        if not shared[member]:
            steps.append((wholes[member].at[:, :, :, :, cut], twin()))
        first.append(sum(len(c) for c in chains))
        chains.append(steps)

    def remote(i, at):
        block, peer = chains[i][at]
        return pltpu.make_async_remote_copy(
            src_ref=block,
            dst_ref=block,
            send_sem=send_sems.at[first[i] + at],
            recv_sem=recv_sems.at[first[i] + at],
            device_id=peer,
            device_id_type=pl.DeviceIdType.MESH,
        )

    late = delays(flows, 1)
    length = max(late[i] + len(chains[i]) for i in range(len(flows)))

    def begin():
        greet(ring_peers() + [twin()])
        for member in range(count):
            own(member).start()
        for member in range(count):
            own(member).wait()

    def tick(time):
        for i, steps in enumerate(chains):
            at = time - late[i]
            if 1 <= at <= len(steps):
                remote(i, at - 1).wait_recv()
            if 0 <= at < len(steps):
                remote(i, at).start()

    def finish():
        for i, steps in enumerate(chains):
            for at in range(len(steps)):
                remote(i, at).wait_send()

    return [begin] + [partial(tick, time) for time in range(length + 1)] + [finish]


def gather_kernel(shared, *refs):
    count = len(shared)
    for step in gather_steps(shared, refs[:count], refs[count : 2 * count], *refs[2 * count :]):
        step()


def gather_scratch(shards, shared):
    parts = axis_parts()
    hops = sum(size - 1 for size in parts.values()) + 1
    spans = [s.shape[1] if shared[m] else s.shape[1] // 2 for m, s in enumerate(shards)]
    copies = hops * len(flows_of(spans, GATHER_ORDERS))
    return [
        pltpu.SemaphoreType.DMA((copies,)),
        pltpu.SemaphoreType.DMA((copies,)),
        pltpu.SemaphoreType.DMA((len(shards),)),
    ]


def gather_shapes(shards):
    parts = axis_parts()
    return [jax.ShapeDtypeStruct((parts["z"], parts["x"], parts["y"], *s.shape), s.dtype) for s in shards]


def gather_all(shards, shared):
    wholes = pl.pallas_call(
        partial(gather_kernel, shared),
        name="gather_all",
        in_specs=[pl.BlockSpec(memory_space=pltpu.VMEM)] * len(shards),
        out_specs=[pl.BlockSpec(memory_space=pl.ANY)] * len(shards),
        out_shape=gather_shapes(shards),
        scratch_shapes=gather_scratch(shards, shared),
        compiler_params=pltpu.CompilerParams(collective_id=0, has_side_effects=True),
    )(*shards)
    return [w.reshape(-1, w.shape[-1]) for w in wholes]


def scatter_plan(widths):
    parts = axis_parts()
    plan = []
    for member, order, begin, width, piece in flows_of(widths, SCATTER_ORDERS):
        left, levels = list(AXES), []
        for axis in order:
            left.remove(axis)
            levels.append((axis, tuple(parts[a] for a in left), [a for a in left]))
        plan.append((member, order, begin, width, piece, levels))
    return plan


def scatter_steps(widths, partials, sums, send_sems, recv_sems, load_sems, *buffers):
    plan = scatter_plan(widths)
    buffers = list(buffers)
    parts, spots = axis_parts(), places()
    chains, copies = [], []
    for member, order, begin, width, _, levels in plan:
        cut = pl.ds(begin, width)
        chain = []
        source, before = partials[member], list(AXES)
        for depth, (axis, extent, left) in enumerate(levels):
            size = parts[axis]
            inbox = [buffers.pop(0) for _ in range(size - 1)]
            terms = []
            for turn in range(size):
                index = lax.rem(spots[axis] + 2 * size - 1 - turn, size)
                select = tuple(index if a == axis else slice(None) for a in before)
                if depth:
                    terms.append(source.at[select])
                else:
                    terms.append(source.at[(*select, slice(None), cut)])
            ready = []
            if depth == 0:
                for turn in range(1, size):
                    local = buffers.pop(0)
                    copies.append((terms[turn], local))
                    ready.append(len(copies) - 1)
                    terms[turn] = local
            chain.append((axis, extent, inbox, terms, ready))
            source, before = inbox[-1], left
        chains.append(chain)

    def accumulate(target, term, extent):
        total = 1
        for size in extent:
            total *= size

        def body(index, carry):
            where, left = [], index
            for size in reversed(extent):
                where.insert(0, lax.rem(left, size))
                left = lax.div(left, size)
            where = tuple(where)
            target[where] = (
                target[where].astype(jnp.float32) + term[where].astype(jnp.float32)
            ).astype(jnp.bfloat16)
            return carry

        lax.fori_loop(0, total, body, 0)

    flat, first = [], []
    for chain in chains:
        steps = []
        for depth, (axis, extent, inbox, terms, ready) in enumerate(chain):
            for turn in range(parts[axis] - 1):
                steps.append((depth, axis, turn))
        first.append(sum(len(f) for f in flat))
        flat.append(steps)
    late = delays([p[:5] for p in plan], 1)
    length = max(late[i] + len(flat[i]) for i in range(len(plan)))

    def load(index):
        return pltpu.make_async_copy(*copies[index], load_sems.at[index])

    def remote(i, at):
        depth, axis, turn = flat[i][at]
        _, extent, inbox, terms, ready = chains[i][depth]
        return pltpu.make_async_remote_copy(
            src_ref=inbox[turn - 1] if turn else terms[0],
            dst_ref=inbox[turn],
            send_sem=send_sems.at[first[i] + at],
            recv_sem=recv_sems.at[first[i] + at],
            device_id=neighbour(axis, 1),
            device_id_type=pl.DeviceIdType.MESH,
        )

    def begin():
        greet(ring_peers())
        for index in range(len(copies)):
            load(index).start()

    def tick(time):
        for i, steps in enumerate(flat):
            at = time - late[i]
            if 1 <= at <= len(steps):
                remote(i, at - 1).wait_recv()
                depth, axis, turn = steps[at - 1]
                _, extent, inbox, terms, ready = chains[i][depth]
                if ready:
                    load(ready[turn]).wait()
                if at < len(steps):
                    accumulate(inbox[turn], terms[turn + 1], extent)
                else:
                    member, _, begin, width = plan[i][:4]
                    sums[member][:, begin : begin + width] = inbox[turn][...].astype(
                        jnp.float32
                    ) + terms[turn + 1][...].astype(jnp.float32)
            if 0 <= at < len(steps):
                remote(i, at).start()

    def finish():
        for i, steps in enumerate(flat):
            for at in range(len(steps)):
                remote(i, at).wait_send()

    return [begin] + [partial(tick, time) for time in range(length + 1)] + [finish]


def scatter_scratch(widths, rows):
    parts = axis_parts()
    buffers, copies, loads = [], 0, 0
    for _, order, _, width, _, levels in scatter_plan(widths):
        for depth, (axis, extent, _) in enumerate(levels):
            slots = parts[axis] - 1
            copies += slots
            if depth == 0:
                loads += slots
                slots *= 2
            buffers += [pltpu.VMEM((*extent, rows, width), jnp.bfloat16)] * slots
    return [
        pltpu.SemaphoreType.DMA((copies,)),
        pltpu.SemaphoreType.DMA((copies,)),
        pltpu.SemaphoreType.DMA((loads,)),
        *buffers,
    ]


def scatter_operands(partials):
    parts = axis_parts()
    return [p.reshape(parts["z"], parts["x"], parts["y"], -1, p.shape[1]) for p in partials]


def spread(work, now, slots, busy):
    ticks = len(work) - 3
    for order, step in enumerate(work[:-2]):
        time = max(0, order - 1)
        if busy:
            slot = min(slots - 1, time * slots // busy)
        elif time < 4:
            slot = time
        else:
            slot = 3 + (time - 3) * (slots - 4) // (ticks - 3)
        pl.when(now == slot)(step)


def chunks(widths):
    return sum(max(1, min(4, width // PIECE)) for width in widths)


def ffn_up_kernel(shared, x_ref, w_ref, bias_ref, *refs):
    count = len(shared)
    active_ref, slope_ref = refs[count : count + 2]
    wholes = refs[count + 2 : 2 * count + 2]
    work = gather_steps(shared, refs[:count], wholes, *refs[2 * count + 2 :])
    now, slots = pl.program_id(0), 16
    spread(work, now, slots, 0)
    rows = 256
    for begin in range(0, x_ref.shape[0], rows):
        block = slice(begin, begin + rows)
        u = dot_nn(x_ref[block, :], w_ref[...]) + bias_ref[:1, :]
        share = 0.5 + 0.5 * lax.erf(u * 0.5**0.5)
        density = (0.5 / jnp.pi) ** 0.5 * jnp.exp(-0.5 * u * u)
        active_ref[block, :] = (u * share).astype(jnp.bfloat16)
        slope_ref[block, :] = (share + u * density).astype(jnp.bfloat16)

    @pl.when(now == slots - 1)
    def _():
        for step in work[-2:]:
            step()


def ffn_up(x, weight, bias, shards):
    rows, depth = x.shape
    width = weight.shape[1]
    tile = width // 16
    shared = (False,) * len(shards)
    got = pl.pallas_call(
        partial(ffn_up_kernel, shared),
        name="ffn_up",
        grid=(16,),
        in_specs=[
            pl.BlockSpec((rows, depth), lambda i: (0, 0)),
            pl.BlockSpec((depth, tile), lambda i: (0, i)),
            pl.BlockSpec((8, tile), lambda i: (0, i)),
            *[pl.BlockSpec(s.shape, lambda i: (0, 0)) for s in shards],
        ],
        out_specs=[
            pl.BlockSpec((rows, tile), lambda i: (0, i)),
            pl.BlockSpec((rows, tile), lambda i: (0, i)),
            *[pl.BlockSpec(memory_space=pl.ANY) for s in shards],
        ],
        out_shape=[
            jax.ShapeDtypeStruct((rows, width), jnp.bfloat16),
            jax.ShapeDtypeStruct((rows, width), jnp.bfloat16),
            *gather_shapes(shards),
        ],
        scratch_shapes=gather_scratch(shards, shared),
        compiler_params=pltpu.CompilerParams(
            vmem_limit_bytes=48 << 20, collective_id=4, has_side_effects=True
        ),
        cost_estimate=pl.CostEstimate(
            flops=2 * rows * depth * width, bytes_accessed=40 << 20, transcendentals=0
        ),
    )(x, weight, jnp.broadcast_to(bias[None, :], (8, width)), *shards)
    return [*got[:2], *[w.reshape(-1, w.shape[-1]) for w in got[2:]]]


def ffn_back_kernel(widths, dz_ref, down_ref, slope_ref, x_ref, up_ref, *refs):
    count = len(widths)
    turned_ref, *refs = refs[2 * count + 3], *refs[: 2 * count + 3], *refs[2 * count + 4 :]
    up_grad_ref, bias_ref, total_ref = refs[count : count + 3]
    sums = refs[count + 3 : 2 * count + 3]
    work = scatter_steps(widths, refs[:count], sums, *refs[2 * count + 3 :])
    now, slots = pl.program_id(0), 16
    spread(work, now, slots, chunks(widths))

    @pl.when(now == 0)
    def _():
        total_ref[...] = jnp.zeros_like(total_ref)
        for begin in range(0, x_ref.shape[0], TILE):
            block = slice(begin, begin + TILE)
            turned_ref[:, block] = jnp.transpose(x_ref[block, :].astype(jnp.float32)).astype(jnp.bfloat16)

    inner = (dot_nn(dz_ref[...], down_ref[...]) * slope_ref[...].astype(jnp.float32)).astype(jnp.bfloat16)
    column = jnp.sum(inner.astype(jnp.float32), axis=0, keepdims=True)
    bias_ref[...] = jnp.broadcast_to(column, bias_ref.shape)
    up_grad_ref[...] = dot_nn(turned_ref[...], inner).astype(jnp.bfloat16)
    total_ref[...] += dot_nt(inner, up_ref[...])

    @pl.when(now == slots - 1)
    def _():
        for step in work[-2:]:
            step()


def ffn_back(dz, weight_down, slope, x, weight_up, partials):
    rows, depth = dz.shape
    width = weight_up.shape[1]
    tile = width // 16
    operands = scatter_operands(partials)
    widths = [p.shape[1] for p in partials]
    shard_rows = operands[0].shape[3]
    whole = pl.BlockSpec((rows, depth), lambda i: (0, 0))
    return pl.pallas_call(
        partial(ffn_back_kernel, widths),
        name="ffn_back",
        grid=(16,),
        in_specs=[
            whole,
            pl.BlockSpec((depth, tile), lambda i: (0, i)),
            pl.BlockSpec((rows, tile), lambda i: (0, i)),
            whole,
            pl.BlockSpec((depth, tile), lambda i: (0, i)),
            *[pl.BlockSpec(memory_space=pl.ANY) for _ in widths],
        ],
        out_specs=[
            pl.BlockSpec((depth, tile), lambda i: (0, i)),
            pl.BlockSpec((8, tile), lambda i: (0, i)),
            whole,
            *[pl.BlockSpec((shard_rows, w), lambda i: (0, 0)) for w in widths],
        ],
        out_shape=[
            jax.ShapeDtypeStruct((depth, width), jnp.bfloat16),
            jax.ShapeDtypeStruct((8, width), jnp.float32),
            jax.ShapeDtypeStruct((rows, depth), jnp.float32),
            *[jax.ShapeDtypeStruct((shard_rows, w), jnp.float32) for w in widths],
        ],
        scratch_shapes=[pltpu.VMEM((depth, rows), jnp.bfloat16), *scatter_scratch(widths, shard_rows)],
        compiler_params=pltpu.CompilerParams(
            vmem_limit_bytes=67043328, collective_id=5, has_side_effects=True
        ),
        cost_estimate=pl.CostEstimate(
            flops=6 * rows * depth * width, bytes_accessed=60 << 20, transcendentals=0
        ),
    )(dz, weight_down, slope, x, weight_up, *operands)


def finish_kernel(widths, base_ref, grad_ref, weight_ref, *refs):
    count = len(widths)
    out_ref = refs[count]
    sums = refs[count + 1 : 2 * count + 1]
    work = scatter_steps(widths, refs[:count], sums, *refs[2 * count + 1 :])
    now, slots = pl.program_id(0), 16
    spread(work, now, slots, chunks(widths))
    out_ref[...] = base_ref[...] + dot_nt(grad_ref[...], weight_ref[...])

    @pl.when(now == slots - 1)
    def _():
        for step in work[-2:]:
            step()


def finish(base, grad, weight, partials):
    rows, depth = base.shape
    width = grad.shape[1]
    tile = rows // 16
    operands = scatter_operands(partials)
    widths = [p.shape[1] for p in partials]
    shard_rows = operands[0].shape[3]
    return pl.pallas_call(
        partial(finish_kernel, widths),
        name="finish",
        grid=(16,),
        in_specs=[
            pl.BlockSpec((tile, depth), lambda i: (i, 0)),
            pl.BlockSpec((tile, width), lambda i: (i, 0)),
            pl.BlockSpec((depth, width), lambda i: (0, 0)),
            *[pl.BlockSpec(memory_space=pl.ANY) for _ in widths],
        ],
        out_specs=[
            pl.BlockSpec((tile, depth), lambda i: (i, 0)),
            *[pl.BlockSpec((shard_rows, w), lambda i: (0, 0)) for w in widths],
        ],
        out_shape=[
            jax.ShapeDtypeStruct((rows, depth), jnp.float32),
            *[jax.ShapeDtypeStruct((shard_rows, w), jnp.float32) for w in widths],
        ],
        scratch_shapes=scatter_scratch(widths, shard_rows),
        compiler_params=pltpu.CompilerParams(
            vmem_limit_bytes=67043328, collective_id=1, has_side_effects=True
        ),
        cost_estimate=pl.CostEstimate(
            flops=2 * rows * depth * width, bytes_accessed=30 << 20, transcendentals=0
        ),
    )(base, grad, weight, *operands)


def adam_step(master, gradient, first, second, step_rate):
    first_new = beta_one * first + (1.0 - beta_one) * gradient
    second_new = beta_two * second + (1.0 - beta_two) * gradient * gradient
    direction = first_new / bias_one / (jnp.sqrt(second_new / bias_two) + adam_eps)
    return (master - step_rate * (direction + weight_decay * master), first_new, second_new)


def on_device(
    tokens,
    cotangent,
    segments,
    weight_qkv,
    weight_out,
    weight_ffn,
    vectors,
    first_qkv,
    first_out,
    first_ffn,
    first_vec,
    second_qkv,
    second_out,
    second_ffn,
    second_vec,
    outer_qkv,
    outer_out,
    outer_ffn,
    outer_vec,
):
    masters = (weight_qkv, weight_out, weight_ffn, vectors)
    lowered = [master.astype(jnp.bfloat16) for master in masters]
    width = weight_out.shape[1]
    entries = vectors.shape[0] // weight_out.shape[0]
    vector_block = jnp.pad(lowered[3].reshape(-1, entries), ((0, 0), (0, 128 - entries)))
    full_qkv, vector_rows = gather_all([lowered[0], vector_block], (False, True))
    full_vec = vector_rows[:, :entries].reshape(-1)
    vector_values = full_vec.astype(jnp.float32)
    pieces = [vector_values[position * width : (position + 1) * width] for position in range(8)]
    (
        bias_query,
        bias_value,
        bias_output,
        bias_second,
        gain_first,
        shift_first,
        gain_second,
        shift_second,
    ) = pieces
    bias_hidden = vector_values[8 * width :]
    token_rows = tokens[0]
    local_rows = token_rows.shape[0]
    side = lax.axis_index("seq")
    is_first = side == 0
    side_operand = jnp.reshape(side, (1,)).astype(jnp.int32)
    far_tokens = partner(jnp.where(is_first, token_rows[local_rows - W :], token_rows[:W]), "seq", 0)
    wide_tokens = jnp.where(
        is_first,
        jnp.concatenate([token_rows, far_tokens], axis=0),
        jnp.concatenate([far_tokens, token_rows], axis=0),
    )
    joined_bias = jnp.concatenate([bias_query, jnp.zeros_like(bias_query), bias_value])
    projected = (
        jnp.dot(wide_tokens, full_qkv, preferred_element_type=jnp.float32) + joined_bias
    ).astype(jnp.bfloat16)
    wide_ids = lax.dynamic_slice_in_dim(segments[0], side * (local_rows - W), local_rows + W, 0)
    ids_col = jnp.broadcast_to(wide_ids[:, None], (local_rows + W, 128))
    ids_row = jnp.broadcast_to(wide_ids[None, :], (8, local_rows + W))
    attended, attended_wide, logsum, full_out, full_up = attend(
        ids_col, ids_row, projected, [lowered[1], lowered[2][0]]
    )
    branch = jnp.dot(attended, full_out, preferred_element_type=jnp.float32) + bias_output
    residue_first = token_rows.astype(jnp.float32) + branch
    hidden_in, first_pullback = jax.vjp(layer_norm, residue_first, gain_first, shift_first)
    hidden_low = hidden_in.astype(jnp.bfloat16)
    activated_low, slope, full_down = ffn_up(hidden_low, full_up, bias_hidden, [lowered[2][1]])
    second_branch = (
        lax.dot_general(
            activated_low, full_down, (((1,), (1,)), ((), ())), preferred_element_type=jnp.float32
        )
        + bias_second
    )
    residue_second = hidden_in + second_branch
    result, second_pullback = jax.vjp(layer_norm, residue_second, gain_second, shift_second)
    upstream = cotangent[0].astype(jnp.float32)
    residue_second_grad, gain_second_grad, shift_second_grad = second_pullback(upstream)
    branch_two_low = residue_second_grad.astype(jnp.bfloat16)
    bias_second_grad = jnp.sum(branch_two_low.astype(jnp.float32), axis=0)
    down_grad = dot_tn(branch_two_low, activated_low).astype(jnp.bfloat16)
    up_grad, bias_rows, hidden_total, down_sum = ffn_back(
        branch_two_low, full_down, slope, hidden_low, full_up, [down_grad]
    )
    bias_hidden_grad = bias_rows[0]
    hidden_grad = residue_second_grad + hidden_total
    residue_first_grad, gain_first_grad, shift_first_grad = first_pullback(hidden_grad)
    branch_low = residue_first_grad.astype(jnp.bfloat16)
    bias_output_grad = jnp.sum(branch_low.astype(jnp.float32), axis=0)
    out_weight_grad = dot_tn(attended, branch_low).astype(jnp.bfloat16)
    mixed_grad = lax.dot_general(
        branch_low, full_out, (((1,), (1,)), ((), ())), preferred_element_type=jnp.float32
    ).astype(jnp.bfloat16)

    heads = width // HD
    head_of = jnp.arange(width, dtype=jnp.int32)[:, None] // HD
    collect = (head_of == jnp.arange(128, dtype=jnp.int32)[None, :]).astype(jnp.float32)
    inner_sums = jnp.dot(
        attended_wide * mixed_grad.astype(jnp.float32), collect, precision=lax.Precision.HIGHEST
    )

    def near_rows(x):
        return jnp.where(is_first, x[local_rows - W :], x[:W])

    far_stats = partner(
        jnp.concatenate([near_rows(logsum)[:, :heads], near_rows(inner_sums)[:, :heads]], axis=1),
        "seq",
        0,
    )
    far_outgrad = partner(near_rows(mixed_grad), "seq", 0)
    lane_pad = ((0, 0), (0, 128 - heads))
    far_logsum = jnp.pad(far_stats[:, :heads], lane_pad)
    far_inner = jnp.pad(far_stats[:, heads:], lane_pad)
    query_grad, key_near, value_near, up_sum = attend_back(
        ids_col, ids_row, projected, mixed_grad, logsum, inner_sums, [up_grad]
    )
    key_grad, value_grad = attend_far(
        side_operand, ids_col, ids_row, projected, far_outgrad, far_logsum, far_inner, key_near, value_near
    )
    projected_grad = jnp.concatenate([query_grad, key_grad, value_grad], axis=1)
    qkv_weight_grad = dot_tn(token_rows, projected_grad).astype(jnp.bfloat16)
    projected_sums = dot_nn(jnp.ones((16, local_rows), jnp.bfloat16), projected_grad)[0]
    vector_grad = jnp.concatenate(
        [
            projected_sums[:width],
            projected_sums[2 * width :],
            bias_output_grad,
            bias_second_grad,
            gain_first_grad,
            shift_first_grad,
            gain_second_grad,
            shift_second_grad,
            bias_hidden_grad,
        ]
    )
    small = jnp.pad(vector_grad.reshape(width, -1), ((0, 0), (0, 128 - entries))).astype(jnp.bfloat16)
    input_grad, qkv_sum, small_sum, out_sum = finish(
        residue_first_grad, projected_grad, full_qkv, [qkv_weight_grad, small, out_weight_grad]
    )
    summed = (qkv_sum, out_sum, jnp.stack([up_sum, down_sum]), small_sum[:, :entries].reshape(-1))
    firsts = (first_qkv[0], first_out[0], first_ffn[0], first_vec[0])
    seconds = (second_qkv[0], second_out[0], second_ffn[0], second_vec[0])
    outers = (outer_qkv, outer_out, outer_ffn, outer_vec)
    stepped = [
        adam_step(
            masters[member], summed[member], firsts[member], seconds[member], step_rates[member]
        )
        for member in range(4)
    ]
    changes = [masters[member] - stepped[member][0] for member in range(4)]
    lowered_changes = [change.astype(jnp.bfloat16) for change in changes]
    other_changes = [partner(change, "grp", 0) for change in lowered_changes]
    deltas = [
        (lowered_changes[member].astype(jnp.float32) + other_changes[member].astype(jnp.float32)) / 2
        for member in range(4)
    ]
    momenta = [outer_beta * outers[member] + deltas[member] for member in range(4)]
    renewed = [
        masters[member] - outer_rate * (deltas[member] + outer_beta * momenta[member])
        for member in range(4)
    ]
    return (
        result.astype(jnp.bfloat16)[None],
        input_grad[None],
        summed[0][None],
        summed[1][None],
        summed[2][None],
        summed[3][None],
        stepped[0][1][None],
        stepped[1][1][None],
        stepped[2][1][None],
        stepped[3][1][None],
        stepped[0][2][None],
        stepped[1][2][None],
        stepped[2][2][None],
        stepped[3][2][None],
        deltas[0],
        deltas[1],
        deltas[2],
        deltas[3],
        momenta[0],
        momenta[1],
        momenta[2],
        momenta[3],
        renewed[0],
        renewed[1],
        renewed[2],
        renewed[3],
    )


def solution(mesh):
    return jax.shard_map(
        on_device,
        mesh=mesh,
        in_specs=(
            P(("grp", "dp"), "seq", None),
            P(("grp", "dp"), "seq", None),
            P(("grp", "dp"), None),
            P(("dp", "seq"), None),
            P(("dp", "seq"), None),
            P(None, ("dp", "seq"), None),
            P(("dp", "seq")),
            P("grp", ("dp", "seq"), None),
            P("grp", ("dp", "seq"), None),
            P("grp", None, ("dp", "seq"), None),
            P("grp", ("dp", "seq")),
            P("grp", ("dp", "seq"), None),
            P("grp", ("dp", "seq"), None),
            P("grp", None, ("dp", "seq"), None),
            P("grp", ("dp", "seq")),
            P(("dp", "seq"), None),
            P(("dp", "seq"), None),
            P(None, ("dp", "seq"), None),
            P(("dp", "seq")),
        ),
        out_specs=(
            P(("grp", "dp"), "seq", None),
            P(("grp", "dp"), "seq", None),
            P("grp", ("dp", "seq"), None),
            P("grp", ("dp", "seq"), None),
            P("grp", None, ("dp", "seq"), None),
            P("grp", ("dp", "seq")),
            P("grp", ("dp", "seq"), None),
            P("grp", ("dp", "seq"), None),
            P("grp", None, ("dp", "seq"), None),
            P("grp", ("dp", "seq")),
            P("grp", ("dp", "seq"), None),
            P("grp", ("dp", "seq"), None),
            P("grp", None, ("dp", "seq"), None),
            P("grp", ("dp", "seq")),
            P(("dp", "seq"), None),
            P(("dp", "seq"), None),
            P(None, ("dp", "seq"), None),
            P(("dp", "seq")),
            P(("dp", "seq"), None),
            P(("dp", "seq"), None),
            P(None, ("dp", "seq"), None),
            P(("dp", "seq")),
            P(("dp", "seq"), None),
            P(("dp", "seq"), None),
            P(None, ("dp", "seq"), None),
            P(("dp", "seq")),
        ),
        check_vma=False,
    )
```
